32 devices in a mesh: dp: 8 (over y, x, core), mp: 4 (over z).
Axes of the slice: x: 2, y: 2, z: 4, core: 2. Of those that a mesh axis runs over, the one named last changes fastest.
Arguments:
- tokens: bfloat16 [64, 1280, 768], P(('dp', 'mp')), may hold values from -6 to 6
- image_ids: int32 [64, 1280], P(('dp', 'mp')), may hold values from -1 to 1, as said below
- selected: int32 [64, 1280], P(('dp', 'mp')), may hold values from 0 to 1, as said below
- cotangent: bfloat16 [64, 1280, 768], P(('dp', 'mp')), may hold values from -6 to 6
- qkv_weight: float32 [768, 2304], P(('dp', 'mp')), may hold values from -0.21875 to 0.21875
- qkv_first: float32 [768, 2304], P(('dp', 'mp')), may hold values from -24 to 24
- qkv_second: float32 [768, 2304], P(('dp', 'mp')), may hold values from 1.6384 to 6.5536
- proj_weight: float32 [768, 768], P(('dp', 'mp')), may hold values from -1.75 to 1.75
- proj_first: float32 [768, 768], P(('dp', 'mp')), may hold values from -24 to 24
- proj_second: float32 [768, 768], P(('dp', 'mp')), may hold values from 1.6384 to 6.5536
- up_weight: float32 [768, 3072], P('dp', 'mp'), may hold values from -0.21875 to 0.21875
- up_first: float32 [768, 3072], P('dp', 'mp'), may hold values from -24 to 24
- up_second: float32 [768, 3072], P('dp', 'mp'), may hold values from 1.6384 to 6.5536
- down_weight: float32 [3072, 768], P('mp', 'dp'), may hold values from -0.109375 to 0.109375
- down_first: float32 [3072, 768], P('mp', 'dp'), may hold values from -24 to 24
- down_second: float32 [3072, 768], P('mp', 'dp'), may hold values from 1.6384 to 6.5536
- up_bias: float32 [3072], replicated, may hold values from -3 to 3
- bias_first: float32 [3072], replicated, may hold values from -32 to 32
- bias_second: float32 [3072], replicated, may hold values from 4.096 to 16.384
- vectors: float32 [7, 768], replicated, may hold values from -4 to 4, as said below
- vector_first: float32 [7, 768], replicated, may hold values from -62.334817 to 62.334817
- vector_second: float32 [7, 768], replicated, may hold values from 2.6133333 to 80.2816, as said below
Outputs:
- block_output: bfloat16 [64, 1280, 768], P(('dp', 'mp'))
- input_grad: float32 [64, 1280, 768], P(('dp', 'mp'))
- weight_norms: float32 [2, 4], replicated
- qkv_new: float32 [768, 2304], P(('dp', 'mp'))
- qkv_first_new: float32 [768, 2304], P(('dp', 'mp'))
- qkv_second_new: float32 [768, 2304], P(('dp', 'mp'))
- proj_new: float32 [768, 768], P(('dp', 'mp'))
- proj_first_new: float32 [768, 768], P(('dp', 'mp'))
- proj_second_new: float32 [768, 768], P(('dp', 'mp'))
- up_new: float32 [768, 3072], P('dp', 'mp')
- up_first_new: float32 [768, 3072], P('dp', 'mp')
- up_second_new: float32 [768, 3072], P('dp', 'mp')
- down_new: float32 [3072, 768], P('mp', 'dp')
- down_first_new: float32 [3072, 768], P('mp', 'dp')
- down_second_new: float32 [3072, 768], P('mp', 'dp')
- bias_new: float32 [3072], replicated
- bias_first_new: float32 [3072], replicated
- bias_second_new: float32 [3072], replicated
- vectors_new: float32 [7, 768], replicated
- vector_first_new: float32 [7, 768], replicated
- vector_second_new: float32 [7, 768], replicated
The draws below stay inside these ranges and needn't reach their ends.
Inputs may be any that keep to these rules, and one draw needn't show every extreme that they name: `image_ids`: each row holds one or two whole images of 577 patches, one after the other from some position of the row, numbered 0 and 1 in order; all other positions are padding -1; some row holds two and some row one. `selected`: each row has exactly 640 ones. `vectors`: gains lie between 0.7 and 1.3. `vector_second`: all entries are positive.
All inputs are finite; a program needn't handle non-finite values.
Results may differ from the reference program's by a relative error of at most 0.0095.
Values may be sent and summed in bfloat16 or wider, within the bound.
No kernel may reach another device: no remote copies, remote signals or barrier semaphores. Data moves between devices by JAX's collectives and lax.ppermute only.
A program may use at most 256 MiB of HBM per device.

```python
import math
import jax
import jax.numpy as jnp
from jax import lax

D = 768
FF = 3072
HEADS = 12
HEAD_DIM = 64
IMG = 577
SEQ = 1280
CAP = 640
STEP = 10
ROWS = 64
SELECTED = 40960


def draw_image_ids(key, part):
    counts = jax.random.randint(jax.random.fold_in(key, 101), (ROWS, 1), 1, 3)
    row_index = jnp.arange(ROWS)[:, None]
    counts = jnp.where(row_index == 0, 2, jnp.where(row_index == 1, 1, counts))
    room = SEQ - counts * IMG + 1
    fresh = jax.random.randint(jax.random.fold_in(key, 107), (ROWS, 1), 0, 1 << 30)
    start = fresh % room
    position = jnp.arange(SEQ)[None, :]
    relative = position - start
    image_no = jnp.where(relative >= 0, relative // IMG, -1)
    live = (relative >= 0) & (image_no < counts)
    return jnp.where(live, image_no, -1).astype(jnp.int32)


def draw_selected(key, part):
    row_keys = jax.random.split(jax.random.fold_in(key, 202), ROWS)

    def select_row(row_key):
        return (jax.random.permutation(row_key, SEQ) < CAP).astype(jnp.int32)
    return jax.vmap(select_row)(row_keys)


def row_factors():
    router_factor = 7.0 / math.sqrt(D)
    return jnp.array([0.3, 0.3, 0.3, 0.3, router_factor, 0.7, 0.7], jnp.float32)[:, None] * math.sqrt(SELECTED)


def draw_vectors(key, part):
    key_pair = jax.random.split(jax.random.fold_in(key, 303), 2)
    spread = jax.random.uniform(key_pair[0], (7, D), jnp.float32, -1.0, 1.0)
    normal_part = jnp.clip(jax.random.normal(key_pair[1], (7, D), jnp.float32), -4.0, 4.0)
    row_kinds = jnp.array([0, 1, 0, 1, 2, 1, 1], jnp.int32)[:, None]
    gain_rows = 1.0 + 0.3 * spread
    biases = 0.2 * normal_part
    router = normal_part
    return jnp.where(row_kinds == 0, gain_rows, jnp.where(row_kinds == 1, biases, router))


def draw_vector_first(key, part):
    normal_part = jnp.clip(jax.random.normal(jax.random.fold_in(key, 404), (7, D), jnp.float32), -4.0, 4.0)
    return 0.11 * row_factors() * normal_part


def draw_vector_second(key, part):
    spread = jax.random.uniform(jax.random.fold_in(key, 505), (7, D), jnp.float32, 0.0, math.log(4.0))
    factors = row_factors()
    return 0.001 * factors * factors * jnp.exp(spread)


def levels(stream_key, extent, pieces, smallest, top_value):
    loudness, own = 1.0, jax.random.fold_in(stream_key, 6)
    for axis_at, blocks in pieces:
        steps = jnp.exp(jax.random.uniform(jax.random.fold_in(own, axis_at), (blocks,), jnp.float32, smallest / len(pieces), top_value / len(pieces)))
        loudness = loudness * jnp.repeat(steps, extent[axis_at] // blocks).reshape([-1 if axis == axis_at else 1 for axis in range(len(extent))])
    return loudness


def centred(key, dims, scale, most, shards=(), held_as=jnp.bfloat16):
    drawn = jax.random.normal(key, dims, jnp.float32) * scale
    if len(shards) > 0:
        drawn = levels(key, dims, shards, -0.22, 0.18) * drawn
    return jnp.clip(drawn, min=-most, max=most).astype(held_as)


def setup_inputs(seed: int = 0) -> dict:
    streams_of = jax.random.split(jax.random.key(seed), 23)
    tokens = centred(streams_of[0], (ROWS, SEQ, D), 1.0, 6.0, ((0, 32),))
    image_ids = draw_image_ids(jax.random.fold_in(streams_of[22], 71), 0)
    selected = draw_selected(jax.random.fold_in(streams_of[22], 71), 0)
    cotangent = centred(streams_of[3], (ROWS, SEQ, D), 1.0, 6.0, ((0, 32),))
    qkv_weight = centred(streams_of[4], (D, 3 * D), D ** -0.5, 0.21875, ((0, 32),), jnp.float32)
    qkv_first = centred(streams_of[5], (D, 3 * D), (0.02 * SELECTED ** 0.5), 24.0, ((0, 32),), jnp.float32)
    qkv_second = jnp.clip(jnp.exp(math.log(6.5536) - 1.3862944 * jax.random.uniform(streams_of[6], (D, 3 * D), jnp.float32) ** levels(streams_of[6], (D, 3 * D), ((0, 32),), -0.2, 0.2)), 1.6384, 6.5536)
    proj_weight = centred(streams_of[7], (D, D), (D // 64) ** -0.5, 1.75, ((0, 32),), jnp.float32)
    proj_first = centred(streams_of[8], (D, D), (0.02 * SELECTED ** 0.5), 24.0, ((0, 32),), jnp.float32)
    proj_second = jnp.clip(jnp.exp(math.log(6.5536) - 1.3862944 * jax.random.uniform(streams_of[9], (D, D), jnp.float32) ** levels(streams_of[9], (D, D), ((0, 32),), -0.2, 0.2)), 1.6384, 6.5536)
    up_weight = centred(streams_of[10], (D, FF), D ** -0.5, 0.21875, ((0, 8), (1, 4)), jnp.float32)
    up_first = centred(streams_of[11], (D, FF), (0.02 * SELECTED ** 0.5), 24.0, ((0, 8), (1, 4)), jnp.float32)
    up_second = jnp.clip(jnp.exp(math.log(6.5536) - 1.3862944 * jax.random.uniform(streams_of[12], (D, FF), jnp.float32) ** levels(streams_of[12], (D, FF), ((0, 8), (1, 4)), -0.2, 0.2)), 1.6384, 6.5536)
    down_weight = centred(streams_of[13], (FF, D), FF ** -0.5, 0.109375, ((0, 4), (1, 8)), jnp.float32)
    down_first = centred(streams_of[14], (FF, D), (0.02 * SELECTED ** 0.5), 24.0, ((0, 4), (1, 8)), jnp.float32)
    down_second = jnp.clip(jnp.exp(math.log(6.5536) - 1.3862944 * jax.random.uniform(streams_of[15], (FF, D), jnp.float32) ** levels(streams_of[15], (FF, D), ((0, 4), (1, 8)), -0.2, 0.2)), 1.6384, 6.5536)
    up_bias = centred(streams_of[16], (FF,), 0.2, 3.0, (), jnp.float32)
    bias_first = centred(streams_of[17], (FF,), (0.03 * SELECTED ** 0.5), 32.0, (), jnp.float32)
    bias_second = jnp.clip(jnp.exp(jax.random.uniform(streams_of[18], (FF,), jnp.float32, math.log(4.096), math.log(16.384))), 4.096, 16.384)
    vectors = draw_vectors(jax.random.fold_in(streams_of[22], 71), 0)
    vector_first = draw_vector_first(jax.random.fold_in(streams_of[22], 71), 0)
    vector_second = draw_vector_second(jax.random.fold_in(streams_of[22], 71), 0)
    return dict(tokens=tokens, image_ids=image_ids, selected=selected, cotangent=cotangent, qkv_weight=qkv_weight, qkv_first=qkv_first, qkv_second=qkv_second, proj_weight=proj_weight, proj_first=proj_first, proj_second=proj_second, up_weight=up_weight, up_first=up_first, up_second=up_second, down_weight=down_weight, down_first=down_first, down_second=down_second, up_bias=up_bias, bias_first=bias_first, bias_second=bias_second, vectors=vectors, vector_first=vector_first, vector_second=vector_second)


@jax.custom_vjp
def low(v):
    return lax.optimization_barrier(v.astype(jnp.bfloat16)).astype(jnp.float32)

@jax.custom_vjp
def low_back(v):
    return v

def low_keep(v):
    return (low(v), None)

def low_pass(kept, grad):
    return (grad,)

def back_keep(v):
    return (v, None)

def back_low(kept, grad):
    return (low(grad),)
low.defvjp(low_keep, low_pass)
low_back.defvjp(back_keep, back_low)
highest = lax.Precision.HIGHEST
eps_norm = 1e-06
eps_adam = 1e-06
beta_one = 0.9
beta_two = 0.999
decay_mat = 0.01
rate_lamb = 0.3
masked_score = -1e+30

def layer_norm(values, gain, shift):
    center = lax.optimization_barrier(jnp.mean(values, -1, keepdims=True))
    offset = values - center
    spread = lax.optimization_barrier(jnp.mean(offset * offset, -1, keepdims=True))
    return offset * lax.rsqrt(spread + eps_norm) * gain + shift

def split_heads(packed):
    return packed.reshape(packed.shape[0], HEADS, HEAD_DIM)

def forward(inputs, image_marks, vectors, qkv_mat, proj_mat, up_mat, up_bias, down_mat):
    score_scale = 1.0 / math.sqrt(HEAD_DIM)
    router_scale = 1.0 / math.sqrt(D)
    normed = low(layer_norm(inputs, vectors[0], vectors[1]))
    qkv_all = low_back(low(jnp.dot(normed, qkv_mat, precision=highest)))
    queries = split_heads(qkv_all[:, :D])
    key_rows = split_heads(qkv_all[:, D:2 * D])
    values = split_heads(qkv_all[:, 2 * D:])
    scores = low_back(jnp.einsum('qhd,khd->hqk', queries, key_rows, precision=highest) * score_scale)
    allowed = image_marks[:, None] == image_marks[None, :]
    scores = jnp.where(allowed[None], scores, masked_score)
    attn_probs = low(jax.nn.softmax(scores, axis=-1))
    context = jnp.einsum('hqk,khd->qhd', attn_probs, values, precision=highest).reshape(inputs.shape[0], D)
    context = low_back(low(context))
    attended = low_back(jnp.dot(context, proj_mat, precision=highest) + vectors[5])
    hidden_res = inputs + attended
    normed_two = low(layer_norm(hidden_res, vectors[2], vectors[3]))
    pre_act = low_back(jnp.dot(normed_two, up_mat, precision=highest) + up_bias)
    activated = low(jax.nn.gelu(pre_act, approximate=False))
    mlp_out = low_back(jnp.dot(activated, down_mat, precision=highest) + vectors[6])
    gating = jax.nn.sigmoid(lax.optimization_barrier(jnp.sum(inputs * vectors[4], -1, keepdims=True)) * router_scale)
    return inputs + gating * (attended + mlp_out)

def lamb_moments(weight, gradient, first_mom, second_mom, decay):
    first_new = beta_one * first_mom + (1.0 - beta_one) * gradient
    second_new = beta_two * second_mom + (1.0 - beta_two) * gradient * gradient
    update = first_new / (1.0 - beta_one ** STEP) / (jnp.sqrt(second_new / (1.0 - beta_two ** STEP)) + eps_adam) + decay * weight
    return (first_new, second_new, update)

def reference(tokens, image_ids, selected, cotangent, qkv_weight, qkv_first, qkv_second, proj_weight, proj_first, proj_second, up_weight, up_first, up_second, down_weight, down_first, down_second, up_bias, bias_first, bias_second, vectors, vector_first, vector_second):

    def rounded(master):
        return master.astype(jnp.bfloat16).astype(jnp.float32)
    qkv_mat = rounded(qkv_weight)
    proj_mat = rounded(proj_weight)
    up_mat = rounded(up_weight)
    down_mat = rounded(down_weight)
    picked = jnp.argsort(1 - selected, axis=-1, stable=True)[:, :CAP].astype(jnp.int32)

    def one_row(totals, row_items):
        row_tokens, row_marks, row_cot, row_pick = row_items
        inputs = jnp.take(row_tokens, row_pick, axis=0).astype(jnp.float32)
        image_marks = jnp.take(row_marks, row_pick, axis=0)

        def local_block(inputs_in, vectors_in, qkv_in, proj_in, up_in, bias_in, down_in):
            return forward(inputs_in, image_marks, vectors_in, qkv_in, proj_in, up_in, bias_in, down_in)
        result, pullback = jax.vjp(local_block, inputs, vectors, qkv_mat, proj_mat, up_mat, up_bias, down_mat)
        grads = pullback(jnp.take(row_cot, row_pick, axis=0).astype(jnp.float32))
        out_row = row_tokens.astype(jnp.float32).at[row_pick].set(result).astype(jnp.bfloat16)
        grad_row = row_cot.astype(jnp.float32).at[row_pick].set(grads[0])
        totals = jax.tree.map(jnp.add, totals, tuple(grads[1:]))
        return (totals, (out_row, grad_row))
    start_totals = (jnp.zeros_like(vectors), jnp.zeros_like(qkv_weight), jnp.zeros_like(proj_weight), jnp.zeros_like(up_weight), jnp.zeros_like(up_bias), jnp.zeros_like(down_weight))
    totals, stacked = lax.scan(one_row, start_totals, (tokens, image_ids, cotangent, picked))
    block_output, input_grad = stacked
    vec_sum, qkv_sum, proj_sum, up_sum, bias_sum, down_sum = totals
    qkv_first_new, qkv_second_new, qkv_upd = lamb_moments(qkv_weight, qkv_sum, qkv_first, qkv_second, decay_mat)
    proj_first_new, proj_second_new, proj_upd = lamb_moments(proj_weight, proj_sum, proj_first, proj_second, decay_mat)
    up_first_new, up_second_new, up_upd = lamb_moments(up_weight, up_sum, up_first, up_second, decay_mat)
    down_first_new, down_second_new, down_upd = lamb_moments(down_weight, down_sum, down_first, down_second, decay_mat)
    weight_sq = jnp.stack([jnp.sum(qkv_weight * qkv_weight), jnp.sum(proj_weight * proj_weight), jnp.sum(up_weight * up_weight), jnp.sum(down_weight * down_weight)])
    update_sq = jnp.stack([jnp.sum(qkv_upd * qkv_upd), jnp.sum(proj_upd * proj_upd), jnp.sum(up_upd * up_upd), jnp.sum(down_upd * down_upd)])
    weight_norms = jnp.sqrt(jnp.stack([weight_sq, update_sq]))
    ratios = weight_norms[0] / weight_norms[1]
    qkv_new = qkv_weight - rate_lamb * ratios[0] * qkv_upd
    proj_new = proj_weight - rate_lamb * ratios[1] * proj_upd
    up_new = up_weight - rate_lamb * ratios[2] * up_upd
    down_new = down_weight - rate_lamb * ratios[3] * down_upd
    bias_first_new, bias_second_new, bias_upd = lamb_moments(up_bias, bias_sum, bias_first, bias_second, 0.0)
    bias_ratio = jnp.sqrt(jnp.sum(up_bias * up_bias)) / jnp.sqrt(jnp.sum(bias_upd * bias_upd))
    bias_new = up_bias - rate_lamb * bias_ratio * bias_upd
    vector_first_new, vector_second_new, vector_upd = lamb_moments(vectors, vec_sum, vector_first, vector_second, 0.0)
    vector_ratio = jnp.sqrt(lax.optimization_barrier(jnp.sum(vectors * vectors, -1, keepdims=True))) / jnp.sqrt(lax.optimization_barrier(jnp.sum(vector_upd * vector_upd, -1, keepdims=True)))
    vectors_new = vectors - rate_lamb * vector_ratio * vector_upd
    return (block_output, input_grad, weight_norms, qkv_new, qkv_first_new, qkv_second_new, proj_new, proj_first_new, proj_second_new, up_new, up_first_new, up_second_new, down_new, down_first_new, down_second_new, bias_new, bias_first_new, bias_second_new, vectors_new, vector_first_new, vector_second_new)
```

```python
from functools import partial
import math

import jax
import jax.numpy as jnp
from jax import lax
from jax.experimental import pallas as pl
from jax.experimental.pallas import tpu as pltpu
from jax.sharding import Mesh, PartitionSpec as P

D = 768
FF = 3072
HEADS = 12
HEAD_DIM = 64
CAP = 640
SEQ = 1280
STEP = 10

eps_norm = 1e-06
eps_adam = 1e-06
beta_one = 0.9
beta_two = 0.999
decay_mat = 0.01
rate_lamb = 0.3
masked_score = -1e30

f32 = jnp.float32
bf16 = jnp.bfloat16
GROUP = 256
GROUPS = D // GROUP
LOG2E = 1.0 / math.log(2.0)
SCORE_SCALE = 1.0 / math.sqrt(HEAD_DIM)
ROUTER_SCALE = 1.0 / math.sqrt(D)


def dot_ab(left, right, left_dim=1, right_dim=0):
    return lax.dot_general(
        left, right, (((left_dim,), (right_dim,)), ((), ())), preferred_element_type=f32
    )


def params(mib, **more):
    return pltpu.CompilerParams(vmem_limit_bytes=mib << 20, **more)


def cost(flops, nbytes, trans=0):
    return pl.CostEstimate(flops=int(flops), bytes_accessed=int(nbytes), transcendentals=int(trans))


def norm_parts(values):
    center = jnp.mean(values, -1, keepdims=True)
    offset = values - center
    spread = jnp.mean(offset * offset, -1, keepdims=True)
    inverse = lax.rsqrt(spread + eps_norm)
    return offset * inverse, inverse


def norm_back(grad, normalized, inverse, gain):
    scaled = grad * gain
    return inverse * (
        scaled
        - jnp.mean(scaled, -1, keepdims=True)
        - normalized * jnp.mean(scaled * normalized, -1, keepdims=True)
    )


def ranks_of(sel, ids):
    kind = jnp.where(ids < 0, 2, ids)
    sub = lax.broadcasted_iota(jnp.int32, (8, SEQ), 0)
    lane = lax.broadcasted_iota(jnp.int32, (8, SEQ), 1)
    member = jnp.where(jnp.broadcast_to(kind, (8, SEQ)) == sub, jnp.broadcast_to(sel, (8, SEQ)), 0)
    total = member
    step = 1
    while step < SEQ:
        total = total + jnp.where(lane >= step, pltpu.roll(total, step, 1), 0)
        step *= 2
    count = jnp.max(total, axis=1, keepdims=True)
    first = count[0:1]
    second = first + count[1:2]
    base = jnp.where(sub == 0, 0, jnp.where(sub == 1, first, second))
    rank = jnp.sum(member * (total + base), axis=0, keepdims=True) - 1
    return rank, first, second


def one_hot(rank):
    place = lax.broadcasted_iota(jnp.int32, (CAP, SEQ), 0)
    return jnp.where(place == rank, 1.0, 0.0).astype(bf16)


def pick_kernel(
    sel_ref, ids_ref, tok_ref, cot_ref, vec_ref,
    x_ref, dy_ref, a_ref, at_ref, dm_ref, rank_ref, bounds_ref, x_scr, dy_scr,
):
    rank, first, second = ranks_of(sel_ref[0], ids_ref[0])
    rank_ref[0] = jnp.broadcast_to(rank, (8, SEQ))
    lane = lax.broadcasted_iota(jnp.int32, (8, 128), 1)
    bounds_ref[0] = jnp.where(lane == 0, first, second)
    hot = one_hot(rank)
    x_scr[...] = dot_ab(hot, tok_ref[0])
    dy_scr[...] = dot_ab(hot, cot_ref[0])
    tile = 128

    def body(i, carry):
        rows = pl.ds(pl.multiple_of(i * tile, tile), tile)
        x = x_scr[rows, :]
        dy = dy_scr[rows, :]
        normalized, _ = norm_parts(x)
        low = (normalized * vec_ref[0:1, :] + vec_ref[1:2, :]).astype(bf16)
        gate = jax.nn.sigmoid(jnp.sum(x * vec_ref[4:5, :], -1, keepdims=True) * ROUTER_SCALE)
        x_ref[rows, :] = x.astype(bf16)
        dy_ref[rows, :] = dy.astype(bf16)
        a_ref[rows, :] = low
        dm_ref[rows, :] = (gate * dy).astype(bf16)
        return carry

    lax.fori_loop(0, CAP // tile, body, 0)
    at_ref[...] = a_ref[...].T


def pick_rows(sel, ids, tokens, cotangent, vectors):
    rows = tokens.shape[0]
    count = rows * CAP
    wide = pl.BlockSpec((CAP, D), lambda r: (r, 0))
    line = pl.BlockSpec((1, 1, SEQ), lambda r: (r, 0, 0))
    full = pl.BlockSpec((1, SEQ, D), lambda r: (r, 0, 0))
    return pl.pallas_call(
        pick_kernel,
        grid=(rows,),
        in_specs=[line, line, full, full, pl.BlockSpec((7, D), lambda r: (0, 0))],
        out_specs=[
            wide, wide, wide, pl.BlockSpec((D, CAP), lambda r: (0, r)), wide,
            pl.BlockSpec((1, 8, SEQ), lambda r: (r, 0, 0)),
            pl.BlockSpec((1, 8, 128), lambda r: (r, 0, 0)),
        ],
        out_shape=[
            jax.ShapeDtypeStruct((count, D), bf16),
            jax.ShapeDtypeStruct((count, D), bf16),
            jax.ShapeDtypeStruct((count, D), bf16),
            jax.ShapeDtypeStruct((D, count), bf16),
            jax.ShapeDtypeStruct((count, D), bf16),
            jax.ShapeDtypeStruct((rows, 8, SEQ), jnp.int32),
            jax.ShapeDtypeStruct((rows, 8, 128), jnp.int32),
        ],
        scratch_shapes=[pltpu.VMEM((CAP, D), f32), pltpu.VMEM((CAP, D), f32)],
        compiler_params=params(48),
        cost_estimate=cost(4 * count * SEQ * D, 4 * rows * SEQ * D * 2),
        name="pick_rows",
    )(sel[:, None, :], ids[:, None, :], tokens, cotangent, vectors)


def fill_bias(bias_scr, bounds_ref):
    first = bounds_ref[0, 0:1, 0:1]
    second = bounds_ref[0, 0:1, 1:2]
    tile = 128
    key = lax.broadcasted_iota(jnp.int32, (tile, CAP), 1)
    key_kind = jnp.where(key >= first, 1, 0) + jnp.where(key >= second, 1, 0)
    for i in range(CAP // tile):
        row = lax.broadcasted_iota(jnp.int32, (tile, CAP), 0) + i * tile
        row_kind = jnp.where(row >= first, 1, 0) + jnp.where(row >= second, 1, 0)
        bias_scr[i * tile : (i + 1) * tile, :] = jnp.where(row_kind == key_kind, 0.0, masked_score)


def half_masks():
    lane = lax.broadcasted_iota(jnp.int32, (1, 128), 1)
    low = jnp.where(lane < HEAD_DIM, 1.0, 0.0)
    return low, 1.0 - low


def attend_kernel(
    a_ref, wq_ref, wk_ref, wv_ref, bounds_ref,
    q_ref, k_ref, v_ref, ctx_ref, lse_ref, bias_scr,
):
    group = pl.program_id(1)

    @pl.when(group == 0)
    def _():
        fill_bias(bias_scr, bounds_ref)
        lse_ref[...] = jnp.zeros_like(lse_ref)

    a = a_ref[...]
    q_ref[...] = dot_ab(a, wq_ref[...]).astype(bf16)
    k_ref[...] = dot_ab(a, wk_ref[...]).astype(bf16)
    v_ref[...] = dot_ab(a, wv_ref[...]).astype(bf16)
    masks = half_masks()
    lane = lax.broadcasted_iota(jnp.int32, (1, 128), 1)
    for pair in range(GROUP // 128):
        cols = slice(pair * 128, pair * 128 + 128)
        queries, key_rows, values = q_ref[:, cols], k_ref[:, cols], v_ref[:, cols]
        halves = []
        for half in range(2):
            scores = dot_ab(queries * masks[half].astype(bf16), key_rows, 1, 1)
            scores = scores * (SCORE_SCALE * LOG2E) + bias_scr[...]
            row_max = jnp.max(scores, -1, keepdims=True)
            probs = jnp.exp2(scores - row_max)
            row_total = jnp.sum(probs, -1, keepdims=True)
            out = dot_ab(probs.astype(bf16), values)
            halves.append(out * (1.0 / row_total))
            head = group * (GROUP // HEAD_DIM) + pair * 2 + half
            lse_ref[...] = jnp.where(lane == head, row_max + jnp.log2(row_total), lse_ref[...])
        ctx_ref[:, cols] = jnp.where(lane < HEAD_DIM, halves[0], halves[1]).astype(bf16)


def attend_forward(a, weights, bounds):
    count = a.shape[0]
    rows = count // CAP
    piece = pl.BlockSpec((CAP, GROUP), lambda r, g: (r, g))
    narrow = jax.ShapeDtypeStruct((count, D), bf16)
    return pl.pallas_call(
        attend_kernel,
        grid=(rows, GROUPS),
        in_specs=[
            pl.BlockSpec((CAP, D), lambda r, g: (r, 0)),
            pl.BlockSpec((D, GROUP), lambda r, g: (0, g)),
            pl.BlockSpec((D, GROUP), lambda r, g: (0, g + GROUPS)),
            pl.BlockSpec((D, GROUP), lambda r, g: (0, g + 2 * GROUPS)),
            pl.BlockSpec((1, 8, 128), lambda r, g: (r, 0, 0)),
        ],
        out_specs=[piece, piece, piece, piece, pl.BlockSpec((CAP, 128), lambda r, g: (r, 0))],
        out_shape=[narrow, narrow, narrow, narrow, jax.ShapeDtypeStruct((count, 128), f32)],
        scratch_shapes=[pltpu.VMEM((CAP, CAP), f32)],
        compiler_params=params(48),
        cost_estimate=cost(
            2 * count * D * 3 * D + rows * HEADS * 16 * CAP * CAP * HEAD_DIM, 12 * count * D,
            rows * HEADS * CAP * CAP,
        ),
        name="attend_forward",
    )(a, weights, weights, weights, bounds)


def attend_back_kernel(
    me_ref, at_ref, q_ref, k_ref, v_ref, ctx_ref, dctx_ref, lse_ref, bounds_ref, gwo_ref,
    dq_ref, dk_ref, dv_ref, keep_ref, send_ref, bias_scr, acc_scr, *, plan,
):
    group, row = pl.program_id(0), pl.program_id(1)
    fill_bias(bias_scr, bounds_ref)
    masks = half_masks()
    lane = lax.broadcasted_iota(jnp.int32, (1, 128), 1)
    for pair in range(GROUP // 128):
        cols = slice(pair * 128, pair * 128 + 128)
        queries, key_rows, values = q_ref[:, cols], k_ref[:, cols], v_ref[:, cols]
        grads = dctx_ref[:, cols]
        product = ctx_ref[:, cols].astype(f32) * grads.astype(f32)
        queries_t, grads_t = queries.T, grads.T
        dq, dk_t, dv_t = [], [], []
        for half in range(2):
            mask_low = masks[half].astype(bf16)
            span = slice(half * HEAD_DIM, half * HEAD_DIM + HEAD_DIM)
            head = group * (GROUP // HEAD_DIM) + pair * 2 + half
            log_total = jnp.sum(jnp.where(lane == head, lse_ref[...], 0.0), -1, keepdims=True)
            delta = jnp.sum(product * masks[half], -1, keepdims=True)
            scores = dot_ab(queries * mask_low, key_rows, 1, 1)
            scores = scores * (SCORE_SCALE * LOG2E) + bias_scr[...]
            probs = jnp.exp2(scores - log_total)
            probs_grad = dot_ab(grads * mask_low, values, 1, 1)
            score_grad = (probs * (probs_grad - delta)).astype(bf16)
            dq.append(dot_ab(score_grad, key_rows))
            dk_t.append(dot_ab(queries_t[span], score_grad))
            dv_t.append(dot_ab(grads_t[span], probs.astype(bf16)))
        dq_ref[:, cols] = (jnp.where(lane < HEAD_DIM, dq[0], dq[1]) * SCORE_SCALE).astype(bf16)
        dk_ref[:, cols] = (jnp.concatenate(dk_t, 0) * SCORE_SCALE).astype(bf16).T
        dv_ref[:, cols] = jnp.concatenate(dv_t, 0).astype(bf16).T
    at = at_ref[...]
    for part, ref in enumerate((dq_ref, dk_ref, dv_ref)):
        span = slice(part * GROUP, part * GROUP + GROUP)
        product = dot_ab(at, ref[...])

        @pl.when(row == 0)
        def _():
            acc_scr[:, span] = product

        @pl.when(row > 0)
        def _():
            acc_scr[:, span] = acc_scr[:, span] + product

    @pl.when(row == pl.num_programs(1) - 1)
    def _():
        acc_scr[:, 3 * GROUP :] = gwo_ref[...]
        split_blocks(me_ref, acc_scr, keep_ref, send_ref, plan)


def split_blocks(me_ref, acc_scr, keep_ref, send_ref, plan):
    if plan is None:
        keep_ref[0] = acc_scr[...].astype(bf16)
        send_ref[0] = jnp.zeros_like(send_ref[0])
        return
    blocks, core_bit = plan
    size = D // blocks
    me = me_ref[0]
    on_high = (me & core_bit) != 0
    for block in range(blocks):
        if block & core_bit:
            continue
        low = acc_scr[block * size : (block + 1) * size, :]
        other = block | core_bit
        high = acc_scr[other * size : (other + 1) * size, :]
        place = me ^ block
        slot = (place // (2 * core_bit)) * core_bit + place % core_bit
        keep_ref[slot] = jnp.where(on_high, high, low).astype(bf16)
        send_ref[slot] = jnp.where(on_high, low, high).astype(bf16)


def attend_backward(me, at, q, k, v, ctx, dctx, lse, bounds, gwo, plan):
    count = q.shape[0]
    rows = count // CAP
    piece = pl.BlockSpec((CAP, GROUP), lambda g, r, me: (r, g))
    narrow = jax.ShapeDtypeStruct((count, D), bf16)
    if plan is None:
        half, size, sent = 1, D, 8
    else:
        half, size = plan[0] // 2, D // plan[0]
        sent = size
    width = 4 * GROUP
    return pl.pallas_call(
        partial(attend_back_kernel, plan=plan),
        grid_spec=pltpu.PrefetchScalarGridSpec(
            num_scalar_prefetch=1,
            grid=(GROUPS, rows),
            in_specs=[
                pl.BlockSpec((D, CAP), lambda g, r, me: (0, r)),
                piece, piece, piece, piece, piece,
                pl.BlockSpec((CAP, 128), lambda g, r, me: (r, 0)),
                pl.BlockSpec((1, 8, 128), lambda g, r, me: (r, 0, 0)),
                pl.BlockSpec((D, GROUP), lambda g, r, me: (0, g)),
            ],
            out_specs=[
                piece, piece, piece,
                pl.BlockSpec((half, size, width), lambda g, r, me: (0, 0, g)),
                pl.BlockSpec((half, sent, width), lambda g, r, me: (0, 0, g)),
            ],
            scratch_shapes=[pltpu.VMEM((CAP, CAP), f32), pltpu.VMEM((D, width), f32)],
        ),
        out_shape=[
            narrow, narrow, narrow,
            jax.ShapeDtypeStruct((half, size, 4 * D), bf16),
            jax.ShapeDtypeStruct((half, sent, 4 * D), bf16),
        ],
        compiler_params=params(56),
        cost_estimate=cost(
            2 * count * D * 3 * D + rows * HEADS * 40 * CAP * CAP * HEAD_DIM, 20 * count * D,
            rows * HEADS * CAP * CAP,
        ),
        name="attend_backward",
    )(me, at, q, k, v, ctx, dctx, lse, bounds, gwo)


def middle_kernel(ctx_ref, wo_ref, x_ref, vec_ref, att_ref, c_ref):
    att = dot_ab(ctx_ref[...], wo_ref[...]) + vec_ref[5:6, :]
    att_ref[...] = att
    normalized, _ = norm_parts(x_ref[...].astype(f32) + att)
    c_ref[...] = (normalized * vec_ref[2:3, :] + vec_ref[3:4, :]).astype(bf16)


def middle(ctx, weights, x, vectors):
    count = ctx.shape[0]
    tile = 320
    wide = pl.BlockSpec((tile, D), lambda t: (t, 0))
    return pl.pallas_call(
        middle_kernel,
        grid=(count // tile,),
        in_specs=[
            wide, pl.BlockSpec((D, D), lambda t: (0, 3)), wide,
            pl.BlockSpec((7, D), lambda t: (0, 0)),
        ],
        out_specs=[wide, wide],
        out_shape=[
            jax.ShapeDtypeStruct((count, D), f32),
            jax.ShapeDtypeStruct((count, D), bf16),
        ],
        compiler_params=params(32),
        cost_estimate=cost(2 * count * D * D, 10 * count * D),
        name="middle",
    )(ctx, weights, x, vectors)


ERF_P = 0.3275911 / math.sqrt(2.0)
ERF_COEF = (0.254829592, -0.284496736, 1.421413741, -1.453152027, 1.061405429)


def gelu_parts(u):
    bell = jnp.exp2(u * u * (-0.5 * LOG2E))
    t = 1.0 / (1.0 + ERF_P * jnp.abs(u))
    poly = ERF_COEF[4]
    for coef in ERF_COEF[3::-1]:
        poly = poly * t + coef
    tail = (0.5 * poly * t) * bell
    phi = jnp.where(u >= 0, 1.0 - tail, tail)
    return u * phi, phi + u * (bell * (1.0 / math.sqrt(2.0 * math.pi)))


def mlp_kernel(
    me_ref, c_ref, dm_ref, wu_ref, wd_ref, bias_ref,
    mlp_ref, dc_ref, keep_ref, send_ref, gbias_ref, ct_scr, dmt_scr, *, blocks, split,
):
    first = (pl.program_id(0) == 0) & (pl.program_id(1) == 0)

    @pl.when(first)
    def _():
        ct_scr[...] = c_ref[...].T
        dmt_scr[...] = dm_ref[...].T
        mlp_ref[...] = jnp.zeros_like(mlp_ref)
        dc_ref[...] = jnp.zeros_like(dc_ref)

    width = wu_ref.shape[-1]
    wu = wu_ref[...].reshape(D, width)
    wd = wd_ref[...].reshape(D, width)
    u = dot_ab(c_ref[...], wu) + bias_ref[0]
    act, slope = gelu_parts(u)
    act = act.astype(bf16)
    du = slope * dot_ab(dm_ref[...], wd)
    du = du.astype(bf16)
    gbias_ref[0] = jnp.broadcast_to(jnp.sum(du.astype(f32), 0, keepdims=True), (8, width))
    mlp_ref[...] += dot_ab(act, wd, 1, 1)
    dc_ref[...] += dot_ab(du, wu, 1, 1)
    size = D // blocks
    for which, grad in enumerate((dot_ab(ct_scr[...], du), dot_ab(dmt_scr[...], act))):
        if not split:
            keep_ref[0, 0, which] = grad.astype(bf16)
            continue
        on_high = (me_ref[2] & 1) != 0
        for block in range(0, blocks, 2):
            low = grad[block * size : (block + 1) * size]
            high = grad[(block + 1) * size : (block + 2) * size]
            keep_ref[block // 2, 0, which] = jnp.where(on_high, high, low).astype(bf16)
            send_ref[block // 2, 0, which] = jnp.where(on_high, low, high).astype(bf16)
    if not split:
        send_ref[...] = jnp.zeros_like(send_ref)


def mlp_all(me, c, dm, weights, bias, split):
    count = c.shape[0]
    blocks, mp, _, size, units = weights.shape
    width = 384
    subs = units // width
    half = blocks // 2 if split else 1
    sent = size if split else 8
    rows_out = size if split else D
    all_rows = pl.BlockSpec((count, D), lambda j, s, me: (0, 0))

    def weight_spec(which):
        return pl.BlockSpec(
            (blocks, 1, 1, size, width), lambda j, s, me, which=which: (0, me[1] ^ j, which, 0, s)
        )

    return pl.pallas_call(
        partial(mlp_kernel, blocks=blocks, split=split),
        grid_spec=pltpu.PrefetchScalarGridSpec(
            num_scalar_prefetch=1,
            grid=(mp, subs),
            in_specs=[
                all_rows, all_rows, weight_spec(0), weight_spec(1),
                pl.BlockSpec((1, 1, width), lambda j, s, me: ((me[1] ^ j) * subs + s, 0, 0)),
            ],
            out_specs=[
                all_rows, all_rows,
                pl.BlockSpec((half, 1, 2, rows_out, width), lambda j, s, me: (0, j, 0, 0, s)),
                pl.BlockSpec((half, 1, 2, sent, width), lambda j, s, me: (0, j, 0, 0, s)),
                pl.BlockSpec((1, 8, width), lambda j, s, me: ((me[1] ^ j) * subs + s, 0, 0)),
            ],
            scratch_shapes=[pltpu.VMEM((D, count), bf16), pltpu.VMEM((D, count), bf16)],
        ),
        out_shape=[
            jax.ShapeDtypeStruct((count, D), f32),
            jax.ShapeDtypeStruct((count, D), f32),
            jax.ShapeDtypeStruct((half, mp, 2, rows_out, units), bf16),
            jax.ShapeDtypeStruct((half, mp, 2, sent, units), bf16),
            jax.ShapeDtypeStruct((mp * subs, 8, width), f32),
        ],
        compiler_params=params(58),
        cost_estimate=cost(
            12 * count * D * mp * units, 12 * count * D + 8 * mp * units * D, 2 * count * mp * units
        ),
        name="mlp_all",
    )(me, c, dm, weights, weights, bias.reshape(mp * subs, 1, width))


def turn_kernel(
    x_ref, dy_ref, att_ref, mlp_ref, dc_ref, ctx_ref, wo_ref, vec_ref,
    y_ref, part_ref, dctx_ref, gwo_ref, gvec_ref, datt_scr,
):
    step = pl.program_id(0)

    @pl.when(step == 0)
    def _():
        gvec_ref[...] = jnp.zeros_like(gvec_ref)
        gwo_ref[...] = jnp.zeros_like(gwo_ref)

    tile = 64
    router = vec_ref[4:5, :]

    def body(i, carry):
        rows = pl.ds(pl.multiple_of(i * tile, tile), tile)
        x = x_ref[rows, :].astype(f32)
        dy = dy_ref[rows, :].astype(f32)
        att = att_ref[rows, :]
        branch = att + mlp_ref[rows, :] + vec_ref[6:7, :]
        gate = jax.nn.sigmoid(jnp.sum(x * router, -1, keepdims=True) * ROUTER_SCALE)
        y_ref[rows, :] = (x + gate * branch).astype(bf16)
        dr = jnp.sum(dy * branch, -1, keepdims=True) * gate * (1.0 - gate) * ROUTER_SCALE
        e = gate * dy
        normalized, inverse = norm_parts(x + att)
        dc = dc_ref[rows, :]
        dh = norm_back(dc, normalized, inverse, vec_ref[2:3, :])
        datt = (e + dh).astype(bf16)
        datt_scr[rows, :] = datt
        part_ref[rows, :] = dy + dr * router + dh
        for place, term in enumerate(
            (dc * normalized, dc, dr * x, datt.astype(f32), e.astype(bf16).astype(f32))
        ):
            gvec_ref[place : place + 1, :] += jnp.sum(term, 0, keepdims=True)
        return carry

    lax.fori_loop(0, x_ref.shape[0] // tile, body, 0)
    datt = datt_scr[...]
    dctx_ref[...] = dot_ab(datt, wo_ref[...], 1, 1).astype(bf16)
    gwo_ref[...] += dot_ab(ctx_ref[...], datt, 0, 0)


def turn(x, dy, att, mlp, dc, ctx, weights, vectors):
    count = x.shape[0]
    tile = 320
    wide = pl.BlockSpec((tile, D), lambda t: (t, 0))
    return pl.pallas_call(
        turn_kernel,
        grid=(count // tile,),
        in_specs=[
            wide, wide, wide, wide, wide, wide, pl.BlockSpec((D, D), lambda t: (0, 3)),
            pl.BlockSpec((7, D), lambda t: (0, 0)),
        ],
        out_specs=[
            wide, wide, wide, pl.BlockSpec((D, D), lambda t: (0, 0)),
            pl.BlockSpec((8, D), lambda t: (0, 0)),
        ],
        out_shape=[
            jax.ShapeDtypeStruct((count, D), bf16),
            jax.ShapeDtypeStruct((count, D), f32),
            jax.ShapeDtypeStruct((count, D), bf16),
            jax.ShapeDtypeStruct((D, D), f32),
            jax.ShapeDtypeStruct((8, D), f32),
        ],
        scratch_shapes=[pltpu.VMEM((tile, D), bf16)],
        compiler_params=params(48),
        cost_estimate=cost(4 * count * D * D, 26 * count * D),
        name="turn",
    )(x, dy, att, mlp, dc, ctx, weights, vectors)


def finish_kernel(
    dq_ref, dk_ref, dv_ref, wq_ref, wk_ref, wv_ref, x_ref, part_ref, vec_ref, rank_ref, cot_ref,
    out_ref, gvec_ref, da_scr, hi_scr,
):
    @pl.when(pl.program_id(0) == 0)
    def _():
        gvec_ref[...] = jnp.zeros_like(gvec_ref)

    da = dot_ab(dq_ref[...], wq_ref[...], 1, 1)
    da += dot_ab(dk_ref[...], wk_ref[...], 1, 1)
    da_scr[...] = da + dot_ab(dv_ref[...], wv_ref[...], 1, 1)
    tile = 64

    def body(i, carry):
        rows = pl.ds(pl.multiple_of(i * tile, tile), tile)
        normalized, inverse = norm_parts(x_ref[rows, :].astype(f32))
        da = da_scr[rows, :]
        for place, term in enumerate((da * normalized, da)):
            gvec_ref[place : place + 1, :] += jnp.sum(term, 0, keepdims=True)
        grad = part_ref[rows, :] + norm_back(da, normalized, inverse, vec_ref[0:1, :])
        high = grad.astype(bf16)
        hi_scr[rows, 0:D] = high
        hi_scr[rows, D : 2 * D] = (grad - high.astype(f32)).astype(bf16)
        hi_scr[rows, 2 * D :] = jnp.ones((tile, 128), bf16)
        return carry

    lax.fori_loop(0, CAP // tile, body, 0)
    hot = one_hot(rank_ref[0, 0:1, :])
    placed = dot_ab(hot, hi_scr[...], 0, 0)
    kept = 1.0 - placed[:, 2 * D : 2 * D + 1]
    out_ref[0] = placed[:, 0:D] + placed[:, D : 2 * D] + kept * cot_ref[0].astype(f32)


def finish(dq, dk, dv, weights, x, part, vectors, rank, cotangent):
    count = x.shape[0]
    rows = count // CAP
    wide = pl.BlockSpec((CAP, D), lambda r: (r, 0))

    def weight_spec(which):
        return pl.BlockSpec((D, D), lambda r, which=which: (0, which))

    return pl.pallas_call(
        finish_kernel,
        grid=(rows,),
        in_specs=[
            wide, wide, wide, weight_spec(0), weight_spec(1), weight_spec(2), wide, wide,
            pl.BlockSpec((7, D), lambda r: (0, 0)),
            pl.BlockSpec((1, 8, SEQ), lambda r: (r, 0, 0)),
            pl.BlockSpec((1, SEQ, D), lambda r: (r, 0, 0)),
        ],
        out_specs=[
            pl.BlockSpec((1, SEQ, D), lambda r: (r, 0, 0)),
            pl.BlockSpec((8, D), lambda r: (0, 0)),
        ],
        out_shape=[
            jax.ShapeDtypeStruct((rows, SEQ, D), f32),
            jax.ShapeDtypeStruct((8, D), f32),
        ],
        scratch_shapes=[pltpu.VMEM((CAP, D), f32), pltpu.VMEM((CAP, 2 * D + 128), bf16)],
        compiler_params=params(60),
        cost_estimate=cost(2 * count * D * 3 * D + 6 * count * SEQ * D, 24 * count * D),
        name="finish",
    )(dq, dk, dv, weights, weights, weights, x, part, vectors, rank, cotangent)


def place_kernel(y_ref, rank_ref, tok_ref, out_ref, ext_scr):
    ext_scr[:, 0:D] = y_ref[...]
    ext_scr[:, D:] = jnp.ones((CAP, 128), bf16)
    placed = dot_ab(one_hot(rank_ref[0, 0:1, :]), ext_scr[...], 0, 0)
    kept = 1.0 - placed[:, D : D + 1]
    out_ref[0] = (placed[:, 0:D] + kept * tok_ref[0].astype(f32)).astype(bf16)


def place(y, rank, tokens):
    rows = tokens.shape[0]
    return pl.pallas_call(
        place_kernel,
        grid=(rows,),
        in_specs=[
            pl.BlockSpec((CAP, D), lambda r: (r, 0)),
            pl.BlockSpec((1, 8, SEQ), lambda r: (r, 0, 0)),
            pl.BlockSpec((1, SEQ, D), lambda r: (r, 0, 0)),
        ],
        out_specs=pl.BlockSpec((1, SEQ, D), lambda r: (r, 0, 0)),
        out_shape=jax.ShapeDtypeStruct((rows, SEQ, D), bf16),
        scratch_shapes=[pltpu.VMEM((CAP, D + 128), bf16)],
        compiler_params=params(48),
        cost_estimate=cost(2 * rows * CAP * SEQ * D, 10 * rows * CAP * D),
        name="place",
    )(y, rank, tokens)


def order_kernel(me_ref, *refs, plan):
    blocks, core_bit, mp, bit_orders = plan
    *sources, out_ref, sem = refs
    size = D // blocks
    me = me_ref[0]
    copies = []
    for half, bits in enumerate(bit_orders):
        for side in range(2):
            source = sources[half * 2 + side]
            for slot in range(blocks // 2):
                place, rest = slot % mp, slot // mp
                for bit in bits:
                    place |= mp * bit * (rest & 1)
                    rest >>= 1
                place |= core_bit * side
                start = pl.multiple_of((me ^ place) * size, 8)
                copies.append(
                    pltpu.make_async_copy(
                        source.at[slot],
                        out_ref.at[pl.ds(start, size), pl.ds(half * 2 * D, 2 * D)],
                        sem,
                    )
                )
    for copy in copies:
        copy.start()
    for copy in copies:
        copy.wait()


def in_order(me, pieces, plan):
    anywhere = pl.BlockSpec(memory_space=pl.ANY)
    return pl.pallas_call(
        partial(order_kernel, plan=plan),
        grid_spec=pltpu.PrefetchScalarGridSpec(
            num_scalar_prefetch=1,
            grid=(1,),
            in_specs=[anywhere] * len(pieces),
            out_specs=anywhere,
            scratch_shapes=[pltpu.SemaphoreType.DMA],
        ),
        out_shape=jax.ShapeDtypeStruct((D, 4 * D), bf16),
        cost_estimate=cost(0, 16 * D * D),
        name="in_order",
    )(me, *pieces)


def lamb_moments(weight, gradient, first_mom, second_mom, decay):
    first_new = beta_one * first_mom + (1.0 - beta_one) * gradient
    second_new = beta_two * second_mom + (1.0 - beta_two) * gradient * gradient
    update = (
        first_new
        / (1.0 - beta_one**STEP)
        / (jnp.sqrt(second_new / (1.0 - beta_two**STEP)) + eps_adam)
        + decay * weight
    )
    return (first_new, second_new, update)


def swap(value, axis, size, bit):
    return lax.ppermute(value, axis, [(i, i ^ bit) for i in range(size)])


def on_device(
    tokens, image_ids, selected, cotangent,
    qkv_weight, qkv_first, qkv_second, proj_weight, proj_first, proj_second,
    up_weight, up_first, up_second, down_weight, down_first, down_second,
    up_bias, bias_first, bias_second, vectors, vector_first, vector_second,
    *, dp, mp,
):
    world = dp * mp
    dq_at, dc_at, mp_at = (lax.axis_index(name) for name in ("dq", "dc", "mp"))
    dp_at = dq_at * 2 + dc_at
    me = jnp.stack([dp_at * mp + mp_at, mp_at, dp_at]).astype(jnp.int32)
    everyone = ("dq", "dc", "mp")
    fast = (D // world) % 8 == 0 and dp >= 4 and (D // dp) % 16 == 0

    def swap_dp(value, bit):
        if bit == 1:
            return swap(value, "dc", 2, 1)
        return swap(value, "dq", dp // 2, bit // 2)

    def swap_mp(value, bit):
        return swap(value, "mp", mp, bit)

    bits = []
    bit = 2
    while bit < dp:
        bits.append(bit)
        bit *= 2
    bit_orders = (tuple(bits), tuple(reversed(bits)))

    attn_low = jnp.concatenate([qkv_weight, proj_weight], 1).astype(bf16)
    mlp_low = jnp.stack([up_weight.astype(bf16), down_weight.astype(bf16).T])
    if fast:
        rel = [attn_low[None]] + [swap_mp(attn_low[None], k) for k in range(1, mp)]
        rel = jnp.concatenate(rel, 0)
        pieces = []
        for half, order in enumerate(bit_orders):
            held = rel[:, :, half * 2 * D : (half + 1) * 2 * D]
            for bit in order:
                held = jnp.concatenate([held, swap_dp(held, bit)], 0)
            pieces += [held, swap_dp(held, 1)]
        attn_mat = in_order(me, pieces, (world, mp, mp, bit_orders))
    else:
        attn_mat = lax.all_gather(attn_low, everyone, axis=0, tiled=True)
    mlp_mat = lax.all_gather(mlp_low[None], everyone, axis=0, tiled=True)
    mlp_mat = mlp_mat.reshape(dp, mp, 2, D // dp, FF // mp)
    if not fast:
        mlp_mat = mlp_mat.transpose(1, 2, 0, 3, 4).reshape(1, mp, 2, D, FF // mp)

    x, dy, a, at, dm, rank, bounds = pick_rows(selected, image_ids, tokens, cotangent, vectors)
    q, k, v, ctx, lse = attend_forward(a, attn_mat, bounds)
    att, c = middle(ctx, attn_mat, x, vectors)
    mlp, dc, mlp_keep, mlp_send, bias_rows = mlp_all(me, c, dm, mlp_mat, up_bias, fast)
    y, part, dctx, gwo, gvec_two = turn(x, dy, att, mlp, dc, ctx, attn_mat, vectors)
    plan = (world, mp) if fast else None
    dq, dk, dv, attn_keep, attn_send = attend_backward(
        me, at, q, k, v, ctx, dctx, lse, bounds, gwo, plan
    )
    input_grad, gvec_one = finish(dq, dk, dv, attn_mat, x, part, vectors, rank, cotangent)
    block_output = place(y, rank, tokens)

    def add(kept, came):
        return (kept.astype(f32) + came.astype(f32)).astype(bf16)

    if fast:
        both = add(mlp_keep, swap_dp(mlp_send, 1))
        mine = lax.psum_scatter(both, "dq", scatter_dimension=0, tiled=True)[0]
        mlp_sum = mine[0].astype(f32)
        for k_at in range(1, mp):
            mlp_sum = mlp_sum + swap_mp(mine[k_at], k_at).astype(f32)
        both = add(attn_keep, swap_dp(attn_send, 1))
        parts = []
        for half, order in enumerate(bit_orders):
            held = both[:, :, half * 2 * D : (half + 1) * 2 * D]
            held = held.reshape((2,) * len(bits) + (mp, D // world, 2 * D))
            left = list(reversed(bits))
            for bit in reversed(order):
                axis = left.index(bit)
                left.remove(bit)
                low = lax.index_in_dim(held, 0, axis, False)
                high = lax.index_in_dim(held, 1, axis, False)
                held = add(low, swap_dp(high, bit))
            total = held[0].astype(f32)
            for k_at in range(1, mp):
                total = total + swap_mp(held[k_at], k_at).astype(f32)
            parts.append(total)
        attn_sum = jnp.concatenate(parts, 1)
    else:
        shaped = mlp_keep[0].reshape(mp, 2, dp, D // dp, FF // mp)
        shaped = jnp.take(shaped, mp_at ^ jnp.arange(mp), axis=0)
        shaped = shaped.transpose(2, 0, 1, 3, 4).reshape(world, 2, D // dp, FF // mp)
        mlp_sum = lax.psum_scatter(shaped, everyone, scatter_dimension=0, tiled=True)[0]
        mlp_sum = mlp_sum.astype(f32)
        attn_sum = lax.psum_scatter(attn_keep[0], everyone, scatter_dimension=0, tiled=True)
        attn_sum = attn_sum.astype(f32)
    attn_sum = attn_sum.reshape(D // world, GROUPS, 4, GROUP).transpose(0, 2, 1, 3)
    attn_sum = attn_sum.reshape(D // world, 4 * D)
    qkv_sum, proj_sum = attn_sum[:, : 3 * D], attn_sum[:, 3 * D :]
    up_sum, down_sum = mlp_sum[0], mlp_sum[1].T

    qkv_first_new, qkv_second_new, qkv_upd = lamb_moments(
        qkv_weight, qkv_sum, qkv_first, qkv_second, decay_mat
    )
    proj_first_new, proj_second_new, proj_upd = lamb_moments(
        proj_weight, proj_sum, proj_first, proj_second, decay_mat
    )
    up_first_new, up_second_new, up_upd = lamb_moments(
        up_weight, up_sum, up_first, up_second, decay_mat
    )
    down_first_new, down_second_new, down_upd = lamb_moments(
        down_weight, down_sum, down_first, down_second, decay_mat
    )
    squares = jnp.stack(
        [
            jnp.sum(value * value)
            for value in (
                qkv_weight, proj_weight, up_weight, down_weight,
                qkv_upd, proj_upd, up_upd, down_upd,
            )
        ]
    )
    small = jnp.concatenate(
        [
            gvec_one[0:2].reshape(-1),
            gvec_two[0:5].reshape(-1),
            bias_rows[:, 0, :].reshape(-1),
            jnp.pad(squares, (0, 120)),
        ]
    ).reshape(-1, 128)
    if fast:
        bit = 1
        while bit < dp:
            small = small + swap_dp(small, bit)
            bit *= 2
        bit = 1
        while bit < mp:
            small = small + swap_mp(small, bit)
            bit *= 2
    else:
        small = lax.psum(small, everyone)
    small = small.reshape(-1)
    vector_sum = small[: 7 * D].reshape(7, D)
    bias_sum = small[7 * D : 7 * D + FF]
    weight_norms = jnp.sqrt(small[7 * D + FF : 7 * D + FF + 8]).reshape(2, 4)
    ratios = weight_norms[0] / weight_norms[1]
    qkv_new = qkv_weight - rate_lamb * ratios[0] * qkv_upd
    proj_new = proj_weight - rate_lamb * ratios[1] * proj_upd
    up_new = up_weight - rate_lamb * ratios[2] * up_upd
    down_new = down_weight - rate_lamb * ratios[3] * down_upd
    bias_first_new, bias_second_new, bias_upd = lamb_moments(
        up_bias, bias_sum, bias_first, bias_second, 0.0
    )
    bias_ratio = jnp.sqrt(jnp.sum(up_bias * up_bias)) / jnp.sqrt(jnp.sum(bias_upd * bias_upd))
    bias_new = up_bias - rate_lamb * bias_ratio * bias_upd
    vector_first_new, vector_second_new, vector_upd = lamb_moments(
        vectors, vector_sum, vector_first, vector_second, 0.0
    )
    vector_ratio = jnp.sqrt(jnp.sum(vectors * vectors, -1, keepdims=True)) / jnp.sqrt(
        jnp.sum(vector_upd * vector_upd, -1, keepdims=True)
    )
    vectors_new = vectors - rate_lamb * vector_ratio * vector_upd
    return (
        block_output, input_grad, weight_norms,
        qkv_new, qkv_first_new, qkv_second_new,
        proj_new, proj_first_new, proj_second_new,
        up_new, up_first_new, up_second_new,
        down_new, down_first_new, down_second_new,
        bias_new, bias_first_new, bias_second_new,
        vectors_new, vector_first_new, vector_second_new,
    )


def solution(mesh):
    dp, mp = mesh.shape["dp"], mesh.shape["mp"]
    split = Mesh(mesh.devices.reshape(dp // 2, 2, mp), ("dq", "dc", "mp"))
    rows = ("dq", "dc", "mp")
    by_rows = (P(rows, None),) * 3
    shared = (P(),) * 3
    up_spec = (P(("dq", "dc"), "mp"),) * 3
    down_spec = (P("mp", ("dq", "dc")),) * 3
    in_specs = (
        (P(rows, None, None), P(rows, None), P(rows, None), P(rows, None, None))
        + by_rows + by_rows + up_spec + down_spec + shared + shared
    )
    out_specs = (
        (P(rows, None, None), P(rows, None, None), P())
        + by_rows + by_rows + up_spec + down_spec + shared + shared
    )
    return jax.shard_map(
        partial(on_device, dp=dp, mp=mp),
        mesh=split, in_specs=in_specs, out_specs=out_specs, check_vma=False,
    )
```

```python
from functools import partial
import math

import jax
import jax.numpy as jnp
from jax import lax
from jax.experimental import pallas as pl
from jax.experimental.pallas import tpu as pltpu
from jax.sharding import Mesh, PartitionSpec as P

D = 768
FF = 3072
HEADS = 12
HEAD_DIM = 64
CAP = 640
SEQ = 1280
STEP = 10

eps_norm = 1e-06
eps_adam = 1e-06
beta_one = 0.9
beta_two = 0.999
decay_mat = 0.01
rate_lamb = 0.3
masked_score = -1e30

f32 = jnp.float32
bf16 = jnp.bfloat16
GROUP = 256
GROUPS = D // GROUP
LOG2E = 1.0 / math.log(2.0)
SCORE_SCALE = 1.0 / math.sqrt(HEAD_DIM)
ROUTER_SCALE = 1.0 / math.sqrt(D)


def dot_ab(left, right, left_dim=1, right_dim=0):
    return lax.dot_general(
        left, right, (((left_dim,), (right_dim,)), ((), ())), preferred_element_type=f32
    )


def params(mib, **more):
    return pltpu.CompilerParams(vmem_limit_bytes=mib << 20, **more)


def cost(flops, nbytes, trans=0):
    return pl.CostEstimate(flops=int(flops), bytes_accessed=int(nbytes), transcendentals=int(trans))


def norm_parts(values):
    center = jnp.mean(values, -1, keepdims=True)
    offset = values - center
    spread = jnp.mean(offset * offset, -1, keepdims=True)
    inverse = lax.rsqrt(spread + eps_norm)
    return offset * inverse, inverse


def norm_back(grad, normalized, inverse, gain):
    scaled = grad * gain
    return inverse * (
        scaled
        - jnp.mean(scaled, -1, keepdims=True)
        - normalized * jnp.mean(scaled * normalized, -1, keepdims=True)
    )


def ranks_of(sel, ids):
    kind = jnp.where(ids < 0, 2, ids)
    sub = lax.broadcasted_iota(jnp.int32, (8, SEQ), 0)
    lane = lax.broadcasted_iota(jnp.int32, (8, SEQ), 1)
    member = jnp.where(jnp.broadcast_to(kind, (8, SEQ)) == sub, jnp.broadcast_to(sel, (8, SEQ)), 0)
    total = member
    step = 1
    while step < SEQ:
        total = total + jnp.where(lane >= step, pltpu.roll(total, step, 1), 0)
        step *= 2
    count = jnp.max(total, axis=1, keepdims=True)
    first = count[0:1]
    second = first + count[1:2]
    base = jnp.where(sub == 0, 0, jnp.where(sub == 1, first, second))
    rank = jnp.sum(member * (total + base), axis=0, keepdims=True) - 1
    return rank, first, second


def one_hot(rank):
    place = lax.broadcasted_iota(jnp.int32, (CAP, SEQ), 0)
    return jnp.where(place == rank, 1.0, 0.0).astype(bf16)


def pick_kernel(
    sel_ref, ids_ref, tok_ref, cot_ref, vec_ref,
    x_ref, dy_ref, a_ref, at_ref, dm_ref, rank_ref, bounds_ref, x_scr, dy_scr,
):
    rank, first, second = ranks_of(sel_ref[0], ids_ref[0])
    rank_ref[0] = jnp.broadcast_to(rank, (8, SEQ))
    lane = lax.broadcasted_iota(jnp.int32, (8, 128), 1)
    bounds_ref[0] = jnp.where(lane == 0, first, second)
    hot = one_hot(rank)
    x_scr[...] = dot_ab(hot, tok_ref[0])
    dy_scr[...] = dot_ab(hot, cot_ref[0])
    tile = 128

    def body(i, carry):
        rows = pl.ds(pl.multiple_of(i * tile, tile), tile)
        x = x_scr[rows, :]
        dy = dy_scr[rows, :]
        normalized, _ = norm_parts(x)
        low = (normalized * vec_ref[0:1, :] + vec_ref[1:2, :]).astype(bf16)
        gate = jax.nn.sigmoid(jnp.sum(x * vec_ref[4:5, :], -1, keepdims=True) * ROUTER_SCALE)
        x_ref[rows, :] = x.astype(bf16)
        dy_ref[rows, :] = dy.astype(bf16)
        a_ref[rows, :] = low
        dm_ref[rows, :] = (gate * dy).astype(bf16)
        return carry

    lax.fori_loop(0, CAP // tile, body, 0)
    at_ref[...] = a_ref[...].T


def pick_rows(sel, ids, tokens, cotangent, vectors):
    rows = tokens.shape[0]
    count = rows * CAP
    wide = pl.BlockSpec((CAP, D), lambda r: (r, 0))
    line = pl.BlockSpec((1, 1, SEQ), lambda r: (r, 0, 0))
    full = pl.BlockSpec((1, SEQ, D), lambda r: (r, 0, 0))
    return pl.pallas_call(
        pick_kernel,
        grid=(rows,),
        in_specs=[line, line, full, full, pl.BlockSpec((7, D), lambda r: (0, 0))],
        out_specs=[
            wide, wide, wide, pl.BlockSpec((D, CAP), lambda r: (0, r)), wide,
            pl.BlockSpec((1, 8, SEQ), lambda r: (r, 0, 0)),
            pl.BlockSpec((1, 8, 128), lambda r: (r, 0, 0)),
        ],
        out_shape=[
            jax.ShapeDtypeStruct((count, D), bf16),
            jax.ShapeDtypeStruct((count, D), bf16),
            jax.ShapeDtypeStruct((count, D), bf16),
            jax.ShapeDtypeStruct((D, count), bf16),
            jax.ShapeDtypeStruct((count, D), bf16),
            jax.ShapeDtypeStruct((rows, 8, SEQ), jnp.int32),
            jax.ShapeDtypeStruct((rows, 8, 128), jnp.int32),
        ],
        scratch_shapes=[pltpu.VMEM((CAP, D), f32), pltpu.VMEM((CAP, D), f32)],
        compiler_params=params(40),
        cost_estimate=cost(4 * count * SEQ * D, 4 * rows * SEQ * D * 2),
        name="pick_rows",
    )(sel[:, None, :], ids[:, None, :], tokens, cotangent, vectors)


def fill_bias(bias_scr, bounds_ref):
    first = bounds_ref[0, 0:1, 0:1]
    second = bounds_ref[0, 0:1, 1:2]
    tile = 128
    key = lax.broadcasted_iota(jnp.int32, (tile, CAP), 1)
    key_kind = jnp.where(key >= first, 1, 0) + jnp.where(key >= second, 1, 0)
    for i in range(CAP // tile):
        row = lax.broadcasted_iota(jnp.int32, (tile, CAP), 0) + i * tile
        row_kind = jnp.where(row >= first, 1, 0) + jnp.where(row >= second, 1, 0)
        bias_scr[i * tile : (i + 1) * tile, :] = jnp.where(row_kind == key_kind, 0.0, masked_score)


def half_masks():
    lane = lax.broadcasted_iota(jnp.int32, (1, 128), 1)
    low = jnp.where(lane < HEAD_DIM, 1.0, 0.0)
    return low, 1.0 - low


def attend_kernel(
    a_ref, wqk_ref, wv_ref, bounds_ref,
    q_ref, k_ref, v_ref, ctx_ref, lse_ref, bias_scr,
):
    group = pl.program_id(1)

    @pl.when(group == 0)
    def _():
        fill_bias(bias_scr, bounds_ref)
        lse_ref[...] = jnp.zeros_like(lse_ref)

    a = a_ref[...]
    q_ref[...] = dot_ab(a, wqk_ref[:, :GROUP]).astype(bf16)
    k_ref[...] = dot_ab(a, wqk_ref[:, GROUP:]).astype(bf16)
    v_ref[...] = dot_ab(a, wv_ref[...]).astype(bf16)
    masks = half_masks()
    lane = lax.broadcasted_iota(jnp.int32, (1, 128), 1)
    for pair in range(GROUP // 128):
        cols = slice(pair * 128, pair * 128 + 128)
        queries, key_rows, values = q_ref[:, cols], k_ref[:, cols], v_ref[:, cols]
        halves = []
        for half in range(2):
            scores = dot_ab(queries * masks[half].astype(bf16), key_rows, 1, 1)
            scores = scores * (SCORE_SCALE * LOG2E) + bias_scr[...]
            row_max = jnp.max(scores, -1, keepdims=True)
            probs = jnp.exp2(scores - row_max)
            row_total = jnp.sum(probs, -1, keepdims=True)
            out = dot_ab(probs.astype(bf16), values)
            halves.append(out * (1.0 / row_total))
            head = group * (GROUP // HEAD_DIM) + pair * 2 + half
            lse_ref[...] = jnp.where(lane == head, row_max + jnp.log2(row_total), lse_ref[...])
        ctx_ref[:, cols] = jnp.where(lane < HEAD_DIM, halves[0], halves[1]).astype(bf16)


def attend_forward(a, w_qk, w_vo, bounds):
    count = a.shape[0]
    rows = count // CAP
    piece = pl.BlockSpec((CAP, GROUP), lambda r, g: (r, g))
    narrow = jax.ShapeDtypeStruct((count, D), bf16)
    return pl.pallas_call(
        attend_kernel,
        grid=(rows, GROUPS),
        in_specs=[
            pl.BlockSpec((CAP, D), lambda r, g: (r, 0)),
            pl.BlockSpec((D, 2 * GROUP), lambda r, g: (0, g)),
            pl.BlockSpec((D, GROUP), lambda r, g: (0, g)),
            pl.BlockSpec((1, 8, 128), lambda r, g: (r, 0, 0)),
        ],
        out_specs=[piece, piece, piece, piece, pl.BlockSpec((CAP, 128), lambda r, g: (r, 0))],
        out_shape=[narrow, narrow, narrow, narrow, jax.ShapeDtypeStruct((count, 128), f32)],
        scratch_shapes=[pltpu.VMEM((CAP, CAP), f32)],
        compiler_params=params(48),
        cost_estimate=cost(
            2 * count * D * 3 * D + rows * HEADS * 16 * CAP * CAP * HEAD_DIM, 12 * count * D,
            rows * HEADS * CAP * CAP,
        ),
        name="attend_forward",
    )(a, w_qk, w_vo, bounds)


def attend_back_kernel(
    me_ref, at_ref, q_ref, k_ref, v_ref, ctx_ref, dctx_ref, lse_ref, bounds_ref, gwo_ref,
    d_ref, keep_ref, send_ref, bias_scr, acc_scr, *, plan, start,
):
    group, row = pl.program_id(0) + start, pl.program_id(1)
    fill_bias(bias_scr, bounds_ref)
    masks = half_masks()
    lane = lax.broadcasted_iota(jnp.int32, (1, 128), 1)
    for pair in range(GROUP // 128):
        cols = slice(pair * 128, pair * 128 + 128)
        queries, key_rows, values = q_ref[:, cols], k_ref[:, cols], v_ref[:, cols]
        grads = dctx_ref[:, cols]
        product = ctx_ref[:, cols].astype(f32) * grads.astype(f32)
        queries_t, grads_t = queries.T, grads.T
        dq, dk_t, dv_t = [], [], []
        for half in range(2):
            mask_low = masks[half].astype(bf16)
            span = slice(half * HEAD_DIM, half * HEAD_DIM + HEAD_DIM)
            head = group * (GROUP // HEAD_DIM) + pair * 2 + half
            log_total = jnp.sum(jnp.where(lane == head, lse_ref[...], 0.0), -1, keepdims=True)
            delta = jnp.sum(product * masks[half], -1, keepdims=True)
            scores = dot_ab(queries * mask_low, key_rows, 1, 1)
            scores = scores * (SCORE_SCALE * LOG2E) + bias_scr[...]
            probs = jnp.exp2(scores - log_total)
            probs_grad = dot_ab(grads * mask_low, values, 1, 1)
            score_grad = (probs * (probs_grad - delta)).astype(bf16)
            dq.append(dot_ab(score_grad, key_rows))
            dk_t.append(dot_ab(queries_t[span], score_grad))
            dv_t.append(dot_ab(grads_t[span], probs.astype(bf16)))
        place = pair * 128
        d_ref[:, place : place + 128] = (jnp.where(lane < HEAD_DIM, dq[0], dq[1]) * SCORE_SCALE).astype(bf16)
        place += GROUP
        d_ref[:, place : place + 128] = (jnp.concatenate(dk_t, 0) * SCORE_SCALE).astype(bf16).T
        place += GROUP
        d_ref[:, place : place + 128] = jnp.concatenate(dv_t, 0).astype(bf16).T
    at = at_ref[...]
    for part in range(3):
        span = slice(part * GROUP, part * GROUP + GROUP)
        product = dot_ab(at, d_ref[:, span])

        @pl.when(row == 0)
        def _():
            acc_scr[:, span] = product

        @pl.when(row > 0)
        def _():
            acc_scr[:, span] = acc_scr[:, span] + product

    @pl.when(row == pl.num_programs(1) - 1)
    def _():
        acc_scr[:, 3 * GROUP :] = gwo_ref[...]
        split_blocks(me_ref, acc_scr, keep_ref, send_ref, plan)


def split_blocks(me_ref, acc_scr, keep_ref, send_ref, plan):
    if plan is None:
        keep_ref[0] = acc_scr[...].astype(bf16)
        send_ref[0] = jnp.zeros_like(send_ref[0])
        return
    blocks, core_bit = plan
    size = D // blocks
    me = me_ref[0]
    on_high = (me & core_bit) != 0
    for block in range(blocks):
        if block & core_bit:
            continue
        low = acc_scr[block * size : (block + 1) * size, :]
        other = block | core_bit
        high = acc_scr[other * size : (other + 1) * size, :]
        place = me ^ block
        slot = (place // (2 * core_bit)) * core_bit + place % core_bit
        keep_ref[slot] = jnp.where(on_high, high, low).astype(bf16)
        send_ref[slot] = jnp.where(on_high, low, high).astype(bf16)


def attend_backward(me, at, q, k, v, ctx, dctx, lse, bounds, gwo, plan, start, groups):
    count = q.shape[0]
    rows = count // CAP
    piece = pl.BlockSpec((CAP, GROUP), lambda g, r, me: (r, g + start))
    if plan is None:
        half, size, sent = 1, D, 8
    else:
        half, size = plan[0] // 2, D // plan[0]
        sent = size
    width = 4 * GROUP
    return pl.pallas_call(
        partial(attend_back_kernel, plan=plan, start=start),
        grid_spec=pltpu.PrefetchScalarGridSpec(
            num_scalar_prefetch=1,
            grid=(groups, rows),
            in_specs=[
                pl.BlockSpec((D, CAP), lambda g, r, me: (0, r)),
                piece, piece, piece, piece, piece,
                pl.BlockSpec((CAP, 128), lambda g, r, me: (r, 0)),
                pl.BlockSpec((1, 8, 128), lambda g, r, me: (r, 0, 0)),
                pl.BlockSpec((D, GROUP), lambda g, r, me: (0, g + start)),
            ],
            out_specs=[
                pl.BlockSpec((CAP, 3 * GROUP), lambda g, r, me: (r, g)),
                pl.BlockSpec((half, size, width), lambda g, r, me: (0, 0, g)),
                pl.BlockSpec((half, sent, width), lambda g, r, me: (0, 0, g)),
            ],
            scratch_shapes=[pltpu.VMEM((CAP, CAP), f32), pltpu.VMEM((D, width), f32)],
        ),
        out_shape=[
            jax.ShapeDtypeStruct((count, groups * 3 * GROUP), bf16),
            jax.ShapeDtypeStruct((half, size, groups * width), bf16),
            jax.ShapeDtypeStruct((half, sent, groups * width), bf16),
        ],
        compiler_params=params(40),
        cost_estimate=cost(
            groups * GROUP * (6 * count * D + 40 * count * CAP),
            groups * GROUP * 20 * count,
            groups * (GROUP // HEAD_DIM) * count * CAP,
        ),
        name="attend_backward",
    )(me, at, q, k, v, ctx, dctx, lse, bounds, gwo)


def middle_kernel(ctx_ref, wo_ref, x_ref, vec_ref, att_ref, c_ref):
    att = dot_ab(ctx_ref[...], wo_ref[...]) + vec_ref[5:6, :]
    att_ref[...] = att
    normalized, _ = norm_parts(x_ref[...].astype(f32) + att)
    c_ref[...] = (normalized * vec_ref[2:3, :] + vec_ref[3:4, :]).astype(bf16)


def middle(ctx, w_vo, x, vectors):
    count = ctx.shape[0]
    tile = 320
    wide = pl.BlockSpec((tile, D), lambda t: (t, 0))
    return pl.pallas_call(
        middle_kernel,
        grid=(count // tile,),
        in_specs=[
            wide, pl.BlockSpec((D, D), lambda t: (0, 1)), wide,
            pl.BlockSpec((7, D), lambda t: (0, 0)),
        ],
        out_specs=[wide, wide],
        out_shape=[
            jax.ShapeDtypeStruct((count, D), f32),
            jax.ShapeDtypeStruct((count, D), bf16),
        ],
        compiler_params=params(32),
        cost_estimate=cost(2 * count * D * D, 10 * count * D),
        name="middle",
    )(ctx, w_vo, x, vectors)


ERF_P = 0.3275911 / math.sqrt(2.0)
ERF_COEF = (0.254829592, -0.284496736, 1.421413741, -1.453152027, 1.061405429)


def gelu_parts(u):
    bell = jnp.exp2(u * u * (-0.5 * LOG2E))
    t = 1.0 / (1.0 + ERF_P * jnp.abs(u))
    poly = ERF_COEF[4]
    for coef in ERF_COEF[3::-1]:
        poly = poly * t + coef
    tail = (0.5 * poly * t) * bell
    phi = jnp.where(u >= 0, 1.0 - tail, tail)
    return u * phi, phi + u * (bell * (1.0 / math.sqrt(2.0 * math.pi)))


def mlp_kernel(
    me_ref, c_ref, dm_ref, wu_ref, wd_ref, bias_ref,
    mlp_ref, dc_ref, keep_ref, send_ref, gbias_ref, ct_scr, dmt_scr, *, blocks, split,
):
    first = (pl.program_id(0) == 0) & (pl.program_id(1) == 0)

    @pl.when(first)
    def _():
        ct_scr[...] = c_ref[...].T
        dmt_scr[...] = dm_ref[...].T
        mlp_ref[...] = jnp.zeros_like(mlp_ref)
        dc_ref[...] = jnp.zeros_like(dc_ref)

    width = wu_ref.shape[-1]
    wu = wu_ref[...].reshape(D, width)
    wd = wd_ref[...].reshape(D, width)
    u = dot_ab(c_ref[...], wu) + bias_ref[0]
    act, slope = gelu_parts(u)
    act = act.astype(bf16)
    du = slope * dot_ab(dm_ref[...], wd)
    du = du.astype(bf16)
    gbias_ref[0] = jnp.broadcast_to(jnp.sum(du.astype(f32), 0, keepdims=True), (8, width))
    mlp_ref[...] += dot_ab(act, wd, 1, 1)
    dc_ref[...] += dot_ab(du, wu, 1, 1)
    size = D // blocks
    for which, grad in enumerate((dot_ab(ct_scr[...], du), dot_ab(dmt_scr[...], act))):
        if not split:
            keep_ref[which, 0, 0] = grad.astype(bf16)
            continue
        on_high = (me_ref[2] & 1) != 0
        for block in range(0, blocks, 2):
            low = grad[block * size : (block + 1) * size]
            high = grad[(block + 1) * size : (block + 2) * size]
            slot = (me_ref[2] ^ block) >> 1
            keep_ref[which, slot, 0] = jnp.where(on_high, high, low).astype(bf16)
            send_ref[which, slot, 0] = jnp.where(on_high, low, high).astype(bf16)
    if not split:
        send_ref[...] = jnp.zeros_like(send_ref)


def mlp_all(me, c, dm, weights, bias, split):
    count = c.shape[0]
    blocks, mp, _, size, units = weights.shape
    width = 384
    subs = units // width
    half = blocks // 2 if split else 1
    sent = size if split else 8
    rows_out = size if split else D
    all_rows = pl.BlockSpec((count, D), lambda j, s, me: (0, 0))

    def weight_spec(which):
        return pl.BlockSpec(
            (blocks, 1, 1, size, width), lambda j, s, me, which=which: (0, me[1] ^ j, which, 0, s)
        )

    return pl.pallas_call(
        partial(mlp_kernel, blocks=blocks, split=split),
        grid_spec=pltpu.PrefetchScalarGridSpec(
            num_scalar_prefetch=1,
            grid=(mp, subs),
            in_specs=[
                all_rows, all_rows, weight_spec(0), weight_spec(1),
                pl.BlockSpec((1, 1, width), lambda j, s, me: ((me[1] ^ j) * subs + s, 0, 0)),
            ],
            out_specs=[
                all_rows, all_rows,
                pl.BlockSpec((2, half, 1, rows_out, width), lambda j, s, me: (0, 0, j, 0, s)),
                pl.BlockSpec((2, half, 1, sent, width), lambda j, s, me: (0, 0, j, 0, s)),
                pl.BlockSpec((1, 8, width), lambda j, s, me: ((me[1] ^ j) * subs + s, 0, 0)),
            ],
            scratch_shapes=[pltpu.VMEM((D, count), bf16), pltpu.VMEM((D, count), bf16)],
        ),
        out_shape=[
            jax.ShapeDtypeStruct((count, D), f32),
            jax.ShapeDtypeStruct((count, D), f32),
            jax.ShapeDtypeStruct((2, half, mp, rows_out, units), bf16),
            jax.ShapeDtypeStruct((2, half, mp, sent, units), bf16),
            jax.ShapeDtypeStruct((mp * subs, 8, width), f32),
        ],
        compiler_params=params(58),
        cost_estimate=cost(
            12 * count * D * mp * units, 12 * count * D + 8 * mp * units * D, 2 * count * mp * units
        ),
        name="mlp_all",
    )(me, c, dm, weights, weights, bias.reshape(mp * subs, 1, width))


def turn_kernel(
    x_ref, dy_ref, att_ref, mlp_ref, dc_ref, ctx_ref, wo_ref, vec_ref,
    y_ref, part_ref, dctx_ref, gwo_ref, gvec_ref, datt_scr,
):
    step = pl.program_id(0)

    @pl.when(step == 0)
    def _():
        gvec_ref[...] = jnp.zeros_like(gvec_ref)
        gwo_ref[...] = jnp.zeros_like(gwo_ref)

    tile = 64
    router = vec_ref[4:5, :]

    def body(i, carry):
        rows = pl.ds(pl.multiple_of(i * tile, tile), tile)
        x = x_ref[rows, :].astype(f32)
        dy = dy_ref[rows, :].astype(f32)
        att = att_ref[rows, :]
        branch = att + mlp_ref[rows, :] + vec_ref[6:7, :]
        gate = jax.nn.sigmoid(jnp.sum(x * router, -1, keepdims=True) * ROUTER_SCALE)
        y_ref[rows, :] = (x + gate * branch).astype(bf16)
        dr = jnp.sum(dy * branch, -1, keepdims=True) * gate * (1.0 - gate) * ROUTER_SCALE
        e = gate * dy
        normalized, inverse = norm_parts(x + att)
        dc = dc_ref[rows, :]
        dh = norm_back(dc, normalized, inverse, vec_ref[2:3, :])
        datt = (e + dh).astype(bf16)
        datt_scr[rows, :] = datt
        part_ref[rows, :] = dy + dr * router + dh
        for place, term in enumerate(
            (dc * normalized, dc, dr * x, datt.astype(f32), e.astype(bf16).astype(f32))
        ):
            gvec_ref[place : place + 1, :] += jnp.sum(term, 0, keepdims=True)
        return carry

    lax.fori_loop(0, x_ref.shape[0] // tile, body, 0)
    datt = datt_scr[...]
    dctx_ref[...] = dot_ab(datt, wo_ref[...], 1, 1).astype(bf16)
    gwo_ref[...] += dot_ab(ctx_ref[...], datt, 0, 0)


def turn(x, dy, att, mlp, dc, ctx, w_vo, vectors):
    count = x.shape[0]
    tile = 320
    wide = pl.BlockSpec((tile, D), lambda t: (t, 0))
    return pl.pallas_call(
        turn_kernel,
        grid=(count // tile,),
        in_specs=[
            wide, wide, wide, wide, wide, wide, pl.BlockSpec((D, D), lambda t: (0, 1)),
            pl.BlockSpec((7, D), lambda t: (0, 0)),
        ],
        out_specs=[
            wide, wide, wide, pl.BlockSpec((D, D), lambda t: (0, 0)),
            pl.BlockSpec((8, D), lambda t: (0, 0)),
        ],
        out_shape=[
            jax.ShapeDtypeStruct((count, D), bf16),
            jax.ShapeDtypeStruct((count, D), f32),
            jax.ShapeDtypeStruct((count, D), bf16),
            jax.ShapeDtypeStruct((D, D), f32),
            jax.ShapeDtypeStruct((8, D), f32),
        ],
        scratch_shapes=[pltpu.VMEM((tile, D), bf16)],
        compiler_params=params(48),
        cost_estimate=cost(4 * count * D * D, 26 * count * D),
        name="turn",
    )(x, dy, att, mlp, dc, ctx, w_vo, vectors)


def entry_kernel(
    *refs, spans,
):
    count = len(spans)
    grads = refs[:count]
    wqk_ref, wv_ref, x_ref, part_ref, vec_ref, out_ref, gvec_ref, da_scr = refs[count:]

    @pl.when(pl.program_id(0) == 0)
    def _():
        gvec_ref[...] = jnp.zeros_like(gvec_ref)

    da = None
    for ref, (start, groups) in zip(grads, spans):
        for at in range(groups):
            group, left = start + at, at * 3 * GROUP
            term = dot_ab(
                ref[:, left : left + 2 * GROUP],
                wqk_ref[:, group * 2 * GROUP : (group + 1) * 2 * GROUP], 1, 1,
            ) + dot_ab(
                ref[:, left + 2 * GROUP : left + 3 * GROUP],
                wv_ref[:, group * GROUP : (group + 1) * GROUP], 1, 1,
            )
            da = term if da is None else da + term
    da_scr[...] = da
    tile = 64

    def body(i, carry):
        rows = pl.ds(pl.multiple_of(i * tile, tile), tile)
        normalized, inverse = norm_parts(x_ref[rows, :].astype(f32))
        da = da_scr[rows, :]
        for place, term in enumerate((da * normalized, da)):
            gvec_ref[place : place + 1, :] += jnp.sum(term, 0, keepdims=True)
        grad = part_ref[rows, :] + norm_back(da, normalized, inverse, vec_ref[0:1, :])
        high = grad.astype(bf16)
        out_ref[rows, 0:D] = high
        out_ref[rows, D:] = (grad - high.astype(f32)).astype(bf16)
        return carry

    lax.fori_loop(0, x_ref.shape[0] // tile, body, 0)


def entry(grads, spans, w_qk, w_vo, x, part, vectors):
    count = x.shape[0]
    tile = 320
    wide = pl.BlockSpec((tile, D), lambda r: (r, 0))
    return pl.pallas_call(
        partial(entry_kernel, spans=spans),
        grid=(count // tile,),
        in_specs=[pl.BlockSpec((tile, g.shape[1]), lambda r: (r, 0)) for g in grads]
        + [
            pl.BlockSpec((D, 2 * D), lambda r: (0, 0)), pl.BlockSpec((D, D), lambda r: (0, 0)),
            wide, wide, pl.BlockSpec((7, D), lambda r: (0, 0)),
        ],
        out_specs=[
            pl.BlockSpec((tile, 2 * D), lambda r: (r, 0)),
            pl.BlockSpec((8, D), lambda r: (0, 0)),
        ],
        out_shape=[
            jax.ShapeDtypeStruct((count, 2 * D), bf16),
            jax.ShapeDtypeStruct((8, D), f32),
        ],
        scratch_shapes=[pltpu.VMEM((tile, D), f32)],
        compiler_params=params(32),
        cost_estimate=cost(2 * count * D * 3 * D, 24 * count * D),
        name="entry",
    )(*grads, w_qk, w_vo, x, part, vectors)


def finish_kernel(grad_ref, rank_ref, cot_ref, out_ref, ext_scr):
    ext_scr[:, 0 : 2 * D] = grad_ref[...]
    ext_scr[:, 2 * D :] = jnp.ones((CAP, 128), bf16)
    placed = dot_ab(one_hot(rank_ref[0, 0:1, :]), ext_scr[...], 0, 0)
    kept = 1.0 - placed[:, 2 * D : 2 * D + 1]
    out_ref[0] = placed[:, 0:D] + placed[:, D : 2 * D] + kept * cot_ref[0].astype(f32)


def finish(grad, rank, cotangent):
    rows = cotangent.shape[0]
    return pl.pallas_call(
        finish_kernel,
        grid=(rows,),
        in_specs=[
            pl.BlockSpec((CAP, 2 * D), lambda r: (r, 0)),
            pl.BlockSpec((1, 8, SEQ), lambda r: (r, 0, 0)),
            pl.BlockSpec((1, SEQ, D), lambda r: (r, 0, 0)),
        ],
        out_specs=pl.BlockSpec((1, SEQ, D), lambda r: (r, 0, 0)),
        out_shape=jax.ShapeDtypeStruct((rows, SEQ, D), f32),
        scratch_shapes=[pltpu.VMEM((CAP, 2 * D + 128), bf16)],
        compiler_params=params(48),
        cost_estimate=cost(4 * rows * CAP * SEQ * D, 18 * rows * CAP * D),
        name="finish",
    )(grad, rank, cotangent)


def place_kernel(y_ref, rank_ref, tok_ref, out_ref, ext_scr):
    ext_scr[:, 0:D] = y_ref[...]
    ext_scr[:, D:] = jnp.ones((CAP, 128), bf16)
    placed = dot_ab(one_hot(rank_ref[0, 0:1, :]), ext_scr[...], 0, 0)
    kept = 1.0 - placed[:, D : D + 1]
    out_ref[0] = (placed[:, 0:D] + kept * tok_ref[0].astype(f32)).astype(bf16)


def place(y, rank, tokens):
    rows = tokens.shape[0]
    return pl.pallas_call(
        place_kernel,
        grid=(rows,),
        in_specs=[
            pl.BlockSpec((CAP, D), lambda r: (r, 0)),
            pl.BlockSpec((1, 8, SEQ), lambda r: (r, 0, 0)),
            pl.BlockSpec((1, SEQ, D), lambda r: (r, 0, 0)),
        ],
        out_specs=pl.BlockSpec((1, SEQ, D), lambda r: (r, 0, 0)),
        out_shape=jax.ShapeDtypeStruct((rows, SEQ, D), bf16),
        scratch_shapes=[pltpu.VMEM((CAP, D + 128), bf16)],
        compiler_params=params(48),
        cost_estimate=cost(2 * rows * CAP * SEQ * D, 10 * rows * CAP * D),
        name="place",
    )(y, rank, tokens)


def lamb_moments(weight, gradient, first_mom, second_mom, decay):
    first_new = beta_one * first_mom + (1.0 - beta_one) * gradient
    second_new = beta_two * second_mom + (1.0 - beta_two) * gradient * gradient
    update = (
        first_new
        / (1.0 - beta_one**STEP)
        / (jnp.sqrt(second_new / (1.0 - beta_two**STEP)) + eps_adam)
        + decay * weight
    )
    return (first_new, second_new, update)


def swap(value, axis, size, bit):
    return lax.ppermute(value, axis, [(i, i ^ bit) for i in range(size)])


def on_device(
    tokens, image_ids, selected, cotangent,
    qkv_weight, qkv_first, qkv_second, proj_weight, proj_first, proj_second,
    up_weight, up_first, up_second, down_weight, down_first, down_second,
    up_bias, bias_first, bias_second, vectors, vector_first, vector_second,
    *, dp, mp,
):
    world = dp * mp
    dq_at, dc_at, mp_at = (lax.axis_index(name) for name in ("dq", "dc", "mp"))
    dp_at = dq_at * 2 + dc_at
    me = jnp.stack([dp_at * mp + mp_at, mp_at, dp_at]).astype(jnp.int32)
    everyone = ("dq", "dc", "mp")
    fast = (D // world) % 8 == 0 and dp >= 4 and (D // dp) % 16 == 0

    def swap_dp(value, bit):
        if bit == 1:
            return swap(value, "dc", 2, 1)
        return swap(value, "dq", dp // 2, bit // 2)

    def swap_mp(value, bit):
        return swap(value, "mp", mp, bit)

    bits = []
    bit = 2
    while bit < dp:
        bits.append(bit)
        bit *= 2
    ups, downs = tuple(bits), tuple(reversed(bits))

    def tie(*values):
        return lax.optimization_barrier(values)

    def total(terms):
        result = terms[0].astype(f32)
        for term in terms[1:]:
            result = result + term.astype(f32)
        return result

    def merge(held, came, high, axis):
        return jnp.where(high, jnp.stack([came, held], axis), jnp.stack([held, came], axis))

    narrow = qkv_weight.astype(bf16)
    size = D // world
    low_qk = narrow[:, : 2 * D].reshape(size, 2, GROUPS, GROUP).transpose(0, 2, 1, 3)
    low_qk = low_qk.reshape(size, 2 * D)
    low_vo = jnp.concatenate([narrow[:, 2 * D :], proj_weight.astype(bf16)], 1)
    mlp_low = jnp.stack([up_weight.astype(bf16), down_weight.astype(bf16).T])
    picked = pick_rows(selected, image_ids, tokens, cotangent, vectors)
    if fast:
        low_both = jnp.concatenate([low_qk, low_vo], 1)
        held = [low_both] + [swap_mp(low_both, k) for k in range(1, mp)]
        held, picked = tie(held, picked)
        held = jnp.stack(held).reshape((2,) * (mp.bit_length() - 1) + (size, 4 * D))
        for axis in range(mp.bit_length() - 1):
            flip = ((mp_at >> (mp.bit_length() - 2 - axis)) & 1) != 0
            held = jnp.where(flip, jnp.flip(held, axis), held)
        held = held.reshape(mp, size, 4 * D)
        halves = []
        for half, order in enumerate((ups, downs)):
            value = held[:, :, half * 2 * D : (half + 1) * 2 * D]
            done = []
            for bit in order + (1,):
                axis = sum(other > bit for other in done)
                done.append(bit)
                value = merge(value, swap_dp(value, bit), (dp_at & bit) != 0, axis)
            halves.append(value.reshape(D, 2 * D))
        w_qk, w_vo = halves
    else:
        w_qk = lax.all_gather(low_qk, everyone, axis=0, tiled=True)
        w_vo = lax.all_gather(low_vo, everyone, axis=0, tiled=True)
    mlp_mat = lax.all_gather(mlp_low[None], everyone, axis=0, tiled=True)
    mlp_mat = mlp_mat.reshape(dp, mp, 2, D // dp, FF // mp)
    if not fast:
        mlp_mat = mlp_mat.transpose(1, 2, 0, 3, 4).reshape(1, mp, 2, D, FF // mp)

    def stage(terms, left, bit):
        axis = left.index(bit)
        give = total([lax.index_in_dim(t, 1, axis, False) for t in terms]).astype(bf16)
        terms = [lax.index_in_dim(t, 0, axis, False) for t in terms]
        return terms + [swap_dp(give, bit)], [b for b in left if b != bit]

    def as_bits(value):
        return value.reshape((2,) * len(bits) + (mp,) + value.shape[-2:])

    x, dy, a, at, dm, rank, bounds = picked
    q, k, v, ctx, lse = attend_forward(a, w_qk, w_vo, bounds)
    att, c = middle(ctx, w_vo, x, vectors)
    mlp, dc, mlp_keep, mlp_send, bias_rows = mlp_all(me, c, dm, mlp_mat, up_bias, fast)
    plan = (world, mp) if fast else None
    spans = ((0, GROUPS - 1), (GROUPS - 1, 1))
    back = partial(attend_backward, me, at, q, k, v, ctx)
    if fast:
        mlp_came = swap_dp(mlp_send, 1)
    y, part, dctx, gwo, gvec_two = turn(x, dy, att, mlp, dc, ctx, w_vo, vectors)
    if fast:
        mlp_came, dctx = tie(mlp_came, dctx)
        chains = []
        for which, order in enumerate((ups, downs)):
            terms = [as_bits(mlp_keep[which]), as_bits(mlp_came[which])]
            chains.append([terms, list(reversed(bits)), list(order)])

        def step(chains):
            for chain in chains:
                chain[0], chain[1] = stage(chain[0], chain[1], chain[2].pop(0))

        step(chains)
        d_one, keep_one, send_one = back(dctx, lse, bounds, gwo, plan, *spans[0])
        (chains[0][0][-1], chains[1][0][-1]), d_one, send_one, dctx = tie(
            (chains[0][0][-1], chains[1][0][-1]), d_one, send_one, dctx
        )
        while chains[0][2]:
            step(chains)
        came_one = swap_dp(send_one, 1)
        d_two, keep_two, send_two = back(dctx, lse, bounds, gwo, plan, *spans[1])
        (chains[0][0][-1], chains[1][0][-1]), came_one, send_two, d_two, y = tie(
            (chains[0][0][-1], chains[1][0][-1]), came_one, send_two, d_two, y
        )
        mlp_sent = []
        for k_at in range(1, mp):
            give = jnp.stack([total([t[k_at] for t in chain[0]]) for chain in chains])
            mlp_sent.append(swap_mp(give.astype(bf16), k_at))
        mlp_mine = jnp.stack([total([t[0] for t in chain[0]]) for chain in chains])
        one = [[as_bits(keep_one), as_bits(came_one)], list(reversed(bits)), list(ups)]
        came_two = swap_dp(send_two, 1)
        step([one])
        block_output = place(y, rank, tokens)
        came_two, block_output, d_one = tie(came_two, block_output, d_one)
        two = [[as_bits(keep_two), as_bits(came_two)], list(reversed(bits)), list(downs)]
        step([two])
        grad, gvec_one = entry((d_one, d_two), spans, w_qk, w_vo, x, part, vectors)
        one[0][-1], two[0][-1], grad, gvec_one = tie(one[0][-1], two[0][-1], grad, gvec_one)
        while one[2]:
            step([one, two])
        input_grad = finish(grad, rank, cotangent)
        one[0][-1], two[0][-1], input_grad, mlp_sent = tie(
            one[0][-1], two[0][-1], input_grad, mlp_sent
        )
        attn_sent = []
        for k_at in range(1, mp):
            give = [total([t[k_at] for t in chain[0]]).astype(bf16) for chain in (one, two)]
            attn_sent.append(swap_mp(jnp.concatenate(give, 1), k_at))
        mlp_sum = mlp_mine + total(mlp_sent)
        attn_sum = jnp.concatenate(
            [total([t[0] for t in chain[0]]) for chain in (one, two)], 1
        ) + total(attn_sent)
    else:
        d_all, attn_keep, _ = back(dctx, lse, bounds, gwo, plan, 0, GROUPS)
        block_output = place(y, rank, tokens)
        grad, gvec_one = entry((d_all,), ((0, GROUPS),), w_qk, w_vo, x, part, vectors)
        input_grad = finish(grad, rank, cotangent)
        shaped = mlp_keep[:, 0].reshape(2, mp, dp, D // dp, FF // mp)
        shaped = jnp.take(shaped, mp_at ^ jnp.arange(mp), axis=1)
        shaped = shaped.transpose(2, 1, 0, 3, 4).reshape(world, 2, D // dp, FF // mp)
        mlp_sum = lax.psum_scatter(shaped, everyone, scatter_dimension=0, tiled=True)[0]
        mlp_sum = mlp_sum.astype(f32)
        attn_sum = lax.psum_scatter(attn_keep[0], everyone, scatter_dimension=0, tiled=True)
        attn_sum = attn_sum.astype(f32)
    attn_sum = attn_sum.reshape(size, GROUPS, 4, GROUP).transpose(0, 2, 1, 3)
    attn_sum = attn_sum.reshape(size, 4 * D)
    qkv_sum, proj_sum = attn_sum[:, : 3 * D], attn_sum[:, 3 * D :]
    up_sum, down_sum = mlp_sum[0], mlp_sum[1].T

    qkv_first_new, qkv_second_new, qkv_upd = lamb_moments(
        qkv_weight, qkv_sum, qkv_first, qkv_second, decay_mat
    )
    proj_first_new, proj_second_new, proj_upd = lamb_moments(
        proj_weight, proj_sum, proj_first, proj_second, decay_mat
    )
    up_first_new, up_second_new, up_upd = lamb_moments(
        up_weight, up_sum, up_first, up_second, decay_mat
    )
    down_first_new, down_second_new, down_upd = lamb_moments(
        down_weight, down_sum, down_first, down_second, decay_mat
    )
    squares = jnp.stack(
        [
            jnp.sum(value * value)
            for value in (
                qkv_weight, proj_weight, up_weight, down_weight,
                qkv_upd, proj_upd, up_upd, down_upd,
            )
        ]
    )
    small = jnp.concatenate(
        [
            gvec_one[0:2].reshape(-1),
            gvec_two[0:5].reshape(-1),
            bias_rows[:, 0, :].reshape(-1),
            jnp.pad(squares, (0, 120)),
        ]
    ).reshape(-1, 128)
    if fast:
        bit = 1
        while bit < dp:
            small = small + swap_dp(small, bit)
            bit *= 2
        bit = 1
        while bit < mp:
            small = small + swap_mp(small, bit)
            bit *= 2
    else:
        small = lax.psum(small, everyone)
    small = small.reshape(-1)
    vector_sum = small[: 7 * D].reshape(7, D)
    bias_sum = small[7 * D : 7 * D + FF]
    weight_norms = jnp.sqrt(small[7 * D + FF : 7 * D + FF + 8]).reshape(2, 4)
    ratios = weight_norms[0] / weight_norms[1]
    qkv_new = qkv_weight - rate_lamb * ratios[0] * qkv_upd
    proj_new = proj_weight - rate_lamb * ratios[1] * proj_upd
    up_new = up_weight - rate_lamb * ratios[2] * up_upd
    down_new = down_weight - rate_lamb * ratios[3] * down_upd
    bias_first_new, bias_second_new, bias_upd = lamb_moments(
        up_bias, bias_sum, bias_first, bias_second, 0.0
    )
    bias_ratio = jnp.sqrt(jnp.sum(up_bias * up_bias)) / jnp.sqrt(jnp.sum(bias_upd * bias_upd))
    bias_new = up_bias - rate_lamb * bias_ratio * bias_upd
    vector_first_new, vector_second_new, vector_upd = lamb_moments(
        vectors, vector_sum, vector_first, vector_second, 0.0
    )
    vector_ratio = jnp.sqrt(jnp.sum(vectors * vectors, -1, keepdims=True)) / jnp.sqrt(
        jnp.sum(vector_upd * vector_upd, -1, keepdims=True)
    )
    vectors_new = vectors - rate_lamb * vector_ratio * vector_upd
    return (
        block_output, input_grad, weight_norms,
        qkv_new, qkv_first_new, qkv_second_new,
        proj_new, proj_first_new, proj_second_new,
        up_new, up_first_new, up_second_new,
        down_new, down_first_new, down_second_new,
        bias_new, bias_first_new, bias_second_new,
        vectors_new, vector_first_new, vector_second_new,
    )


def solution(mesh):
    dp, mp = mesh.shape["dp"], mesh.shape["mp"]
    split = Mesh(mesh.devices.reshape(dp // 2, 2, mp), ("dq", "dc", "mp"))
    rows = ("dq", "dc", "mp")
    by_rows = (P(rows, None),) * 3
    shared = (P(),) * 3
    up_spec = (P(("dq", "dc"), "mp"),) * 3
    down_spec = (P("mp", ("dq", "dc")),) * 3
    in_specs = (
        (P(rows, None, None), P(rows, None), P(rows, None), P(rows, None, None))
        + by_rows + by_rows + up_spec + down_spec + shared + shared
    )
    out_specs = (
        (P(rows, None, None), P(rows, None, None), P())
        + by_rows + by_rows + up_spec + down_spec + shared + shared
    )
    return jax.shard_map(
        partial(on_device, dp=dp, mp=mp),
        mesh=split, in_specs=in_specs, out_specs=out_specs, check_vma=False,
    )
```

```python
from functools import partial
import math

import jax
import jax.numpy as jnp
from jax import lax
from jax.experimental import pallas as pl
from jax.experimental.pallas import tpu as pltpu
from jax.sharding import Mesh, PartitionSpec as P

D = 768
FF = 3072
HEADS = 12
HEAD_DIM = 64
CAP = 640
SEQ = 1280
STEP = 10

eps_norm = 1e-06
eps_adam = 1e-06
beta_one = 0.9
beta_two = 0.999
decay_mat = 0.01
rate_lamb = 0.3
masked_score = -1e30

f32 = jnp.float32
bf16 = jnp.bfloat16
GROUP = 256
GROUPS = D // GROUP
LOG2E = 1.0 / math.log(2.0)
SCORE_SCALE = 1.0 / math.sqrt(HEAD_DIM)
ROUTER_SCALE = 1.0 / math.sqrt(D)


def dot_ab(left, right, left_dim=1, right_dim=0):
    return lax.dot_general(
        left, right, (((left_dim,), (right_dim,)), ((), ())), preferred_element_type=f32
    )


def params(mib, **more):
    return pltpu.CompilerParams(vmem_limit_bytes=mib << 20, **more)


def hbm(shape, dtype):
    return pltpu.HBM(shape, dtype)


def pinned(*arrays):
    return [
        pltpu.with_memory_space_constraint(array, pltpu.HBM) if array.size >= 1 << 17 else array
        for array in arrays
    ]


def cost(flops, nbytes, trans=0):
    return pl.CostEstimate(flops=int(flops), bytes_accessed=int(nbytes), transcendentals=int(trans))


def norm_parts(values):
    center = jnp.mean(values, -1, keepdims=True)
    offset = values - center
    spread = jnp.mean(offset * offset, -1, keepdims=True)
    inverse = lax.rsqrt(spread + eps_norm)
    return offset * inverse, inverse


def norm_back(grad, normalized, inverse, gain):
    scaled = grad * gain
    return inverse * (
        scaled
        - jnp.mean(scaled, -1, keepdims=True)
        - normalized * jnp.mean(scaled * normalized, -1, keepdims=True)
    )


def ranks_of(sel, ids):
    kind = jnp.where(ids < 0, 2, ids)
    sub = lax.broadcasted_iota(jnp.int32, (8, SEQ), 0)
    lane = lax.broadcasted_iota(jnp.int32, (8, SEQ), 1)
    member = jnp.where(jnp.broadcast_to(kind, (8, SEQ)) == sub, jnp.broadcast_to(sel, (8, SEQ)), 0)
    total = member
    step = 1
    while step < SEQ:
        total = total + jnp.where(lane >= step, pltpu.roll(total, step, 1), 0)
        step *= 2
    count = jnp.max(total, axis=1, keepdims=True)
    first = count[0:1]
    second = first + count[1:2]
    base = jnp.where(sub == 0, 0, jnp.where(sub == 1, first, second))
    rank = jnp.sum(member * (total + base), axis=0, keepdims=True) - 1
    return rank, first, second


def one_hot(rank):
    place = lax.broadcasted_iota(jnp.int32, (CAP, SEQ), 0)
    return jnp.where(place == rank, 1.0, 0.0).astype(bf16)


def pick_kernel(
    sel_ref, ids_ref, tok_ref, cot_ref, vec_ref,
    x_ref, dy_ref, a_ref, at_ref, dm_ref, rank_ref, bounds_ref, x_scr, dy_scr,
):
    rank, first, second = ranks_of(sel_ref[0], ids_ref[0])
    rank_ref[0] = jnp.broadcast_to(rank, (8, SEQ))
    lane = lax.broadcasted_iota(jnp.int32, (8, 128), 1)
    bounds_ref[0] = jnp.where(lane == 0, first, second)
    hot = one_hot(rank)
    x_scr[...] = dot_ab(hot, tok_ref[0])
    dy_scr[...] = dot_ab(hot, cot_ref[0])
    tile = 128

    def body(i, carry):
        rows = pl.ds(pl.multiple_of(i * tile, tile), tile)
        x = x_scr[rows, :]
        dy = dy_scr[rows, :]
        normalized, _ = norm_parts(x)
        low = (normalized * vec_ref[0:1, :] + vec_ref[1:2, :]).astype(bf16)
        gate = jax.nn.sigmoid(jnp.sum(x * vec_ref[4:5, :], -1, keepdims=True) * ROUTER_SCALE)
        x_ref[rows, :] = x.astype(bf16)
        dy_ref[rows, :] = dy.astype(bf16)
        a_ref[rows, :] = low
        dm_ref[rows, :] = (gate * dy).astype(bf16)
        return carry

    lax.fori_loop(0, CAP // tile, body, 0)
    at_ref[...] = a_ref[...].T


def pick_rows(sel, ids, tokens, cotangent, vectors):
    rows = tokens.shape[0]
    count = rows * CAP
    wide = pl.BlockSpec((CAP, D), lambda r: (r, 0))
    line = pl.BlockSpec((1, 1, SEQ), lambda r: (r, 0, 0))
    full = pl.BlockSpec((1, SEQ, D), lambda r: (r, 0, 0))
    return pl.pallas_call(
        pick_kernel,
        grid=(rows,),
        in_specs=[line, line, full, full, pl.BlockSpec((7, D), lambda r: (0, 0))],
        out_specs=[
            wide, wide, wide, pl.BlockSpec((D, CAP), lambda r: (0, r)), wide,
            pl.BlockSpec((1, 8, SEQ), lambda r: (r, 0, 0)),
            pl.BlockSpec((1, 8, 128), lambda r: (r, 0, 0)),
        ],
        out_shape=[
            hbm((count, D), bf16),
            hbm((count, D), bf16),
            hbm((count, D), bf16),
            hbm((D, count), bf16),
            hbm((count, D), bf16),
            hbm((rows, 8, SEQ), jnp.int32),
            hbm((rows, 8, 128), jnp.int32),
        ],
        scratch_shapes=[pltpu.VMEM((CAP, D), f32), pltpu.VMEM((CAP, D), f32)],
        compiler_params=params(40),
        cost_estimate=cost(4 * count * SEQ * D, 4 * rows * SEQ * D * 2),
        name="pick_rows",
    )(*pinned(sel[:, None, :], ids[:, None, :], tokens, cotangent, vectors))


def fill_bias(bias_scr, bounds_ref):
    first = bounds_ref[0, 0:1, 0:1]
    second = bounds_ref[0, 0:1, 1:2]
    tile = 128
    key = lax.broadcasted_iota(jnp.int32, (tile, CAP), 1)
    key_kind = jnp.where(key >= first, 1, 0) + jnp.where(key >= second, 1, 0)
    for i in range(CAP // tile):
        row = lax.broadcasted_iota(jnp.int32, (tile, CAP), 0) + i * tile
        row_kind = jnp.where(row >= first, 1, 0) + jnp.where(row >= second, 1, 0)
        bias_scr[i * tile : (i + 1) * tile, :] = jnp.where(row_kind == key_kind, 0.0, masked_score)


def half_masks():
    lane = lax.broadcasted_iota(jnp.int32, (1, 128), 1)
    low = jnp.where(lane < HEAD_DIM, 1.0, 0.0)
    return low, 1.0 - low


def attend_kernel(
    a_ref, w_ref, bounds_ref,
    q_ref, k_ref, v_ref, ctx_ref, lse_ref, bias_scr,
):
    group = pl.program_id(1)

    @pl.when(group == 0)
    def _():
        fill_bias(bias_scr, bounds_ref)
        lse_ref[...] = jnp.zeros_like(lse_ref)

    a = a_ref[...]
    for part, ref in enumerate((q_ref, k_ref, v_ref)):
        ref[...] = dot_ab(a, w_ref[:, part * GROUP : (part + 1) * GROUP]).astype(bf16)
    masks = half_masks()
    lane = lax.broadcasted_iota(jnp.int32, (1, 128), 1)
    for pair in range(GROUP // 128):
        cols = slice(pair * 128, pair * 128 + 128)
        queries, key_rows, values = q_ref[:, cols], k_ref[:, cols], v_ref[:, cols]
        halves = []
        for half in range(2):
            scores = dot_ab(queries * masks[half].astype(bf16), key_rows, 1, 1)
            scores = scores * (SCORE_SCALE * LOG2E) + bias_scr[...]
            row_max = jnp.max(scores, -1, keepdims=True)
            probs = jnp.exp2(scores - row_max)
            row_total = jnp.sum(probs, -1, keepdims=True)
            out = dot_ab(probs.astype(bf16), values)
            halves.append(out * (1.0 / row_total))
            head = group * (GROUP // HEAD_DIM) + pair * 2 + half
            lse_ref[...] = jnp.where(lane == head, row_max + jnp.log2(row_total), lse_ref[...])
        ctx_ref[:, cols] = jnp.where(lane < HEAD_DIM, halves[0], halves[1]).astype(bf16)


def attend_forward(a, w_qkv, bounds):
    count = a.shape[0]
    rows = count // CAP
    piece = pl.BlockSpec((CAP, GROUP), lambda r, g: (r, g))
    narrow = hbm((count, D), bf16)
    return pl.pallas_call(
        attend_kernel,
        grid=(rows, GROUPS),
        in_specs=[
            pl.BlockSpec((CAP, D), lambda r, g: (r, 0)),
            pl.BlockSpec((D, 3 * GROUP), lambda r, g: (0, g)),
            pl.BlockSpec((1, 8, 128), lambda r, g: (r, 0, 0)),
        ],
        out_specs=[piece, piece, piece, piece, pl.BlockSpec((CAP, 128), lambda r, g: (r, 0))],
        out_shape=[narrow, narrow, narrow, narrow, hbm((count, 128), f32)],
        scratch_shapes=[pltpu.VMEM((CAP, CAP), f32)],
        compiler_params=params(48),
        cost_estimate=cost(
            2 * count * D * 3 * D + rows * HEADS * 16 * CAP * CAP * HEAD_DIM, 12 * count * D,
            rows * HEADS * CAP * CAP,
        ),
        name="attend_forward",
    )(*pinned(a, w_qkv, bounds))


def attend_back_kernel(
    me_ref, at_ref, q_ref, k_ref, v_ref, ctx_ref, dctx_ref, lse_ref, bounds_ref, gwo_ref,
    d_ref, keep_ref, send_ref, bias_scr, acc_scr, *, plan, start,
):
    group, row = pl.program_id(0) + start, pl.program_id(1)
    fill_bias(bias_scr, bounds_ref)
    masks = half_masks()
    lane = lax.broadcasted_iota(jnp.int32, (1, 128), 1)
    for pair in range(GROUP // 128):
        cols = slice(pair * 128, pair * 128 + 128)
        queries, key_rows, values = q_ref[:, cols], k_ref[:, cols], v_ref[:, cols]
        grads = dctx_ref[:, cols]
        product = ctx_ref[:, cols].astype(f32) * grads.astype(f32)
        queries_t, grads_t = queries.T, grads.T
        dq, dk_t, dv_t = [], [], []
        for half in range(2):
            mask_low = masks[half].astype(bf16)
            span = slice(half * HEAD_DIM, half * HEAD_DIM + HEAD_DIM)
            head = group * (GROUP // HEAD_DIM) + pair * 2 + half
            log_total = jnp.sum(jnp.where(lane == head, lse_ref[...], 0.0), -1, keepdims=True)
            delta = jnp.sum(product * masks[half], -1, keepdims=True)
            scores = dot_ab(queries * mask_low, key_rows, 1, 1)
            scores = scores * (SCORE_SCALE * LOG2E) + bias_scr[...]
            probs = jnp.exp2(scores - log_total)
            probs_grad = dot_ab(grads * mask_low, values, 1, 1)
            score_grad = (probs * (probs_grad - delta)).astype(bf16)
            dq.append(dot_ab(score_grad, key_rows))
            dk_t.append(dot_ab(queries_t[span], score_grad))
            dv_t.append(dot_ab(grads_t[span], probs.astype(bf16)))
        place = pair * 128
        d_ref[:, place : place + 128] = (jnp.where(lane < HEAD_DIM, dq[0], dq[1]) * SCORE_SCALE).astype(bf16)
        place += GROUP
        d_ref[:, place : place + 128] = (jnp.concatenate(dk_t, 0) * SCORE_SCALE).astype(bf16).T
        place += GROUP
        d_ref[:, place : place + 128] = jnp.concatenate(dv_t, 0).astype(bf16).T
    at = at_ref[...]
    for part in range(3):
        span = slice(part * GROUP, part * GROUP + GROUP)
        product = dot_ab(at, d_ref[:, span])

        @pl.when(row == 0)
        def _():
            acc_scr[:, span] = product

        @pl.when(row > 0)
        def _():
            acc_scr[:, span] = acc_scr[:, span] + product

    @pl.when(row == pl.num_programs(1) - 1)
    def _():
        acc_scr[:, 3 * GROUP :] = gwo_ref[...]
        split_blocks(me_ref, acc_scr, keep_ref, send_ref, plan)


def split_blocks(me_ref, acc_scr, keep_ref, send_ref, plan):
    if plan is None:
        keep_ref[0] = acc_scr[...].astype(bf16)
        send_ref[0] = jnp.zeros_like(send_ref[0])
        return
    blocks, core_bit = plan
    size = D // blocks
    on_high = (me_ref[0] & core_bit) != 0
    for block in range(blocks):
        if block & core_bit:
            continue
        low = acc_scr[block * size : (block + 1) * size, :]
        other = block | core_bit
        high = acc_scr[other * size : (other + 1) * size, :]
        slot = (block // (2 * core_bit)) * core_bit + block % core_bit
        keep_ref[slot] = jnp.where(on_high, high, low).astype(bf16)
        send_ref[slot] = jnp.where(on_high, low, high).astype(bf16)


def attend_backward(me, at, q, k, v, ctx, dctx, lse, bounds, gwo, plan, start, groups):
    count = q.shape[0]
    rows = count // CAP
    piece = pl.BlockSpec((CAP, GROUP), lambda g, r, me: (r, g + start))
    if plan is None:
        half, size, sent = 1, D, 8
    else:
        half, size = plan[0] // 2, D // plan[0]
        sent = size
    width = 4 * GROUP
    return pl.pallas_call(
        partial(attend_back_kernel, plan=plan, start=start),
        grid_spec=pltpu.PrefetchScalarGridSpec(
            num_scalar_prefetch=1,
            grid=(groups, rows),
            in_specs=[
                pl.BlockSpec((D, CAP), lambda g, r, me: (0, r)),
                piece, piece, piece, piece, piece,
                pl.BlockSpec((CAP, 128), lambda g, r, me: (r, 0)),
                pl.BlockSpec((1, 8, 128), lambda g, r, me: (r, 0, 0)),
                pl.BlockSpec((D, GROUP), lambda g, r, me: (0, g + start)),
            ],
            out_specs=[
                pl.BlockSpec((CAP, 3 * GROUP), lambda g, r, me: (r, g)),
                pl.BlockSpec((half, size, width), lambda g, r, me: (0, 0, g)),
                pl.BlockSpec((half, sent, width), lambda g, r, me: (0, 0, g)),
            ],
            scratch_shapes=[pltpu.VMEM((CAP, CAP), f32), pltpu.VMEM((D, width), f32)],
        ),
        out_shape=[
            hbm((count, groups * 3 * GROUP), bf16),
            hbm((half, size, groups * width), bf16),
            hbm((half, sent, groups * width), bf16),
        ],
        compiler_params=params(40),
        cost_estimate=cost(
            groups * GROUP * (6 * count * D + 40 * count * CAP),
            groups * GROUP * 20 * count,
            groups * (GROUP // HEAD_DIM) * count * CAP,
        ),
        name="attend_backward",
    )(me, *pinned(at, q, k, v, ctx, dctx, lse, bounds, gwo))


def middle_kernel(ctx_ref, wo_ref, x_ref, vec_ref, att_ref, c_ref):
    att = dot_ab(ctx_ref[...], wo_ref[...]) + vec_ref[5:6, :]
    att_ref[...] = att
    normalized, _ = norm_parts(x_ref[...].astype(f32) + att)
    c_ref[...] = (normalized * vec_ref[2:3, :] + vec_ref[3:4, :]).astype(bf16)


def middle(ctx, w_o, x, vectors):
    count = ctx.shape[0]
    tile = 320
    wide = pl.BlockSpec((tile, D), lambda t: (t, 0))
    return pl.pallas_call(
        middle_kernel,
        grid=(count // tile,),
        in_specs=[
            wide, pl.BlockSpec((D, D), lambda t: (0, 0)), wide,
            pl.BlockSpec((7, D), lambda t: (0, 0)),
        ],
        out_specs=[wide, wide],
        out_shape=[
            hbm((count, D), f32),
            hbm((count, D), bf16),
        ],
        compiler_params=params(32),
        cost_estimate=cost(2 * count * D * D, 10 * count * D),
        name="middle",
    )(*pinned(ctx, w_o, x, vectors))


ERF_P = 0.3275911 / math.sqrt(2.0)
ERF_COEF = (0.254829592, -0.284496736, 1.421413741, -1.453152027, 1.061405429)


def gelu_parts(u):
    bell = jnp.exp2(u * u * (-0.5 * LOG2E))
    t = 1.0 / (1.0 + ERF_P * jnp.abs(u))
    poly = ERF_COEF[4]
    for coef in ERF_COEF[3::-1]:
        poly = poly * t + coef
    tail = (0.5 * poly * t) * bell
    phi = jnp.where(u >= 0, 1.0 - tail, tail)
    return u * phi, phi + u * (bell * (1.0 / math.sqrt(2.0 * math.pi)))


def mlp_kernel(
    me_ref, c_ref, dm_ref, wu_ref, wd_ref, bias_ref,
    mlp_ref, dc_ref, keep_ref, send_ref, gbias_ref, ct_scr, dmt_scr, *, blocks, split,
):
    first = (pl.program_id(0) == 0) & (pl.program_id(1) == 0)

    @pl.when(first)
    def _():
        ct_scr[...] = c_ref[...].T
        dmt_scr[...] = dm_ref[...].T
        mlp_ref[...] = jnp.zeros_like(mlp_ref)
        dc_ref[...] = jnp.zeros_like(dc_ref)

    width = wu_ref.shape[-1]
    wu = wu_ref[...].reshape(D, width)
    wd = wd_ref[...].reshape(D, width)
    u = dot_ab(c_ref[...], wu) + bias_ref[0]
    act, slope = gelu_parts(u)
    act = act.astype(bf16)
    du = slope * dot_ab(dm_ref[...], wd)
    du = du.astype(bf16)
    gbias_ref[0] = jnp.broadcast_to(jnp.sum(du.astype(f32), 0, keepdims=True), (8, width))
    mlp_ref[...] += dot_ab(act, wd, 1, 1)
    dc_ref[...] += dot_ab(du, wu, 1, 1)
    size = D // blocks
    for which, grad in enumerate((dot_ab(ct_scr[...], du), dot_ab(dmt_scr[...], act))):
        if not split:
            keep_ref[which, 0, 0] = grad.astype(bf16)
            continue
        on_high = (me_ref[2] & 1) != 0
        for block in range(0, blocks, 2):
            low = grad[block * size : (block + 1) * size]
            high = grad[(block + 1) * size : (block + 2) * size]
            slot = block // 2
            keep_ref[which, slot, 0] = jnp.where(on_high, high, low).astype(bf16)
            send_ref[which, slot, 0] = jnp.where(on_high, low, high).astype(bf16)
    if not split:
        send_ref[...] = jnp.zeros_like(send_ref)


def mlp_all(me, c, dm, weights, bias, split):
    count = c.shape[0]
    blocks, mp, _, units = weights.shape
    size = D // blocks
    width = 384
    subs = units // width
    half = blocks // 2 if split else 1
    sent = size if split else 8
    rows_out = size if split else D
    all_rows = pl.BlockSpec((count, D), lambda j, s, me: (0, 0))

    def weight_spec(which):
        return pl.BlockSpec(
            (blocks, 1, size, width), lambda j, s, me, which=which: (0, me[1] ^ j, which, s)
        )

    return pl.pallas_call(
        partial(mlp_kernel, blocks=blocks, split=split),
        grid_spec=pltpu.PrefetchScalarGridSpec(
            num_scalar_prefetch=1,
            grid=(mp, subs),
            in_specs=[
                all_rows, all_rows, weight_spec(0), weight_spec(1),
                pl.BlockSpec((1, 1, width), lambda j, s, me: ((me[1] ^ j) * subs + s, 0, 0)),
            ],
            out_specs=[
                all_rows, all_rows,
                pl.BlockSpec((2, half, 1, rows_out, width), lambda j, s, me: (0, 0, j, 0, s)),
                pl.BlockSpec((2, half, 1, sent, width), lambda j, s, me: (0, 0, j, 0, s)),
                pl.BlockSpec((1, 8, width), lambda j, s, me: (me[1] ^ j, 0, s)),
            ],
            scratch_shapes=[pltpu.VMEM((D, count), bf16), pltpu.VMEM((D, count), bf16)],
        ),
        out_shape=[
            hbm((count, D), f32),
            hbm((count, D), f32),
            hbm((2, half, mp, rows_out, units), bf16),
            hbm((2, half, mp, sent, units), bf16),
            hbm((mp, 8, units), f32),
        ],
        compiler_params=params(58),
        cost_estimate=cost(
            12 * count * D * mp * units, 12 * count * D + 8 * mp * units * D, 2 * count * mp * units
        ),
        name="mlp_all",
    )(me, *pinned(c, dm, weights, weights, bias.reshape(mp * subs, 1, width)))


def turn_kernel(
    x_ref, dy_ref, att_ref, mlp_ref, dc_ref, ctx_ref, wo_ref, vec_ref,
    y_ref, part_ref, dctx_ref, gwo_ref, gvec_ref, datt_scr,
):
    step = pl.program_id(0)

    @pl.when(step == 0)
    def _():
        gvec_ref[...] = jnp.zeros_like(gvec_ref)
        gwo_ref[...] = jnp.zeros_like(gwo_ref)

    tile = 64
    router = vec_ref[4:5, :]

    def body(i, carry):
        rows = pl.ds(pl.multiple_of(i * tile, tile), tile)
        x = x_ref[rows, :].astype(f32)
        dy = dy_ref[rows, :].astype(f32)
        att = att_ref[rows, :]
        branch = att + mlp_ref[rows, :] + vec_ref[6:7, :]
        gate = jax.nn.sigmoid(jnp.sum(x * router, -1, keepdims=True) * ROUTER_SCALE)
        y_ref[rows, :] = (x + gate * branch).astype(bf16)
        dr = jnp.sum(dy * branch, -1, keepdims=True) * gate * (1.0 - gate) * ROUTER_SCALE
        e = gate * dy
        normalized, inverse = norm_parts(x + att)
        dc = dc_ref[rows, :]
        dh = norm_back(dc, normalized, inverse, vec_ref[2:3, :])
        datt = (e + dh).astype(bf16)
        datt_scr[rows, :] = datt
        part_ref[rows, :] = dy + dr * router + dh
        for place, term in enumerate(
            (dc * normalized, dc, dr * x, datt.astype(f32), e.astype(bf16).astype(f32))
        ):
            gvec_ref[place : place + 1, :] += jnp.sum(term, 0, keepdims=True)
        return carry

    lax.fori_loop(0, x_ref.shape[0] // tile, body, 0)
    datt = datt_scr[...]
    dctx_ref[...] = dot_ab(datt, wo_ref[...], 1, 1).astype(bf16)
    gwo_ref[...] += dot_ab(ctx_ref[...], datt, 0, 0)


def turn(x, dy, att, mlp, dc, ctx, w_o, vectors):
    count = x.shape[0]
    tile = 320
    wide = pl.BlockSpec((tile, D), lambda t: (t, 0))
    return pl.pallas_call(
        turn_kernel,
        grid=(count // tile,),
        in_specs=[
            wide, wide, wide, wide, wide, wide, pl.BlockSpec((D, D), lambda t: (0, 0)),
            pl.BlockSpec((7, D), lambda t: (0, 0)),
        ],
        out_specs=[
            wide, wide, wide, pl.BlockSpec((D, D), lambda t: (0, 0)),
            pl.BlockSpec((8, D), lambda t: (0, 0)),
        ],
        out_shape=[
            hbm((count, D), bf16),
            hbm((count, D), f32),
            hbm((count, D), bf16),
            hbm((D, D), f32),
            hbm((8, D), f32),
        ],
        scratch_shapes=[pltpu.VMEM((tile, D), bf16)],
        compiler_params=params(48),
        cost_estimate=cost(4 * count * D * D, 26 * count * D),
        name="turn",
    )(*pinned(x, dy, att, mlp, dc, ctx, w_o, vectors))


def entry_kernel(
    *refs, spans,
):
    count = len(spans)
    grads = refs[:count]
    w_ref, x_ref, part_ref, vec_ref, out_ref, gvec_ref, da_scr = refs[count:]

    @pl.when(pl.program_id(0) == 0)
    def _():
        gvec_ref[...] = jnp.zeros_like(gvec_ref)

    da = None
    for ref, (start, groups) in zip(grads, spans):
        left, right = start * 3 * GROUP, (start + groups) * 3 * GROUP
        term = dot_ab(ref[...], w_ref[:, left:right], 1, 1)
        da = term if da is None else da + term
    da_scr[...] = da
    tile = 64

    def body(i, carry):
        rows = pl.ds(pl.multiple_of(i * tile, tile), tile)
        normalized, inverse = norm_parts(x_ref[rows, :].astype(f32))
        da = da_scr[rows, :]
        for place, term in enumerate((da * normalized, da)):
            gvec_ref[place : place + 1, :] += jnp.sum(term, 0, keepdims=True)
        grad = part_ref[rows, :] + norm_back(da, normalized, inverse, vec_ref[0:1, :])
        high = grad.astype(bf16)
        out_ref[rows, 0:D] = high
        out_ref[rows, D:] = (grad - high.astype(f32)).astype(bf16)
        return carry

    lax.fori_loop(0, x_ref.shape[0] // tile, body, 0)


def entry(grads, spans, w_qkv, x, part, vectors):
    count = x.shape[0]
    tile = 320
    wide = pl.BlockSpec((tile, D), lambda r: (r, 0))
    return pl.pallas_call(
        partial(entry_kernel, spans=spans),
        grid=(count // tile,),
        in_specs=[pl.BlockSpec((tile, g.shape[1]), lambda r: (r, 0)) for g in grads]
        + [
            pl.BlockSpec((D, 3 * D), lambda r: (0, 0)), wide, wide, pl.BlockSpec((7, D), lambda r: (0, 0)),
        ],
        out_specs=[
            pl.BlockSpec((tile, 2 * D), lambda r: (r, 0)),
            pl.BlockSpec((8, D), lambda r: (0, 0)),
        ],
        out_shape=[
            hbm((count, 2 * D), bf16),
            hbm((8, D), f32),
        ],
        scratch_shapes=[pltpu.VMEM((tile, D), f32)],
        compiler_params=params(32),
        cost_estimate=cost(2 * count * D * 3 * D, 24 * count * D),
        name="entry",
    )(*pinned(*grads, w_qkv, x, part, vectors))


def finish_kernel(grad_ref, rank_ref, cot_ref, out_ref, ext_scr):
    ext_scr[:, 0 : 2 * D] = grad_ref[...]
    ext_scr[:, 2 * D :] = jnp.ones((CAP, 128), bf16)
    placed = dot_ab(one_hot(rank_ref[0, 0:1, :]), ext_scr[...], 0, 0)
    kept = 1.0 - placed[:, 2 * D : 2 * D + 1]
    out_ref[0] = placed[:, 0:D] + placed[:, D : 2 * D] + kept * cot_ref[0].astype(f32)


def finish(grad, rank, cotangent):
    rows = cotangent.shape[0]
    return pl.pallas_call(
        finish_kernel,
        grid=(rows,),
        in_specs=[
            pl.BlockSpec((CAP, 2 * D), lambda r: (r, 0)),
            pl.BlockSpec((1, 8, SEQ), lambda r: (r, 0, 0)),
            pl.BlockSpec((1, SEQ, D), lambda r: (r, 0, 0)),
        ],
        out_specs=pl.BlockSpec((1, SEQ, D), lambda r: (r, 0, 0)),
        out_shape=hbm((rows, SEQ, D), f32),
        scratch_shapes=[pltpu.VMEM((CAP, 2 * D + 128), bf16)],
        compiler_params=params(48),
        cost_estimate=cost(4 * rows * CAP * SEQ * D, 18 * rows * CAP * D),
        name="finish",
    )(*pinned(grad, rank, cotangent))


def place_kernel(y_ref, rank_ref, tok_ref, out_ref, ext_scr):
    ext_scr[:, 0:D] = y_ref[...]
    ext_scr[:, D:] = jnp.ones((CAP, 128), bf16)
    placed = dot_ab(one_hot(rank_ref[0, 0:1, :]), ext_scr[...], 0, 0)
    kept = 1.0 - placed[:, D : D + 1]
    out_ref[0] = (placed[:, 0:D] + kept * tok_ref[0].astype(f32)).astype(bf16)


def place(y, rank, tokens):
    rows = tokens.shape[0]
    return pl.pallas_call(
        place_kernel,
        grid=(rows,),
        in_specs=[
            pl.BlockSpec((CAP, D), lambda r: (r, 0)),
            pl.BlockSpec((1, 8, SEQ), lambda r: (r, 0, 0)),
            pl.BlockSpec((1, SEQ, D), lambda r: (r, 0, 0)),
        ],
        out_specs=pl.BlockSpec((1, SEQ, D), lambda r: (r, 0, 0)),
        out_shape=hbm((rows, SEQ, D), bf16),
        scratch_shapes=[pltpu.VMEM((CAP, D + 128), bf16)],
        compiler_params=params(48),
        cost_estimate=cost(2 * rows * CAP * SEQ * D, 10 * rows * CAP * D),
        name="place",
    )(*pinned(y, rank, tokens))


def lamb_moments(weight, gradient, first_mom, second_mom, decay):
    first_new = beta_one * first_mom + (1.0 - beta_one) * gradient
    second_new = beta_two * second_mom + (1.0 - beta_two) * gradient * gradient
    update = (
        first_new
        / (1.0 - beta_one**STEP)
        / (jnp.sqrt(second_new / (1.0 - beta_two**STEP)) + eps_adam)
        + decay * weight
    )
    return (first_new, second_new, update)


def square_sum(value):
    return jnp.sum(jnp.sum(value * value, 1, keepdims=True), 0, keepdims=True)


def added(mine_ref, got_refs, place):
    result = mine_ref[place]
    for ref in got_refs:
        result = result + ref[place].astype(f32)
    return result


def lanes_of(pairs):
    lane = lax.broadcasted_iota(jnp.int32, (8, 128), 1)
    result = jnp.zeros((8, 128), f32)
    for place, value in pairs:
        result = result + jnp.where(lane == place, value, 0.0)
    return result


def mlp_lamb_kernel(*refs, gots):
    weights, (mine_ref, *rest) = refs[:6], refs[6:]
    got_refs, outs = rest[:gots], rest[gots:]
    pairs = []
    for which in range(2):
        weight_ref, first_ref, second_ref = weights[3 * which : 3 * which + 3]
        grad = added(mine_ref, got_refs, which)
        weight = weight_ref[...]
        news = lamb_moments(weight, grad, first_ref[...], second_ref[...], decay_mat)
        for ref, value in zip(outs[3 * which : 3 * which + 3], news):
            ref[...] = value
        pairs += [(2 + which, square_sum(weight)), (6 + which, square_sum(news[2]))]
    outs[6][...] = lanes_of(pairs)


def mlp_lamb(moments, mine, gots):
    like = jax.ShapeDtypeStruct(moments[0].shape, f32)
    return pl.pallas_call(
        partial(mlp_lamb_kernel, gots=len(gots)),
        out_shape=[like] * 6 + [jax.ShapeDtypeStruct((8, 128), f32)],
        compiler_params=params(24),
        cost_estimate=cost(40 * mine.size, 40 * mine.size),
        name="mlp_lamb",
    )(*moments, mine, *gots)


def attn_lamb_kernel(*refs, gots):
    moments, (mine_ref, *rest) = refs[:6], refs[6:]
    got_refs, rest = rest[:gots], rest[gots:]
    one_ref, two_ref, bias_ref, sq_ref, *outs = rest
    sums = [jnp.zeros((1, 1), f32) for _ in range(4)]
    for part in range(4):
        tensor = part // 3
        weight_ref, first_ref, second_ref = moments[3 * tensor : 3 * tensor + 3]
        for group in range(GROUPS):
            left = (group * 4 + part) * GROUP
            grad = added(mine_ref, got_refs, (slice(None), slice(left, left + GROUP)))
            left = (part % 3) * D + group * GROUP
            cols = (slice(None), slice(left, left + GROUP))
            weight = weight_ref[cols]
            news = lamb_moments(weight, grad, first_ref[cols], second_ref[cols], decay_mat)
            for ref, value in zip(outs[3 * tensor : 3 * tensor + 3], news):
                ref[cols] = value
            sums[tensor] += square_sum(weight)
            sums[2 + tensor] += square_sum(news[2])
    load_ref = outs[6]
    load_ref[...] = jnp.zeros_like(load_ref)
    load_ref[0:2, :] = one_ref[0:2, :]
    load_ref[2:7, :] = two_ref[0:5, :]
    for i in range(FF // D):
        load_ref[7 + i : 8 + i, :] = bias_ref[i, 0:1, :]
    squares = sq_ref[...] + lanes_of(list(zip((0, 1, 4, 5), sums)))
    load_ref[LOAD_SQ : LOAD_SQ + 1, 0:128] = squares[0:1]


LOAD_SQ = 7 + FF // D
LOAD_ROWS = 16


def attn_lamb(moments, mine, gots, gvec_one, gvec_two, gbias, squares):
    qkv_like = jax.ShapeDtypeStruct(moments[0].shape, f32)
    proj_like = jax.ShapeDtypeStruct(moments[3].shape, f32)
    return pl.pallas_call(
        partial(attn_lamb_kernel, gots=len(gots)),
        out_shape=[qkv_like] * 3 + [proj_like] * 3
        + [jax.ShapeDtypeStruct((LOAD_ROWS, D), f32)],
        compiler_params=params(24),
        cost_estimate=cost(40 * mine.size, 40 * mine.size),
        name="attn_lamb",
    )(*moments, mine, *gots, gvec_one, gvec_two, gbias, squares)


def last_kernel(
    load_ref, qkv_ref, proj_ref, up_ref, down_ref, qkv_upd, proj_upd, up_upd, down_upd,
    bias_ref, bias_one, bias_two, vec_ref, vec_one, vec_two,
    norms_ref, qkv_new, proj_new, up_new, down_new,
    bias_new, bias_first, bias_second, vec_new, vec_first, vec_second, bias_scr,
):
    norms = jnp.sqrt(load_ref[LOAD_SQ : LOAD_SQ + 1, 0:128])
    norms_ref[0:1, :] = norms[:, 0:4]
    norms_ref[1:2, :] = norms[:, 4:8]
    for i, (weight, upd, new) in enumerate(
        (
            (qkv_ref, qkv_upd, qkv_new), (proj_ref, proj_upd, proj_new),
            (up_ref, up_upd, up_new), (down_ref, down_upd, down_new),
        )
    ):
        ratio = norms[:, i : i + 1] / norms[:, 4 + i : 5 + i]
        new[...] = weight[...] - rate_lamb * ratio * upd[...]
    for i in range(FF // 128):
        row, left = 7 + i // (D // 128), i % (D // 128) * 128
        bias_scr[i : i + 1, :] = load_ref[row : row + 1, left : left + 128]
    bias = bias_ref[...]
    first, second, upd = lamb_moments(bias, bias_scr[...], bias_one[...], bias_two[...], 0.0)
    bias_first[...] = first
    bias_second[...] = second
    bias_new[...] = bias - rate_lamb * (
        jnp.sqrt(square_sum(bias)) / jnp.sqrt(square_sum(upd))
    ) * upd
    vec = vec_ref[...]
    first, second, upd = lamb_moments(vec, load_ref[0:7, :], vec_one[...], vec_two[...], 0.0)
    vec_first[...] = first
    vec_second[...] = second
    ratio = jnp.sqrt(jnp.sum(vec * vec, -1, keepdims=True)) / jnp.sqrt(
        jnp.sum(upd * upd, -1, keepdims=True)
    )
    vec_new[...] = vec - rate_lamb * ratio * upd


def last(load, weights, upds, bias, vecs):
    def like(value):
        return jax.ShapeDtypeStruct(value.shape, f32)

    return pl.pallas_call(
        last_kernel,
        out_shape=[jax.ShapeDtypeStruct((2, 4), f32)] + [like(w) for w in weights]
        + [like(b) for b in bias] + [like(v) for v in vecs],
        scratch_shapes=[pltpu.VMEM((FF // 128, 128), f32)],
        compiler_params=params(24),
        cost_estimate=cost(1 << 20, 4 << 20),
        name="last",
    )(load, *weights, *upds, *bias, *vecs)


def swap(value, axis, size, bit):
    return lax.ppermute(value, axis, [(i, i ^ bit) for i in range(size)])


def on_device(
    tokens, image_ids, selected, cotangent,
    qkv_weight, qkv_first, qkv_second, proj_weight, proj_first, proj_second,
    up_weight, up_first, up_second, down_weight, down_first, down_second,
    up_bias, bias_first, bias_second, vectors, vector_first, vector_second,
    *, dp, mp,
):
    world = dp * mp
    dq_at, dc_at, mp_at = (lax.axis_index(name) for name in ("dq", "dc", "mp"))
    dp_at = dq_at * 2 + dc_at
    me = jnp.stack([dp_at * mp + mp_at, mp_at, dp_at]).astype(jnp.int32)
    everyone = ("dq", "dc", "mp")
    fast = (D // world) % 8 == 0 and dp >= 4 and (D // dp) % 16 == 0

    def swap_dp(value, bit):
        if bit == 1:
            return swap(value, "dc", 2, 1)
        return swap(value, "dq", dp // 2, bit // 2)

    def swap_mp(value, bit):
        return swap(value, "mp", mp, bit)

    bits = []
    bit = 2
    while bit < dp:
        bits.append(bit)
        bit *= 2
    ups, downs = tuple(bits), tuple(reversed(bits))

    def tie(*values):
        return lax.optimization_barrier(values)

    def total(terms):
        result = terms[0].astype(f32)
        for term in terms[1:]:
            result = result + term.astype(f32)
        return result

    def merge(held, came, high, axis):
        return jnp.where(high, jnp.stack([came, held], axis), jnp.stack([held, came], axis))

    size = D // world
    low_qkv = qkv_weight.astype(bf16).reshape(size, 3, GROUPS, GROUP).transpose(0, 2, 1, 3)
    low_qkv = low_qkv.reshape(size, 3 * D)
    proj_low = proj_weight.astype(bf16)
    mlp_low = jnp.concatenate([up_weight.astype(bf16), down_weight.astype(bf16).T], 0)
    picked = pick_rows(selected, image_ids, tokens, cotangent, vectors)
    if fast:
        held = [low_qkv] + [swap_mp(low_qkv, k) for k in range(1, mp)]
        held, picked = tie(held, picked)
        held = jnp.stack(held).reshape((2,) * (mp.bit_length() - 1) + (size, 3 * D))
        for axis in range(mp.bit_length() - 1):
            flip = ((mp_at >> (mp.bit_length() - 2 - axis)) & 1) != 0
            held = jnp.where(flip, jnp.flip(held, axis), held)
        held = held.reshape(mp, size, 3 * D)
        halves = []
        for half, order in enumerate((ups, downs)):
            value = held[:, :, half * D * 3 // 2 : (half + 1) * D * 3 // 2]
            done = []
            for bit in order + (1,):
                axis = sum(other > bit for other in done)
                done.append(bit)
                value = merge(value, swap_dp(value, bit), (dp_at & bit) != 0, axis)
            halves.append(value.reshape(D, 3 * D // 2))
        w_qkv = jnp.concatenate(halves, 1)
        mlp_mat = lax.all_gather(
            jnp.concatenate([mlp_low, proj_low], 0), everyone, axis=0, tiled=True
        )
        mlp_mat = mlp_mat.reshape(dp, mp, mlp_low.shape[0] + size, FF // mp)
        w_o = mlp_mat[:, :, mlp_low.shape[0] :].reshape(D, D)
    else:
        w_qkv = lax.all_gather(low_qkv, everyone, axis=0, tiled=True)
        w_o = lax.all_gather(proj_low, everyone, axis=0, tiled=True)
        mlp_mat = lax.all_gather(mlp_low, everyone, axis=0, tiled=True)
        mlp_mat = mlp_mat.reshape(dp, mp, 2, D // dp, FF // mp).transpose(1, 2, 0, 3, 4)
        mlp_mat = mlp_mat.reshape(1, mp, 2 * D, FF // mp)

    def view(term, **more):
        array, names, fixed = term
        fixed = {**fixed, **more}
        start = [fixed.get(name, 0) for name in names] + [0, 0]
        extent = [1 if name in fixed else n for name, n in zip(names, array.shape)]
        kept = [n for name, n in zip(names, array.shape) if name not in fixed]
        out = lax.dynamic_slice(array, start, tuple(extent) + array.shape[-2:])
        return out.reshape(tuple(kept) + array.shape[-2:])

    def name_of(bit):
        return f"b{bit}"

    def opened(array, which=None):
        names = [name_of(bit) for bit in reversed(bits)] + ["mp"]
        fixed = {}
        shape = (2,) * len(bits) + (mp,) + array.shape[-2:]
        if which is not None:
            names, shape, fixed = ["which"] + names, (2,) + shape, {"which": which}
        return (array.reshape(shape), names, fixed)

    def step(chains):
        for chain in chains:
            terms, order = chain
            bit = order.pop(0)
            name, mine = name_of(bit), (dp_at // bit) & 1
            give = total([view(term, **{name: 1 - mine}) for term in terms]).astype(bf16)
            left = [n for n in terms[0][1] if n not in terms[0][2] and n != name]
            chain[0] = [(t[0], t[1], {**t[2], name: mine}) for t in terms]
            chain[0].append((swap_dp(give, bit), left, {}))

    def newest(chains):
        return [chain[0][-1][0] for chain in chains]

    def renew(chains, arrays):
        for chain, array in zip(chains, arrays):
            chain[0][-1] = (array,) + chain[0][-1][1:]

    x, dy, a, at, dm, rank, bounds = picked
    q, k, v, ctx, lse = attend_forward(a, w_qkv, bounds)
    att, c = middle(ctx, w_o, x, vectors)
    mlp, dc, mlp_keep, mlp_send, gbias = mlp_all(me, c, dm, mlp_mat, up_bias, fast)
    plan = (world, mp) if fast else None
    spans = ((0, GROUPS - 1), (GROUPS - 1, 1))
    back = partial(attend_backward, me, at, q, k, v, ctx)
    if fast:
        mlp_came = swap_dp(mlp_send, 1)
    y, part, dctx, gwo, gvec_two = turn(x, dy, att, mlp, dc, ctx, w_o, vectors)
    if fast:
        mlp_came, dctx = tie(mlp_came, dctx)
        chains = [
            [[opened(mlp_keep, which), opened(mlp_came, which)], list(order)]
            for which, order in enumerate((ups, downs))
        ]
        step(chains)
        d_one, keep_one, send_one = back(dctx, lse, bounds, gwo, plan, *spans[0])
        arrays, d_one, send_one, dctx = tie(newest(chains), d_one, send_one, dctx)
        renew(chains, arrays)
        while chains[0][1]:
            step(chains)
        came_one = swap_dp(send_one, 1)
        d_two, keep_two, send_two = back(dctx, lse, bounds, gwo, plan, *spans[1])
        arrays, came_one, send_two, d_two, y = tie(newest(chains), came_one, send_two, d_two, y)
        renew(chains, arrays)
        mlp_sent = []
        for k_at in range(1, mp):
            give = jnp.stack([total([view(t, mp=k_at) for t in chain[0]]) for chain in chains])
            mlp_sent.append(swap_mp(give.astype(bf16), k_at))
        mlp_mine = jnp.stack([total([view(t, mp=0) for t in chain[0]]) for chain in chains])
        one = [[opened(keep_one), opened(came_one)], list(ups)]
        came_two = swap_dp(send_two, 1)
        step([one])
        block_output = place(y, rank, tokens)
        came_two, block_output, d_one = tie(came_two, block_output, d_one)
        two = [[opened(keep_two), opened(came_two)], list(downs)]
        step([two])
        grad, gvec_one = entry((d_one, d_two), spans, w_qkv, x, part, vectors)
        arrays, grad, gvec_one = tie(newest([one, two]), grad, gvec_one)
        renew([one, two], arrays)
        while one[1]:
            step([one, two])
        input_grad = finish(grad, rank, cotangent)
        arrays, input_grad, mlp_sent = tie(newest([one, two]), input_grad, mlp_sent)
        renew([one, two], arrays)
        attn_sent = []
        for k_at in range(1, mp):
            give = [
                total([view(t, mp=mp_at ^ k_at) for t in chain[0]]).astype(bf16)
                for chain in (one, two)
            ]
            attn_sent.append(swap_mp(jnp.concatenate(give, 1), k_at))
        attn_mine = jnp.concatenate(
            [total([view(t, mp=mp_at) for t in chain[0]]) for chain in (one, two)], 1
        )
    else:
        d_all, attn_keep, _ = back(dctx, lse, bounds, gwo, plan, 0, GROUPS)
        block_output = place(y, rank, tokens)
        grad, gvec_one = entry((d_all,), ((0, GROUPS),), w_qkv, x, part, vectors)
        input_grad = finish(grad, rank, cotangent)
        shaped = mlp_keep[:, 0].reshape(2, mp, dp, D // dp, FF // mp)
        shaped = jnp.take(shaped, mp_at ^ jnp.arange(mp), axis=1)
        shaped = shaped.transpose(2, 1, 0, 3, 4).reshape(world, 2, D // dp, FF // mp)
        mlp_mine = lax.psum_scatter(shaped, everyone, scatter_dimension=0, tiled=True)[0]
        mlp_mine = mlp_mine.astype(f32)
        attn_mine = lax.psum_scatter(attn_keep[0], everyone, scatter_dimension=0, tiled=True)
        attn_mine = attn_mine.astype(f32)
        mlp_sent, attn_sent = [], []

    *mlp_news, squares = mlp_lamb(
        (up_weight, up_first, up_second, down_weight.T, down_first.T, down_second.T),
        mlp_mine, mlp_sent,
    )
    *attn_news, load = attn_lamb(
        (qkv_weight, qkv_first, qkv_second, proj_weight, proj_first, proj_second),
        attn_mine, attn_sent, gvec_one, gvec_two, gbias, squares,
    )
    if fast:
        bit = 1
        while bit < dp:
            load = load + swap_dp(load, bit)
            bit *= 2
        bit = 1
        while bit < mp:
            load = load + swap_mp(load, bit)
            bit *= 2
    else:
        load = lax.psum(load, everyone)
    square = (FF // 128, 128)
    (
        weight_norms, qkv_new, proj_new, up_new, down_new,
        bias_new, bias_first_new, bias_second_new, *vector_news,
    ) = last(
        load,
        (qkv_weight, proj_weight, up_weight, down_weight.T),
        (attn_news[2], attn_news[5], mlp_news[2], mlp_news[5]),
        [value.reshape(square) for value in (up_bias, bias_first, bias_second)],
        (vectors, vector_first, vector_second),
    )
    return (
        block_output, input_grad, weight_norms,
        qkv_new, attn_news[0], attn_news[1],
        proj_new, attn_news[3], attn_news[4],
        up_new, mlp_news[0], mlp_news[1],
        down_new.T, mlp_news[3].T, mlp_news[4].T,
        bias_new.reshape(FF), bias_first_new.reshape(FF), bias_second_new.reshape(FF),
        *vector_news,
    )


def solution(mesh):
    dp, mp = mesh.shape["dp"], mesh.shape["mp"]
    split = Mesh(mesh.devices.reshape(dp // 2, 2, mp), ("dq", "dc", "mp"))
    rows = ("dq", "dc", "mp")
    by_rows = (P(rows, None),) * 3
    shared = (P(),) * 3
    up_spec = (P(("dq", "dc"), "mp"),) * 3
    down_spec = (P("mp", ("dq", "dc")),) * 3
    in_specs = (
        (P(rows, None, None), P(rows, None), P(rows, None), P(rows, None, None))
        + by_rows + by_rows + up_spec + down_spec + shared + shared
    )
    out_specs = (
        (P(rows, None, None), P(rows, None, None), P())
        + by_rows + by_rows + up_spec + down_spec + shared + shared
    )
    return jax.shard_map(
        partial(on_device, dp=dp, mp=mp),
        mesh=split, in_specs=in_specs, out_specs=out_specs, check_vma=False,
    )
```

```python
from functools import partial
import math

import jax
import jax.numpy as jnp
from jax import lax
from jax.experimental import pallas as pl
from jax.experimental.pallas import tpu as pltpu
from jax.sharding import Mesh, PartitionSpec as P

D = 768
FF = 3072
HEADS = 12
HEAD_DIM = 64
CAP = 640
SEQ = 1280
STEP = 10

eps_norm = 1e-06
eps_adam = 1e-06
beta_one = 0.9
beta_two = 0.999
decay_mat = 0.01
rate_lamb = 0.3
masked_score = -1e30

f32 = jnp.float32
bf16 = jnp.bfloat16
GROUP = 256
GROUPS = D // GROUP
LOG2E = 1.0 / math.log(2.0)
SCORE_SCALE = 1.0 / math.sqrt(HEAD_DIM)
ROUTER_SCALE = 1.0 / math.sqrt(D)


def dot_ab(left, right, left_dim=1, right_dim=0):
    return lax.dot_general(
        left, right, (((left_dim,), (right_dim,)), ((), ())), preferred_element_type=f32
    )


def params(mib, **more):
    return pltpu.CompilerParams(vmem_limit_bytes=mib << 20, **more)


def hbm(shape, dtype):
    return pltpu.HBM(shape, dtype)


def pinned(*arrays):
    return [
        pltpu.with_memory_space_constraint(array, pltpu.HBM) if array.size >= 1 << 17 else array
        for array in arrays
    ]


def cost(flops, nbytes, trans=0):
    return pl.CostEstimate(flops=int(flops), bytes_accessed=int(nbytes), transcendentals=int(trans))


def norm_parts(values):
    center = jnp.mean(values, -1, keepdims=True)
    offset = values - center
    spread = jnp.mean(offset * offset, -1, keepdims=True)
    inverse = lax.rsqrt(spread + eps_norm)
    return offset * inverse, inverse


def norm_back(grad, normalized, inverse, gain):
    scaled = grad * gain
    return inverse * (
        scaled
        - jnp.mean(scaled, -1, keepdims=True)
        - normalized * jnp.mean(scaled * normalized, -1, keepdims=True)
    )


def ranks_of(sel, ids):
    kind = jnp.where(ids < 0, 2, ids)
    sub = lax.broadcasted_iota(jnp.int32, (8, SEQ), 0)
    lane = lax.broadcasted_iota(jnp.int32, (8, SEQ), 1)
    member = jnp.where(jnp.broadcast_to(kind, (8, SEQ)) == sub, jnp.broadcast_to(sel, (8, SEQ)), 0)
    total = member
    step = 1
    while step < SEQ:
        total = total + jnp.where(lane >= step, pltpu.roll(total, step, 1), 0)
        step *= 2
    count = jnp.max(total, axis=1, keepdims=True)
    first = count[0:1]
    second = first + count[1:2]
    base = jnp.where(sub == 0, 0, jnp.where(sub == 1, first, second))
    rank = jnp.sum(member * (total + base), axis=0, keepdims=True) - 1
    return rank, first, second


def one_hot(rank):
    place = lax.broadcasted_iota(jnp.int32, (CAP, SEQ), 0)
    return jnp.where(place == rank, 1.0, 0.0).astype(bf16)


def pick_kernel(
    sel_ref, ids_ref, tok_ref, cot_ref, vec_ref,
    x_ref, dy_ref, a_ref, at_ref, dm_ref, rank_ref, bounds_ref, x_scr, dy_scr,
):
    rank, first, second = ranks_of(sel_ref[0], ids_ref[0])
    rank_ref[0] = jnp.broadcast_to(rank, (8, SEQ))
    lane = lax.broadcasted_iota(jnp.int32, (8, 128), 1)
    bounds_ref[0] = jnp.where(lane == 0, first, second)
    hot = one_hot(rank)
    x_scr[...] = dot_ab(hot, tok_ref[0])
    dy_scr[...] = dot_ab(hot, cot_ref[0])
    tile = 128

    def body(i, carry):
        rows = pl.ds(pl.multiple_of(i * tile, tile), tile)
        x = x_scr[rows, :]
        dy = dy_scr[rows, :]
        normalized, _ = norm_parts(x)
        low = (normalized * vec_ref[0:1, :] + vec_ref[1:2, :]).astype(bf16)
        gate = jax.nn.sigmoid(jnp.sum(x * vec_ref[4:5, :], -1, keepdims=True) * ROUTER_SCALE)
        x_ref[rows, :] = x.astype(bf16)
        dy_ref[rows, :] = dy.astype(bf16)
        a_ref[rows, :] = low
        dm_ref[rows, :] = (gate * dy).astype(bf16)
        return carry

    lax.fori_loop(0, CAP // tile, body, 0, unroll=True)
    at_ref[...] = a_ref[...].T


def pick_rows(sel, ids, tokens, cotangent, vectors):
    rows = tokens.shape[0]
    count = rows * CAP
    wide = pl.BlockSpec((CAP, D), lambda r: (r, 0))
    line = pl.BlockSpec((1, 1, SEQ), lambda r: (r, 0, 0))
    full = pl.BlockSpec((1, SEQ, D), lambda r: (r, 0, 0))
    return pl.pallas_call(
        pick_kernel,
        grid=(rows,),
        in_specs=[line, line, full, full, pl.BlockSpec((7, D), lambda r: (0, 0))],
        out_specs=[
            wide, wide, wide, pl.BlockSpec((D, CAP), lambda r: (0, r)), wide,
            pl.BlockSpec((1, 8, SEQ), lambda r: (r, 0, 0)),
            pl.BlockSpec((1, 8, 128), lambda r: (r, 0, 0)),
        ],
        out_shape=[
            hbm((count, D), bf16),
            hbm((count, D), bf16),
            hbm((count, D), bf16),
            hbm((D, count), bf16),
            hbm((count, D), bf16),
            hbm((rows, 8, SEQ), jnp.int32),
            hbm((rows, 8, 128), jnp.int32),
        ],
        scratch_shapes=[pltpu.VMEM((CAP, D), f32), pltpu.VMEM((CAP, D), f32)],
        compiler_params=params(40),
        cost_estimate=cost(4 * count * SEQ * D, 4 * rows * SEQ * D * 2),
        name="pick_rows",
    )(*pinned(sel[:, None, :], ids[:, None, :], tokens, cotangent, vectors))


def fill_bias(bias_scr, bounds_ref):
    first = bounds_ref[0, 0:1, 0:1]
    second = bounds_ref[0, 0:1, 1:2]
    tile = 128
    key = lax.broadcasted_iota(jnp.int32, (tile, CAP), 1)
    key_kind = jnp.where(key >= first, 1, 0) + jnp.where(key >= second, 1, 0)
    for i in range(CAP // tile):
        row = lax.broadcasted_iota(jnp.int32, (tile, CAP), 0) + i * tile
        row_kind = jnp.where(row >= first, 1, 0) + jnp.where(row >= second, 1, 0)
        bias_scr[i * tile : (i + 1) * tile, :] = jnp.where(row_kind == key_kind, 0.0, masked_score)


def half_masks():
    lane = lax.broadcasted_iota(jnp.int32, (1, 128), 1)
    low = jnp.where(lane < HEAD_DIM, 1.0, 0.0)
    return low, 1.0 - low


def attend_kernel(
    a_ref, w_ref, bounds_ref,
    q_ref, k_ref, v_ref, ctx_ref, probs_ref, bias_scr,
):
    @pl.when(pl.program_id(1) == 0)
    def _():
        fill_bias(bias_scr, bounds_ref)

    a = a_ref[...]
    for part, ref in enumerate((q_ref, k_ref, v_ref)):
        ref[...] = dot_ab(a, w_ref[:, part * GROUP : (part + 1) * GROUP]).astype(bf16)
    masks = half_masks()
    lane = lax.broadcasted_iota(jnp.int32, (1, 128), 1)
    for pair in range(GROUP // 128):
        cols = slice(pair * 128, pair * 128 + 128)
        queries, key_rows, values = q_ref[:, cols], k_ref[:, cols], v_ref[:, cols]
        halves = []
        for half in range(2):
            scores = dot_ab(queries * masks[half].astype(bf16), key_rows, 1, 1)
            scores = scores * (SCORE_SCALE * LOG2E) + bias_scr[...]
            row_max = jnp.max(scores, -1, keepdims=True)
            probs = jnp.exp2(scores - row_max)
            row_total = jnp.sum(probs, -1, keepdims=True)
            probs = (probs * (1.0 / row_total)).astype(bf16)
            probs_ref[0, pair * 2 + half] = probs
            halves.append(dot_ab(probs, values))
        ctx_ref[:, cols] = jnp.where(lane < HEAD_DIM, halves[0], halves[1]).astype(bf16)


def attend_forward(a, w_all, bounds):
    count = a.shape[0]
    rows = count // CAP
    piece = pl.BlockSpec((CAP, GROUP), lambda r, g: (r, g))
    narrow = hbm((count, D), bf16)
    return pl.pallas_call(
        attend_kernel,
        grid=(rows, GROUPS),
        in_specs=[
            pl.BlockSpec((CAP, D), lambda r, g: (r, 0)),
            pl.BlockSpec((D, 3 * GROUP), lambda r, g: (0, g)),
            pl.BlockSpec((1, 8, 128), lambda r, g: (r, 0, 0)),
        ],
        out_specs=[
            piece, piece, piece, piece,
            pl.BlockSpec((1, GROUP // HEAD_DIM, CAP, CAP), lambda r, g: (r, g, 0, 0)),
        ],
        out_shape=[narrow, narrow, narrow, narrow, hbm((rows, HEADS, CAP, CAP), bf16)],
        scratch_shapes=[pltpu.VMEM((CAP, CAP), f32)],
        compiler_params=params(48),
        cost_estimate=cost(
            2 * count * D * 3 * D + rows * HEADS * 16 * CAP * CAP * HEAD_DIM, 12 * count * D,
            rows * HEADS * CAP * CAP,
        ),
        name="attend_forward",
    )(*pinned(a, w_all, bounds))


def attend_back_kernel(
    me_ref, at_ref, q_ref, k_ref, v_ref, ctx_ref, dctx_ref, probs_ref, gwo_ref,
    d_ref, keep_ref, send_ref, held_scr, acc_scr, *, plan,
):
    row = pl.program_id(1)
    masks = half_masks()
    lane = lax.broadcasted_iota(jnp.int32, (1, 128), 1)
    for pair in range(GROUP // 128):
        cols = slice(pair * 128, pair * 128 + 128)
        queries, key_rows, values = q_ref[:, cols], k_ref[:, cols], v_ref[:, cols]
        grads = dctx_ref[:, cols]
        product = ctx_ref[:, cols].astype(f32) * grads.astype(f32)
        queries_t, grads_t = queries.T, grads.T
        dq, dk_t, dv_t = [], [], []
        for half in range(2):
            mask_low = masks[half].astype(bf16)
            span = slice(half * HEAD_DIM, half * HEAD_DIM + HEAD_DIM)
            probs = probs_ref[0, pair * 2 + half]
            delta = jnp.sum(product * masks[half], -1, keepdims=True)
            probs_grad = dot_ab(grads * mask_low, values, 1, 1)
            score_grad = (probs.astype(f32) * (probs_grad - delta)).astype(bf16)
            dq.append(dot_ab(score_grad, key_rows))
            dk_t.append(dot_ab(queries_t[span], score_grad))
            dv_t.append(dot_ab(grads_t[span], probs))
        place = pair * 128
        d_ref[:, place : place + 128] = (jnp.where(lane < HEAD_DIM, dq[0], dq[1]) * SCORE_SCALE).astype(bf16)
        place += GROUP
        d_ref[:, place : place + 128] = (jnp.concatenate(dk_t, 0) * SCORE_SCALE).astype(bf16).T
        place += GROUP
        d_ref[:, place : place + 128] = jnp.concatenate(dv_t, 0).astype(bf16).T
    held_scr[pl.ds(pl.multiple_of(row * CAP, CAP), CAP), :] = d_ref[...]

    @pl.when(row == pl.num_programs(1) - 1)
    def _():
        acc_scr[:, : 3 * GROUP] = dot_ab(at_ref[...], held_scr[...])
        acc_scr[:, 3 * GROUP :] = gwo_ref[...]
        split_blocks(me_ref, acc_scr, keep_ref, send_ref, plan)


def split_blocks(me_ref, acc_scr, keep_ref, send_ref, plan):
    if plan is None:
        keep_ref[0] = acc_scr[...].astype(bf16)
        send_ref[0] = jnp.zeros_like(send_ref[0])
        return
    blocks, core_bit = plan
    size = D // blocks
    on_high = (me_ref[0] & core_bit) != 0
    for block in range(blocks):
        if block & core_bit:
            continue
        low = acc_scr[block * size : (block + 1) * size, :]
        other = block | core_bit
        high = acc_scr[other * size : (other + 1) * size, :]
        slot = (block // (2 * core_bit)) * core_bit + block % core_bit
        keep_ref[slot] = jnp.where(on_high, high, low).astype(bf16)
        send_ref[slot] = jnp.where(on_high, low, high).astype(bf16)


def attend_backward(me, at, q, k, v, ctx, probs, dctx, gwo, plan, start, groups):
    count = q.shape[0]
    rows = count // CAP
    piece = pl.BlockSpec((CAP, GROUP), lambda g, r, me: (r, g + start))
    if plan is None:
        half, size, sent = 1, D, 8
    else:
        half, size = plan[0] // 2, D // plan[0]
        sent = size
    width = 4 * GROUP
    return pl.pallas_call(
        partial(attend_back_kernel, plan=plan),
        grid_spec=pltpu.PrefetchScalarGridSpec(
            num_scalar_prefetch=1,
            grid=(groups, rows),
            in_specs=[
                pl.BlockSpec((D, count), lambda g, r, me: (0, 0)),
                piece, piece, piece, piece, piece,
                pl.BlockSpec(
                    (1, GROUP // HEAD_DIM, CAP, CAP), lambda g, r, me: (r, g + start, 0, 0)
                ),
                pl.BlockSpec((D, GROUP), lambda g, r, me: (0, g + start)),
            ],
            out_specs=[
                pl.BlockSpec((CAP, 3 * GROUP), lambda g, r, me: (r, g)),
                pl.BlockSpec((half, size, width), lambda g, r, me: (0, 0, g)),
                pl.BlockSpec((half, sent, width), lambda g, r, me: (0, 0, g)),
            ],
            scratch_shapes=[
                pltpu.VMEM((count, 3 * GROUP), bf16), pltpu.VMEM((D, width), f32),
            ],
        ),
        out_shape=[
            hbm((count, groups * 3 * GROUP), bf16),
            hbm((half, size, groups * width), bf16),
            hbm((half, sent, groups * width), bf16),
        ],
        compiler_params=params(40),
        cost_estimate=cost(
            groups * GROUP * (6 * count * D + 40 * count * CAP),
            groups * GROUP * 20 * count,
            groups * (GROUP // HEAD_DIM) * count * CAP,
        ),
        name="attend_backward",
    )(me, *pinned(at, q, k, v, ctx, dctx, probs, gwo))


def middle_kernel(ctx_ref, wo_ref, x_ref, vec_ref, att_ref, c_ref):
    att = dot_ab(ctx_ref[...], wo_ref[...]) + vec_ref[5:6, :]
    att_ref[...] = att
    normalized, _ = norm_parts(x_ref[...].astype(f32) + att)
    c_ref[...] = (normalized * vec_ref[2:3, :] + vec_ref[3:4, :]).astype(bf16)


def middle(ctx, w_all, x, vectors):
    count = ctx.shape[0]
    tile = 320
    wide = pl.BlockSpec((tile, D), lambda t: (t, 0))
    return pl.pallas_call(
        middle_kernel,
        grid=(count // tile,),
        in_specs=[
            wide, pl.BlockSpec((D, D), lambda t: (0, 3)), wide,
            pl.BlockSpec((7, D), lambda t: (0, 0)),
        ],
        out_specs=[wide, wide],
        out_shape=[
            hbm((count, D), f32),
            hbm((count, D), bf16),
        ],
        compiler_params=params(32),
        cost_estimate=cost(2 * count * D * D, 10 * count * D),
        name="middle",
    )(*pinned(ctx, w_all, x, vectors))


ERF_P = 0.3275911 / math.sqrt(2.0)
ERF_COEF = (0.254829592, -0.284496736, 1.421413741, -1.453152027, 1.061405429)


def gelu_parts(u):
    bell = jnp.exp2(u * u * (-0.5 * LOG2E))
    t = 1.0 / (1.0 + ERF_P * jnp.abs(u))
    poly = ERF_COEF[4]
    for coef in ERF_COEF[3::-1]:
        poly = poly * t + coef
    tail = (0.5 * poly * t) * bell
    phi = jnp.where(u >= 0, 1.0 - tail, tail)
    return u * phi, phi + u * (bell * (1.0 / math.sqrt(2.0 * math.pi)))


def mlp_kernel(
    me_ref, c_ref, dm_ref, wu_ref, wd_ref, bias_ref,
    mlp_ref, dc_ref, keep_ref, send_ref, gbias_ref, ct_scr, dmt_scr, *, blocks, split,
):
    first = (pl.program_id(0) == 0) & (pl.program_id(1) == 0)

    @pl.when(first)
    def _():
        ct_scr[...] = c_ref[...].T
        dmt_scr[...] = dm_ref[...].T
        mlp_ref[...] = jnp.zeros_like(mlp_ref)
        dc_ref[...] = jnp.zeros_like(dc_ref)

    width = wu_ref.shape[-1]
    wu = wu_ref[...].reshape(D, width)
    wd = wd_ref[...].reshape(D, width)
    u = dot_ab(c_ref[...], wu) + bias_ref[0]
    act, slope = gelu_parts(u)
    act = act.astype(bf16)
    du = slope * dot_ab(dm_ref[...], wd)
    du = du.astype(bf16)
    gbias_ref[0] = jnp.broadcast_to(jnp.sum(du.astype(f32), 0, keepdims=True), (8, width))
    mlp_ref[...] += dot_ab(act, wd, 1, 1)
    dc_ref[...] += dot_ab(du, wu, 1, 1)
    size = D // blocks
    for which, grad in enumerate((dot_ab(ct_scr[...], du), dot_ab(dmt_scr[...], act))):
        if not split:
            keep_ref[which, 0, 0] = grad.astype(bf16)
            continue
        on_high = (me_ref[2] & 1) != 0
        for block in range(0, blocks, 2):
            low = grad[block * size : (block + 1) * size]
            high = grad[(block + 1) * size : (block + 2) * size]
            slot = block // 2
            keep_ref[which, slot, 0] = jnp.where(on_high, high, low).astype(bf16)
            send_ref[which, slot, 0] = jnp.where(on_high, low, high).astype(bf16)
    if not split:
        send_ref[...] = jnp.zeros_like(send_ref)


def mlp_all(me, c, dm, weights, bias, split):
    count = c.shape[0]
    blocks, mp, _, units = weights.shape
    size = D // blocks
    width = 768
    subs = units // width
    half = blocks // 2 if split else 1
    sent = size if split else 8
    rows_out = size if split else D
    all_rows = pl.BlockSpec((count, D), lambda j, s, me: (0, 0))

    def weight_spec(which):
        return pl.BlockSpec(
            (blocks, 1, size, width), lambda j, s, me, which=which: (0, me[1] ^ j, which, s)
        )

    return pl.pallas_call(
        partial(mlp_kernel, blocks=blocks, split=split),
        grid_spec=pltpu.PrefetchScalarGridSpec(
            num_scalar_prefetch=1,
            grid=(mp, subs),
            in_specs=[
                all_rows, all_rows, weight_spec(0), weight_spec(1),
                pl.BlockSpec((1, 1, width), lambda j, s, me: ((me[1] ^ j) * subs + s, 0, 0)),
            ],
            out_specs=[
                all_rows, all_rows,
                pl.BlockSpec((2, half, 1, rows_out, width), lambda j, s, me: (0, 0, j, 0, s)),
                pl.BlockSpec((2, half, 1, sent, width), lambda j, s, me: (0, 0, j, 0, s)),
                pl.BlockSpec((1, 8, width), lambda j, s, me: (me[1] ^ j, 0, s)),
            ],
            scratch_shapes=[pltpu.VMEM((D, count), bf16), pltpu.VMEM((D, count), bf16)],
        ),
        out_shape=[
            hbm((count, D), f32),
            hbm((count, D), f32),
            hbm((2, half, mp, rows_out, units), bf16),
            hbm((2, half, mp, sent, units), bf16),
            hbm((mp, 8, units), f32),
        ],
        compiler_params=params(62),
        cost_estimate=cost(
            12 * count * D * mp * units, 12 * count * D + 8 * mp * units * D, 2 * count * mp * units
        ),
        name="mlp_all",
    )(me, *pinned(c, dm, weights, weights, bias.reshape(mp * subs, 1, width)))


def turn_kernel(
    x_ref, dy_ref, att_ref, mlp_ref, dc_ref, ctx_ref, wo_ref, vec_ref,
    y_ref, part_ref, dctx_ref, gwo_ref, gvec_ref, datt_scr,
):
    step = pl.program_id(0)

    @pl.when(step == 0)
    def _():
        gvec_ref[...] = jnp.zeros_like(gvec_ref)
        gwo_ref[...] = jnp.zeros_like(gwo_ref)

    tile = 64
    router = vec_ref[4:5, :]

    def body(i, carry):
        rows = pl.ds(pl.multiple_of(i * tile, tile), tile)
        x = x_ref[rows, :].astype(f32)
        dy = dy_ref[rows, :].astype(f32)
        att = att_ref[rows, :]
        branch = att + mlp_ref[rows, :] + vec_ref[6:7, :]
        gate = jax.nn.sigmoid(jnp.sum(x * router, -1, keepdims=True) * ROUTER_SCALE)
        y_ref[rows, :] = (x + gate * branch).astype(bf16)
        dr = jnp.sum(dy * branch, -1, keepdims=True) * gate * (1.0 - gate) * ROUTER_SCALE
        e = gate * dy
        normalized, inverse = norm_parts(x + att)
        dc = dc_ref[rows, :]
        dh = norm_back(dc, normalized, inverse, vec_ref[2:3, :])
        datt = (e + dh).astype(bf16)
        datt_scr[rows, :] = datt
        part_ref[rows, :] = dy + dr * router + dh
        for place, term in enumerate(
            (dc * normalized, dc, dr * x, datt.astype(f32), e.astype(bf16).astype(f32))
        ):
            gvec_ref[place : place + 1, :] += jnp.sum(term, 0, keepdims=True)
        return carry

    lax.fori_loop(0, x_ref.shape[0] // tile, body, 0, unroll=True)
    datt = datt_scr[...]
    dctx_ref[...] = dot_ab(datt, wo_ref[...], 1, 1).astype(bf16)
    gwo_ref[...] += dot_ab(ctx_ref[...], datt, 0, 0)


def turn(x, dy, att, mlp, dc, ctx, w_all, vectors):
    count = x.shape[0]
    tile = 320
    wide = pl.BlockSpec((tile, D), lambda t: (t, 0))
    return pl.pallas_call(
        turn_kernel,
        grid=(count // tile,),
        in_specs=[
            wide, wide, wide, wide, wide, wide, pl.BlockSpec((D, D), lambda t: (0, 3)),
            pl.BlockSpec((7, D), lambda t: (0, 0)),
        ],
        out_specs=[
            wide, wide, wide, pl.BlockSpec((D, D), lambda t: (0, 0)),
            pl.BlockSpec((8, D), lambda t: (0, 0)),
        ],
        out_shape=[
            hbm((count, D), bf16),
            hbm((count, D), f32),
            hbm((count, D), bf16),
            hbm((D, D), f32),
            hbm((8, D), f32),
        ],
        scratch_shapes=[pltpu.VMEM((tile, D), bf16)],
        compiler_params=params(48),
        cost_estimate=cost(4 * count * D * D, 26 * count * D),
        name="turn",
    )(*pinned(x, dy, att, mlp, dc, ctx, w_all, vectors))


def entry_kernel(
    *refs, spans,
):
    count = len(spans)
    grads = refs[:count]
    w_refs, refs = refs[count : count + GROUPS], refs[count + GROUPS :]
    x_ref, part_ref, vec_ref, out_ref, gvec_ref, da_scr = refs

    @pl.when(pl.program_id(0) == 0)
    def _():
        gvec_ref[...] = jnp.zeros_like(gvec_ref)

    da = None
    for ref, (start, groups) in zip(grads, spans):
        for at in range(groups):
            term = dot_ab(ref[:, at * D : (at + 1) * D], w_refs[start + at][...], 1, 1)
            da = term if da is None else da + term
    da_scr[...] = da
    tile = 64

    def body(i, carry):
        rows = pl.ds(pl.multiple_of(i * tile, tile), tile)
        normalized, inverse = norm_parts(x_ref[rows, :].astype(f32))
        da = da_scr[rows, :]
        for place, term in enumerate((da * normalized, da)):
            gvec_ref[place : place + 1, :] += jnp.sum(term, 0, keepdims=True)
        grad = part_ref[rows, :] + norm_back(da, normalized, inverse, vec_ref[0:1, :])
        high = grad.astype(bf16)
        out_ref[rows, 0:D] = high
        out_ref[rows, D:] = (grad - high.astype(f32)).astype(bf16)
        return carry

    lax.fori_loop(0, x_ref.shape[0] // tile, body, 0, unroll=True)


def entry(grads, spans, w_all, x, part, vectors):
    count = x.shape[0]
    tile = 320
    wide = pl.BlockSpec((tile, D), lambda r: (r, 0))
    return pl.pallas_call(
        partial(entry_kernel, spans=spans),
        grid=(count // tile,),
        in_specs=[pl.BlockSpec((tile, g.shape[1]), lambda r: (r, 0)) for g in grads]
        + [pl.BlockSpec((D, D), lambda r, group=group: (0, group)) for group in range(GROUPS)]
        + [
            wide, wide, pl.BlockSpec((7, D), lambda r: (0, 0)),
        ],
        out_specs=[
            pl.BlockSpec((tile, 2 * D), lambda r: (r, 0)),
            pl.BlockSpec((8, D), lambda r: (0, 0)),
        ],
        out_shape=[
            hbm((count, 2 * D), bf16),
            hbm((8, D), f32),
        ],
        scratch_shapes=[pltpu.VMEM((tile, D), f32)],
        compiler_params=params(32),
        cost_estimate=cost(2 * count * D * 3 * D, 24 * count * D),
        name="entry",
    )(*pinned(*grads, *[w_all] * GROUPS, x, part, vectors))


def put_kernel(value_ref, rank_ref, base_ref, *refs, parts):
    out_ref, ext_scr = refs[-2:]
    ext_scr[:, 0 : parts * D] = value_ref[...]
    ext_scr[:, parts * D :] = jnp.ones((CAP, 128), bf16)
    placed = dot_ab(one_hot(rank_ref[0, 0:1, :]), ext_scr[...], 0, 0)
    kept = 1.0 - placed[:, parts * D : parts * D + 1]
    result = placed[:, 0:D]
    for part in range(1, parts):
        result = result + placed[:, part * D : (part + 1) * D]
    out_ref[0] = (result + kept * base_ref[0].astype(f32)).astype(out_ref.dtype)


def put_row(value, rank, base, row, dtype, before=None):
    parts = value.shape[1] // D
    full = pl.BlockSpec((1, SEQ, D), lambda r: (row, 0, 0))
    held = [] if before is None else [before]
    return pl.pallas_call(
        partial(put_kernel, parts=parts),
        grid=(1,),
        in_specs=[
            pl.BlockSpec((CAP, parts * D), lambda r: (row, 0)),
            pl.BlockSpec((1, 8, SEQ), lambda r: (row, 0, 0)),
            full,
        ]
        + [pl.BlockSpec(memory_space=pl.ANY)] * len(held),
        out_specs=full,
        out_shape=hbm(base.shape, dtype),
        input_output_aliases={3: 0} if held else {},
        scratch_shapes=[pltpu.VMEM((CAP, parts * D + 128), bf16)],
        compiler_params=params(48),
        cost_estimate=cost(2 * parts * CAP * SEQ * D, 5 * parts * CAP * D),
        name=f"put_row_{parts}",
    )(*pinned(value, rank, base), *held)


def lamb_moments(weight, gradient, first_mom, second_mom, decay):
    first_new = beta_one * first_mom + (1.0 - beta_one) * gradient
    second_new = beta_two * second_mom + (1.0 - beta_two) * gradient * gradient
    update = (
        first_new
        / (1.0 - beta_one**STEP)
        / (jnp.sqrt(second_new / (1.0 - beta_two**STEP)) + eps_adam)
        + decay * weight
    )
    return (first_new, second_new, update)


def square_sum(value):
    return jnp.sum(jnp.sum(value * value, 1, keepdims=True), 0, keepdims=True)


def added(mine_ref, got_refs, place):
    result = mine_ref[place]
    for ref in got_refs:
        result = result + ref[place].astype(f32)
    return result


def lanes_of(pairs):
    lane = lax.broadcasted_iota(jnp.int32, (8, 128), 1)
    result = jnp.zeros((8, 128), f32)
    for place, value in pairs:
        result = result + jnp.where(lane == place, value, 0.0)
    return result


def mlp_lamb_kernel(*refs, gots):
    weights, (mine_ref, *rest) = refs[:6], refs[6:]
    got_refs, outs = rest[:gots], rest[gots:]
    pairs = []
    for which in range(2):
        weight_ref, first_ref, second_ref = weights[3 * which : 3 * which + 3]
        grad = added(mine_ref, got_refs, which)
        weight = weight_ref[...]
        news = lamb_moments(weight, grad, first_ref[...], second_ref[...], decay_mat)
        for ref, value in zip(outs[3 * which : 3 * which + 3], news):
            ref[...] = value
        pairs += [(2 + which, square_sum(weight)), (6 + which, square_sum(news[2]))]
    outs[6][...] = lanes_of(pairs)


def mlp_lamb(moments, mine, gots):
    like = jax.ShapeDtypeStruct(moments[0].shape, f32)
    return pl.pallas_call(
        partial(mlp_lamb_kernel, gots=len(gots)),
        out_shape=[like] * 6 + [jax.ShapeDtypeStruct((8, 128), f32)],
        compiler_params=params(24),
        cost_estimate=cost(40 * mine.size, 40 * mine.size),
        name="mlp_lamb",
    )(*moments, mine, *gots)


def attn_lamb_kernel(*refs, gots):
    moments, (mine_ref, *rest) = refs[:6], refs[6:]
    got_refs, rest = rest[:gots], rest[gots:]
    one_ref, two_ref, bias_ref, sq_ref, *outs = rest
    sums = [jnp.zeros((1, 1), f32) for _ in range(4)]
    for part in range(4):
        tensor = part // 3
        weight_ref, first_ref, second_ref = moments[3 * tensor : 3 * tensor + 3]
        for group in range(GROUPS):
            left = (group * 4 + part) * GROUP
            grad = added(mine_ref, got_refs, (slice(None), slice(left, left + GROUP)))
            left = (part % 3) * D + group * GROUP
            cols = (slice(None), slice(left, left + GROUP))
            weight = weight_ref[cols]
            news = lamb_moments(weight, grad, first_ref[cols], second_ref[cols], decay_mat)
            for ref, value in zip(outs[3 * tensor : 3 * tensor + 3], news):
                ref[cols] = value
            sums[tensor] += square_sum(weight)
            sums[2 + tensor] += square_sum(news[2])
    load_ref = outs[6]
    load_ref[...] = jnp.zeros_like(load_ref)
    load_ref[0:2, :] = one_ref[0:2, :]
    load_ref[2:7, :] = two_ref[0:5, :]
    for i in range(FF // D):
        load_ref[7 + i : 8 + i, :] = bias_ref[i, 0:1, :]
    squares = sq_ref[...] + lanes_of(list(zip((0, 1, 4, 5), sums)))
    load_ref[LOAD_SQ : LOAD_SQ + 1, 0:128] = squares[0:1]


LOAD_SQ = 7 + FF // D
LOAD_ROWS = 16


def attn_lamb(moments, mine, gots, gvec_one, gvec_two, gbias, squares):
    qkv_like = jax.ShapeDtypeStruct(moments[0].shape, f32)
    proj_like = jax.ShapeDtypeStruct(moments[3].shape, f32)
    return pl.pallas_call(
        partial(attn_lamb_kernel, gots=len(gots)),
        out_shape=[qkv_like] * 3 + [proj_like] * 3
        + [jax.ShapeDtypeStruct((LOAD_ROWS, D), f32)],
        compiler_params=params(24),
        cost_estimate=cost(40 * mine.size, 40 * mine.size),
        name="attn_lamb",
    )(*moments, mine, *gots, gvec_one, gvec_two, gbias, squares)


def last_kernel(
    load_ref, qkv_ref, proj_ref, up_ref, down_ref, qkv_upd, proj_upd, up_upd, down_upd,
    bias_ref, bias_one, bias_two, vec_ref, vec_one, vec_two,
    norms_ref, qkv_new, proj_new, up_new, down_new,
    bias_new, bias_first, bias_second, vec_new, vec_first, vec_second, bias_scr,
):
    norms = jnp.sqrt(load_ref[LOAD_SQ : LOAD_SQ + 1, 0:128])
    norms_ref[0:1, :] = norms[:, 0:4]
    norms_ref[1:2, :] = norms[:, 4:8]
    for i, (weight, upd, new) in enumerate(
        (
            (qkv_ref, qkv_upd, qkv_new), (proj_ref, proj_upd, proj_new),
            (up_ref, up_upd, up_new), (down_ref, down_upd, down_new),
        )
    ):
        ratio = norms[:, i : i + 1] / norms[:, 4 + i : 5 + i]
        new[...] = weight[...] - rate_lamb * ratio * upd[...]
    for i in range(FF // 128):
        row, left = 7 + i // (D // 128), i % (D // 128) * 128
        bias_scr[i : i + 1, :] = load_ref[row : row + 1, left : left + 128]
    bias = bias_ref[...]
    first, second, upd = lamb_moments(bias, bias_scr[...], bias_one[...], bias_two[...], 0.0)
    bias_first[...] = first
    bias_second[...] = second
    bias_new[...] = bias - rate_lamb * (
        jnp.sqrt(square_sum(bias)) / jnp.sqrt(square_sum(upd))
    ) * upd
    vec = vec_ref[...]
    first, second, upd = lamb_moments(vec, load_ref[0:7, :], vec_one[...], vec_two[...], 0.0)
    vec_first[...] = first
    vec_second[...] = second
    ratio = jnp.sqrt(jnp.sum(vec * vec, -1, keepdims=True)) / jnp.sqrt(
        jnp.sum(upd * upd, -1, keepdims=True)
    )
    vec_new[...] = vec - rate_lamb * ratio * upd


def last(load, weights, upds, bias, vecs):
    def like(value):
        return jax.ShapeDtypeStruct(value.shape, f32)

    return pl.pallas_call(
        last_kernel,
        out_shape=[jax.ShapeDtypeStruct((2, 4), f32)] + [like(w) for w in weights]
        + [like(b) for b in bias] + [like(v) for v in vecs],
        scratch_shapes=[pltpu.VMEM((FF // 128, 128), f32)],
        compiler_params=params(24),
        cost_estimate=cost(1 << 20, 4 << 20),
        name="last",
    )(load, *weights, *upds, *bias, *vecs)


def swap(value, axis, size, bit):
    return lax.ppermute(value, axis, [(i, i ^ bit) for i in range(size)])


def on_device(
    tokens, image_ids, selected, cotangent,
    qkv_weight, qkv_first, qkv_second, proj_weight, proj_first, proj_second,
    up_weight, up_first, up_second, down_weight, down_first, down_second,
    up_bias, bias_first, bias_second, vectors, vector_first, vector_second,
    *, dp, mp,
):
    world = dp * mp
    rows = tokens.shape[0]
    dq_at, dc_at, mp_at = (lax.axis_index(name) for name in ("dq", "dc", "mp"))
    dp_at = dq_at * 2 + dc_at
    me = jnp.stack([dp_at * mp + mp_at, mp_at, dp_at]).astype(jnp.int32)
    everyone = ("dq", "dc", "mp")
    fast = (D // world) % 8 == 0 and dp >= 4 and (D // dp) % 16 == 0

    def swap_dp(value, bit):
        if bit == 1:
            return swap(value, "dc", 2, 1)
        return swap(value, "dq", dp // 2, bit // 2)

    def swap_mp(value, bit):
        return swap(value, "mp", mp, bit)

    bits = []
    bit = 2
    while bit < dp:
        bits.append(bit)
        bit *= 2
    ups, downs = tuple(bits), tuple(reversed(bits))

    def tie(*values):
        return lax.optimization_barrier(values)

    def total(terms):
        result = terms[0].astype(f32)
        for term in terms[1:]:
            result = result + term.astype(f32)
        return result

    def merge(held, came, high, axis):
        return jnp.where(high, jnp.stack([came, held], axis), jnp.stack([held, came], axis))

    size = D // world
    low_qkv = qkv_weight.astype(bf16).reshape(size, 3, GROUPS, GROUP).transpose(0, 2, 1, 3)
    low_qkv = low_qkv.reshape(size, 3 * D)
    proj_low = proj_weight.astype(bf16)
    mlp_low = jnp.concatenate([up_weight.astype(bf16), down_weight.astype(bf16).T], 0)
    picked = pick_rows(selected, image_ids, tokens, cotangent, vectors)
    mlp_mat = lax.all_gather(mlp_low, everyone, axis=0, tiled=True)
    mlp_mat = mlp_mat.reshape(dp, mp, 2 * (D // dp), FF // mp)

    def grown(value, bit, done):
        axis = sum(other > bit for other in done)
        done.append(bit)
        return merge(value, swap_dp(value, bit), (dp_at & bit) != 0, axis)

    low_all = jnp.concatenate([low_qkv, proj_low], 1)
    if fast:
        held = [low_all] + [swap_mp(low_all, k) for k in range(1, mp)]
        held, picked = tie(held, picked)
        held = jnp.stack(held).reshape((2,) * (mp.bit_length() - 1) + (size, 4 * D))
        for axis in range(mp.bit_length() - 1):
            flip = ((mp_at >> (mp.bit_length() - 2 - axis)) & 1) != 0
            held = jnp.where(flip, jnp.flip(held, axis), held)
        held = held.reshape(mp, size, 4 * D)
        halves = [held[:, :, half * 2 * D : (half + 1) * 2 * D] for half in range(2)]
        for half, order in enumerate((ups, downs)):
            done = []
            for bit in order + (1,):
                halves[half] = grown(halves[half], bit, done)
        w_all = jnp.concatenate([value.reshape(D, 2 * D) for value in halves], 1)
    else:
        w_all = lax.all_gather(low_all, everyone, axis=0, tiled=True)
        mlp_mat = mlp_mat.reshape(dp, mp, 2, D // dp, FF // mp).transpose(1, 2, 0, 3, 4)
        mlp_mat = mlp_mat.reshape(1, mp, 2 * D, FF // mp)

    def view(term, **more):
        array, names, fixed = term
        fixed = {**fixed, **more}
        start = [fixed.get(name, 0) for name in names] + [0, 0]
        extent = [1 if name in fixed else n for name, n in zip(names, array.shape)]
        kept = [n for name, n in zip(names, array.shape) if name not in fixed]
        out = lax.dynamic_slice(array, start, tuple(extent) + array.shape[-2:])
        return out.reshape(tuple(kept) + array.shape[-2:])

    def name_of(bit):
        return f"b{bit}"

    def opened(array, which=None):
        names = [name_of(bit) for bit in reversed(bits)] + ["mp"]
        fixed = {}
        shape = (2,) * len(bits) + (mp,) + array.shape[-2:]
        if which is not None:
            names, shape, fixed = ["which"] + names, (2,) + shape, {"which": which}
        return (array.reshape(shape), names, fixed)

    def step(chains):
        for chain in chains:
            terms, order = chain
            bit = order.pop(0)
            name, mine = name_of(bit), (dp_at // bit) & 1
            give = total([view(term, **{name: 1 - mine}) for term in terms]).astype(bf16)
            left = [n for n in terms[0][1] if n not in terms[0][2] and n != name]
            chain[0] = [(t[0], t[1], {**t[2], name: mine}) for t in terms]
            chain[0].append((swap_dp(give, bit), left, {}))

    def newest(chains):
        return [chain[0][-1][0] for chain in chains]

    def renew(chains, arrays):
        for chain, array in zip(chains, arrays):
            chain[0][-1] = (array,) + chain[0][-1][1:]

    x, dy, a, at, dm, rank, bounds = picked
    q, k, v, ctx, probs = attend_forward(a, w_all, bounds)
    att, c = middle(ctx, w_all, x, vectors)
    mlp, dc, mlp_keep, mlp_send, gbias = mlp_all(me, c, dm, mlp_mat, up_bias, fast)
    plan = (world, mp) if fast else None
    spans = ((0, GROUPS - 1), (GROUPS - 1, 1))
    back = partial(attend_backward, me, at, q, k, v, ctx, probs)
    if fast:
        mlp_came = swap_dp(mlp_send, 1)
    y, part, dctx, gwo, gvec_two = turn(x, dy, att, mlp, dc, ctx, w_all, vectors)
    if fast:
        mlp_came, dctx = tie(mlp_came, dctx)
        chains = [
            [[opened(mlp_keep, which), opened(mlp_came, which)], list(order)]
            for which, order in enumerate((ups, downs))
        ]
        step(chains)
        d_one, keep_one, send_one = back(dctx, gwo, plan, *spans[0])
        arrays, d_one, send_one, dctx = tie(newest(chains), d_one, send_one, dctx)
        renew(chains, arrays)
        while chains[0][1]:
            step(chains)
        came_one = swap_dp(send_one, 1)
        d_two, keep_two, send_two = back(dctx, gwo, plan, *spans[1])
        arrays, came_one, send_two, d_two, y = tie(newest(chains), came_one, send_two, d_two, y)
        renew(chains, arrays)
        mlp_sent = []
        for k_at in range(1, mp):
            give = jnp.stack([total([view(t, mp=k_at) for t in chain[0]]) for chain in chains])
            mlp_sent.append(swap_mp(give.astype(bf16), k_at))
        mlp_mine = jnp.stack([total([view(t, mp=0) for t in chain[0]]) for chain in chains])
        one = [[opened(keep_one), opened(came_one)], list(ups)]
        came_two = swap_dp(send_two, 1)
        step([one])
        two = [[opened(keep_two), opened(came_two)], list(downs)]
        grad, gvec_one = entry((d_one, d_two), spans, w_all, x, part, vectors)
        arrays, grad, gvec_one = tie(newest([one, two]), grad, gvec_one)
        renew([one, two], arrays)
        step([two])
        while one[1]:
            step([one])
        input_grad = put_row(grad, rank, cotangent, 0, f32)
        arrays, input_grad, y = tie(newest([one, two]), input_grad, y)
        renew([one, two], arrays)
        while two[1]:
            step([two])
        block_output = put_row(y, rank, tokens, 0, bf16)
        arrays, block_output, grad = tie(newest([one, two]), block_output, grad)
        renew([one, two], arrays)
        attn_sent = []
        for k_at in range(1, mp):
            give = [
                total([view(t, mp=mp_at ^ k_at) for t in chain[0]]).astype(bf16)
                for chain in (one, two)
            ]
            attn_sent.append(swap_mp(jnp.concatenate(give, 1), k_at))
        attn_mine = jnp.concatenate(
            [total([view(t, mp=mp_at) for t in chain[0]]) for chain in (one, two)], 1
        )
        for row in range(1, rows):
            input_grad = put_row(grad, rank, cotangent, row, f32, input_grad)
        mlp_sent, input_grad = tie(mlp_sent, input_grad)
    else:
        d_all, attn_keep, _ = back(dctx, gwo, plan, 0, GROUPS)
        grad, gvec_one = entry((d_all,), ((0, GROUPS),), w_all, x, part, vectors)
        input_grad = put_row(grad, rank, cotangent, 0, f32)
        block_output = put_row(y, rank, tokens, 0, bf16)
        for row in range(1, rows):
            input_grad = put_row(grad, rank, cotangent, row, f32, input_grad)
        shaped = mlp_keep[:, 0].reshape(2, mp, dp, D // dp, FF // mp)
        shaped = jnp.take(shaped, mp_at ^ jnp.arange(mp), axis=1)
        shaped = shaped.transpose(2, 1, 0, 3, 4).reshape(world, 2, D // dp, FF // mp)
        mlp_mine = lax.psum_scatter(shaped, everyone, scatter_dimension=0, tiled=True)[0]
        mlp_mine = mlp_mine.astype(f32)
        attn_mine = lax.psum_scatter(attn_keep[0], everyone, scatter_dimension=0, tiled=True)
        attn_mine = attn_mine.astype(f32)
        mlp_sent, attn_sent = [], []

    *mlp_news, squares = mlp_lamb(
        (up_weight, up_first, up_second, down_weight.T, down_first.T, down_second.T),
        mlp_mine, mlp_sent,
    )
    *attn_news, load = attn_lamb(
        (qkv_weight, qkv_first, qkv_second, proj_weight, proj_first, proj_second),
        attn_mine, attn_sent, gvec_one, gvec_two, gbias, squares,
    )
    load, y = tie(load, y)
    came = swap_dp(load, 1) if fast else lax.psum(load, everyone)
    for row in range(1, rows):
        block_output = put_row(y, rank, tokens, row, bf16, block_output)
    came, block_output = tie(came, block_output)
    if fast:
        load = load + came
        bit = 2
        while bit < dp:
            load = load + swap_dp(load, bit)
            bit *= 2
        bit = 1
        while bit < mp:
            load = load + swap_mp(load, bit)
            bit *= 2
    else:
        load = came
    square = (FF // 128, 128)
    (
        weight_norms, qkv_new, proj_new, up_new, down_new,
        bias_new, bias_first_new, bias_second_new, *vector_news,
    ) = last(
        load,
        (qkv_weight, proj_weight, up_weight, down_weight.T),
        (attn_news[2], attn_news[5], mlp_news[2], mlp_news[5]),
        [value.reshape(square) for value in (up_bias, bias_first, bias_second)],
        (vectors, vector_first, vector_second),
    )
    return (
        block_output, input_grad, weight_norms,
        qkv_new, attn_news[0], attn_news[1],
        proj_new, attn_news[3], attn_news[4],
        up_new, mlp_news[0], mlp_news[1],
        down_new.T, mlp_news[3].T, mlp_news[4].T,
        bias_new.reshape(FF), bias_first_new.reshape(FF), bias_second_new.reshape(FF),
        *vector_news,
    )


def solution(mesh):
    dp, mp = mesh.shape["dp"], mesh.shape["mp"]
    split = Mesh(mesh.devices.reshape(dp // 2, 2, mp), ("dq", "dc", "mp"))
    rows = ("dq", "dc", "mp")
    by_rows = (P(rows, None),) * 3
    shared = (P(),) * 3
    up_spec = (P(("dq", "dc"), "mp"),) * 3
    down_spec = (P("mp", ("dq", "dc")),) * 3
    in_specs = (
        (P(rows, None, None), P(rows, None), P(rows, None), P(rows, None, None))
        + by_rows + by_rows + up_spec + down_spec + shared + shared
    )
    out_specs = (
        (P(rows, None, None), P(rows, None, None), P())
        + by_rows + by_rows + up_spec + down_spec + shared + shared
    )
    return jax.shard_map(
        partial(on_device, dp=dp, mp=mp),
        mesh=split, in_specs=in_specs, out_specs=out_specs, check_vma=False,
    )
```

```python
from functools import partial
import math

import jax
import jax.numpy as jnp
from jax import lax
from jax.experimental import pallas as pl
from jax.experimental.pallas import tpu as pltpu
from jax.sharding import Mesh, PartitionSpec as P

D = 768
FF = 3072
HEADS = 12
HEAD_DIM = 64
CAP = 640
SEQ = 1280
STEP = 10

eps_norm = 1e-06
eps_adam = 1e-06
beta_one = 0.9
beta_two = 0.999
decay_mat = 0.01
rate_lamb = 0.3
masked_score = -1e30

f32 = jnp.float32
bf16 = jnp.bfloat16
GROUP = 256
GROUPS = D // GROUP
LOG2E = 1.0 / math.log(2.0)
SCORE_SCALE = 1.0 / math.sqrt(HEAD_DIM)
ROUTER_SCALE = 1.0 / math.sqrt(D)


def dot_ab(left, right, left_dim=1, right_dim=0):
    return lax.dot_general(
        left, right, (((left_dim,), (right_dim,)), ((), ())), preferred_element_type=f32
    )


def params(mib, **more):
    return pltpu.CompilerParams(vmem_limit_bytes=mib << 20, **more)


def hbm(shape, dtype):
    return pltpu.HBM(shape, dtype)


def pinned(*arrays):
    return [
        pltpu.with_memory_space_constraint(array, pltpu.HBM) if array.size >= 1 << 17 else array
        for array in arrays
    ]


def cost(flops, nbytes, trans=0):
    return pl.CostEstimate(flops=int(flops), bytes_accessed=int(nbytes), transcendentals=int(trans))


def norm_parts(values):
    center = jnp.mean(values, -1, keepdims=True)
    offset = values - center
    spread = jnp.mean(offset * offset, -1, keepdims=True)
    inverse = lax.rsqrt(spread + eps_norm)
    return offset * inverse, inverse


def norm_back(grad, normalized, inverse, gain):
    scaled = grad * gain
    return inverse * (
        scaled
        - jnp.mean(scaled, -1, keepdims=True)
        - normalized * jnp.mean(scaled * normalized, -1, keepdims=True)
    )


def ranks_of(sel, ids):
    kind = jnp.where(ids < 0, 2, ids)
    sub = lax.broadcasted_iota(jnp.int32, (8, SEQ), 0)
    lane = lax.broadcasted_iota(jnp.int32, (8, SEQ), 1)
    member = jnp.where(jnp.broadcast_to(kind, (8, SEQ)) == sub, jnp.broadcast_to(sel, (8, SEQ)), 0)
    total = member
    step = 1
    while step < SEQ:
        total = total + jnp.where(lane >= step, pltpu.roll(total, step, 1), 0)
        step *= 2
    count = jnp.max(total, axis=1, keepdims=True)
    first = count[0:1]
    second = first + count[1:2]
    base = jnp.where(sub == 0, 0, jnp.where(sub == 1, first, second))
    rank = jnp.sum(member * (total + base), axis=0, keepdims=True) - 1
    return rank, first, second


def one_hot(rank):
    place = lax.broadcasted_iota(jnp.int32, (CAP, rank.shape[1]), 0)
    return jnp.where(place == rank, 1.0, 0.0).astype(bf16)


def pick_kernel(
    sel_ref, ids_ref, tok_ref, cot_ref, vec_ref,
    x_ref, dy_ref, a_ref, at_ref, dm_ref, rank_ref, bounds_ref, x_scr, dy_scr,
):
    rank, first, second = ranks_of(sel_ref[0], ids_ref[0])
    rank_ref[0] = jnp.broadcast_to(rank, (8, SEQ))
    lane = lax.broadcasted_iota(jnp.int32, (8, 128), 1)
    bounds_ref[0] = jnp.where(lane == 0, first, second)
    hot = one_hot(rank)
    x_scr[...] = dot_ab(hot, tok_ref[0])
    dy_scr[...] = dot_ab(hot, cot_ref[0])
    tile = 128

    def body(i, carry):
        rows = pl.ds(pl.multiple_of(i * tile, tile), tile)
        x = x_scr[rows, :]
        dy = dy_scr[rows, :]
        normalized, _ = norm_parts(x)
        low = (normalized * vec_ref[0:1, :] + vec_ref[1:2, :]).astype(bf16)
        gate = jax.nn.sigmoid(jnp.sum(x * vec_ref[4:5, :], -1, keepdims=True) * ROUTER_SCALE)
        x_ref[rows, :] = x.astype(bf16)
        dy_ref[rows, :] = dy.astype(bf16)
        a_ref[rows, :] = low
        dm_ref[rows, :] = (gate * dy).astype(bf16)
        return carry

    lax.fori_loop(0, CAP // tile, body, 0, unroll=True)
    at_ref[...] = a_ref[...].T


def pick_rows(sel, ids, tokens, cotangent, vectors):
    rows = tokens.shape[0]
    count = rows * CAP
    wide = pl.BlockSpec((CAP, D), lambda r: (r, 0))
    line = pl.BlockSpec((1, 1, SEQ), lambda r: (r, 0, 0))
    full = pl.BlockSpec((1, SEQ, D), lambda r: (r, 0, 0))
    return pl.pallas_call(
        pick_kernel,
        grid=(rows,),
        in_specs=[line, line, full, full, pl.BlockSpec((7, D), lambda r: (0, 0))],
        out_specs=[
            wide, wide, wide, pl.BlockSpec((D, CAP), lambda r: (0, r)), wide,
            pl.BlockSpec((1, 8, SEQ), lambda r: (r, 0, 0)),
            pl.BlockSpec((1, 8, 128), lambda r: (r, 0, 0)),
        ],
        out_shape=[
            hbm((count, D), bf16),
            hbm((count, D), bf16),
            hbm((count, D), bf16),
            hbm((D, count), bf16),
            hbm((count, D), bf16),
            hbm((rows, 8, SEQ), jnp.int32),
            hbm((rows, 8, 128), jnp.int32),
        ],
        scratch_shapes=[pltpu.VMEM((CAP, D), f32), pltpu.VMEM((CAP, D), f32)],
        compiler_params=params(40),
        cost_estimate=cost(4 * count * SEQ * D, 4 * rows * SEQ * D * 2),
        name="pick_rows",
    )(*pinned(sel[:, None, :], ids[:, None, :], tokens, cotangent, vectors))


def fill_bias(bias_scr, bounds_ref):
    first = bounds_ref[0, 0:1, 0:1]
    second = bounds_ref[0, 0:1, 1:2]
    tile = 128
    key = lax.broadcasted_iota(jnp.int32, (tile, CAP), 1)
    key_kind = jnp.where(key >= first, 1, 0) + jnp.where(key >= second, 1, 0)
    for i in range(CAP // tile):
        row = lax.broadcasted_iota(jnp.int32, (tile, CAP), 0) + i * tile
        row_kind = jnp.where(row >= first, 1, 0) + jnp.where(row >= second, 1, 0)
        bias_scr[i * tile : (i + 1) * tile, :] = jnp.where(row_kind == key_kind, 0.0, masked_score)


def half_masks():
    lane = lax.broadcasted_iota(jnp.int32, (1, 128), 1)
    low = jnp.where(lane < HEAD_DIM, 1.0, 0.0)
    return low, 1.0 - low


def attend_kernel(
    a_ref, w_ref, bounds_ref,
    q_ref, k_ref, v_ref, ctx_ref, probs_ref, bias_scr,
):
    @pl.when(pl.program_id(1) == 0)
    def _():
        fill_bias(bias_scr, bounds_ref)

    a = a_ref[...]
    for part, ref in enumerate((q_ref, k_ref, v_ref)):
        ref[...] = dot_ab(a, w_ref[:, part * GROUP : (part + 1) * GROUP]).astype(bf16)
    masks = half_masks()
    lane = lax.broadcasted_iota(jnp.int32, (1, 128), 1)
    for pair in range(GROUP // 128):
        cols = slice(pair * 128, pair * 128 + 128)
        queries, key_rows, values = q_ref[:, cols], k_ref[:, cols], v_ref[:, cols]
        halves = []
        for half in range(2):
            scores = dot_ab(queries * masks[half].astype(bf16), key_rows, 1, 1)
            scores = scores * (SCORE_SCALE * LOG2E) + bias_scr[...]
            row_max = jnp.max(scores, -1, keepdims=True)
            probs = jnp.exp2(scores - row_max)
            row_total = jnp.sum(probs, -1, keepdims=True)
            probs = (probs * (1.0 / row_total)).astype(bf16)
            probs_ref[0, pair * 2 + half] = probs
            halves.append(dot_ab(probs, values))
        ctx_ref[:, cols] = jnp.where(lane < HEAD_DIM, halves[0], halves[1]).astype(bf16)


def attend_forward(a, w_all, bounds):
    count = a.shape[0]
    rows = count // CAP
    piece = pl.BlockSpec((CAP, GROUP), lambda r, g: (r, g))
    narrow = hbm((count, D), bf16)
    return pl.pallas_call(
        attend_kernel,
        grid=(rows, GROUPS),
        in_specs=[
            pl.BlockSpec((CAP, D), lambda r, g: (r, 0)),
            pl.BlockSpec((D, 3 * GROUP), lambda r, g: (0, g)),
            pl.BlockSpec((1, 8, 128), lambda r, g: (r, 0, 0)),
        ],
        out_specs=[
            piece, piece, piece, piece,
            pl.BlockSpec((1, GROUP // HEAD_DIM, CAP, CAP), lambda r, g: (r, g, 0, 0)),
        ],
        out_shape=[narrow, narrow, narrow, narrow, hbm((rows, HEADS, CAP, CAP), bf16)],
        scratch_shapes=[pltpu.VMEM((CAP, CAP), f32)],
        compiler_params=params(48),
        cost_estimate=cost(
            2 * count * D * 3 * D + rows * HEADS * 16 * CAP * CAP * HEAD_DIM, 12 * count * D,
            rows * HEADS * CAP * CAP,
        ),
        name="attend_forward",
    )(*pinned(a, w_all, bounds))


def attend_back_kernel(
    me_ref, at_ref, q_ref, k_ref, v_ref, ctx_ref, dctx_ref, probs_ref, gwo_ref,
    d_ref, keep_ref, send_ref, held_scr, acc_scr, *, plan,
):
    row = pl.program_id(1)
    masks = half_masks()
    lane = lax.broadcasted_iota(jnp.int32, (1, 128), 1)
    for pair in range(GROUP // 128):
        cols = slice(pair * 128, pair * 128 + 128)
        queries, key_rows, values = q_ref[:, cols], k_ref[:, cols], v_ref[:, cols]
        grads = dctx_ref[:, cols]
        product = ctx_ref[:, cols].astype(f32) * grads.astype(f32)
        queries_t, grads_t = queries.T, grads.T
        dq, dk_t, dv_t = [], [], []
        for half in range(2):
            mask_low = masks[half].astype(bf16)
            span = slice(half * HEAD_DIM, half * HEAD_DIM + HEAD_DIM)
            probs = probs_ref[0, pair * 2 + half]
            delta = jnp.sum(product * masks[half], -1, keepdims=True)
            probs_grad = dot_ab(grads * mask_low, values, 1, 1)
            score_grad = (probs.astype(f32) * (probs_grad - delta)).astype(bf16)
            dq.append(dot_ab(score_grad, key_rows))
            dk_t.append(dot_ab(queries_t[span], score_grad))
            dv_t.append(dot_ab(grads_t[span], probs))
        place = pair * 128
        d_ref[:, place : place + 128] = (jnp.where(lane < HEAD_DIM, dq[0], dq[1]) * SCORE_SCALE).astype(bf16)
        place += GROUP
        d_ref[:, place : place + 128] = (jnp.concatenate(dk_t, 0) * SCORE_SCALE).astype(bf16).T
        place += GROUP
        d_ref[:, place : place + 128] = jnp.concatenate(dv_t, 0).astype(bf16).T
    held_scr[pl.ds(pl.multiple_of(row * CAP, CAP), CAP), :] = d_ref[...]

    @pl.when(row == pl.num_programs(1) - 1)
    def _():
        acc_scr[:, : 3 * GROUP] = dot_ab(at_ref[...], held_scr[...])
        acc_scr[:, 3 * GROUP :] = gwo_ref[...]
        split_blocks(me_ref, acc_scr, keep_ref, send_ref, plan)


def split_blocks(me_ref, acc_scr, keep_ref, send_ref, plan):
    if plan is None:
        keep_ref[0] = acc_scr[...].astype(bf16)
        send_ref[0] = jnp.zeros_like(send_ref[0])
        return
    blocks, core_bit = plan
    size = D // blocks
    on_high = (me_ref[0] & core_bit) != 0
    for block in range(blocks):
        if block & core_bit:
            continue
        low = acc_scr[block * size : (block + 1) * size, :]
        other = block | core_bit
        high = acc_scr[other * size : (other + 1) * size, :]
        slot = (block // (2 * core_bit)) * core_bit + block % core_bit
        keep_ref[slot] = jnp.where(on_high, high, low).astype(bf16)
        send_ref[slot] = jnp.where(on_high, low, high).astype(bf16)


def attend_backward(me, at, q, k, v, ctx, probs, dctx, gwo, plan, start, groups):
    count = q.shape[0]
    rows = count // CAP
    piece = pl.BlockSpec((CAP, GROUP), lambda g, r, me: (r, g + start))
    if plan is None:
        half, size, sent = 1, D, 8
    else:
        half, size = plan[0] // 2, D // plan[0]
        sent = size
    width = 4 * GROUP
    return pl.pallas_call(
        partial(attend_back_kernel, plan=plan),
        grid_spec=pltpu.PrefetchScalarGridSpec(
            num_scalar_prefetch=1,
            grid=(groups, rows),
            in_specs=[
                pl.BlockSpec((D, count), lambda g, r, me: (0, 0)),
                piece, piece, piece, piece, piece,
                pl.BlockSpec(
                    (1, GROUP // HEAD_DIM, CAP, CAP), lambda g, r, me: (r, g + start, 0, 0)
                ),
                pl.BlockSpec((D, GROUP), lambda g, r, me: (0, g + start)),
            ],
            out_specs=[
                pl.BlockSpec((CAP, 3 * GROUP), lambda g, r, me: (r, g)),
                pl.BlockSpec((half, size, width), lambda g, r, me: (0, 0, g)),
                pl.BlockSpec((half, sent, width), lambda g, r, me: (0, 0, g)),
            ],
            scratch_shapes=[
                pltpu.VMEM((count, 3 * GROUP), bf16), pltpu.VMEM((D, width), f32),
            ],
        ),
        out_shape=[
            hbm((count, groups * 3 * GROUP), bf16),
            hbm((half, size, groups * width), bf16),
            hbm((half, sent, groups * width), bf16),
        ],
        compiler_params=params(40),
        cost_estimate=cost(
            groups * GROUP * (6 * count * D + 40 * count * CAP),
            groups * GROUP * 20 * count,
            groups * (GROUP // HEAD_DIM) * count * CAP,
        ),
        name="attend_backward",
    )(me, *pinned(at, q, k, v, ctx, dctx, probs, gwo))


def middle_kernel(ctx_ref, wo_ref, x_ref, vec_ref, att_ref, c_ref):
    att = dot_ab(ctx_ref[...], wo_ref[...]) + vec_ref[5:6, :]
    att_ref[...] = att
    normalized, _ = norm_parts(x_ref[...].astype(f32) + att)
    c_ref[...] = (normalized * vec_ref[2:3, :] + vec_ref[3:4, :]).astype(bf16)


def middle(ctx, w_o, x, vectors):
    count = ctx.shape[0]
    tile = 320
    wide = pl.BlockSpec((tile, D), lambda t: (t, 0))
    return pl.pallas_call(
        middle_kernel,
        grid=(count // tile,),
        in_specs=[
            wide, pl.BlockSpec((D, D), lambda t: (0, 0)), wide,
            pl.BlockSpec((7, D), lambda t: (0, 0)),
        ],
        out_specs=[wide, wide],
        out_shape=[
            hbm((count, D), f32),
            hbm((count, D), bf16),
        ],
        compiler_params=params(32),
        cost_estimate=cost(2 * count * D * D, 10 * count * D),
        name="middle",
    )(*pinned(ctx, w_o, x, vectors))


ERF_P = 0.3275911 / math.sqrt(2.0)
ERF_COEF = (0.254829592, -0.284496736, 1.421413741, -1.453152027, 1.061405429)


def gelu_parts(u):
    bell = jnp.exp2(u * u * (-0.5 * LOG2E))
    t = 1.0 / (1.0 + ERF_P * jnp.abs(u))
    poly = ERF_COEF[4]
    for coef in ERF_COEF[3::-1]:
        poly = poly * t + coef
    tail = (0.5 * poly * t) * bell
    phi = jnp.where(u >= 0, 1.0 - tail, tail)
    return u * phi, phi + u * (bell * (1.0 / math.sqrt(2.0 * math.pi)))


def mlp_kernel(
    me_ref, c_ref, dm_ref, wu_ref, wd_ref, bias_ref,
    mlp_ref, dc_ref, keep_ref, send_ref, gbias_ref, ct_scr, dmt_scr, act_scr, du_scr,
    *, blocks, split,
):
    first = (pl.program_id(0) == 0) & (pl.program_id(1) == 0)

    @pl.when(first)
    def _():
        ct_scr[...] = c_ref[...].T
        dmt_scr[...] = dm_ref[...].T
        mlp_ref[...] = jnp.zeros_like(mlp_ref)
        dc_ref[...] = jnp.zeros_like(dc_ref)

    width = wu_ref.shape[-1]
    wu = wu_ref[...].reshape(D, width)
    wd = wd_ref[...].reshape(D, width)
    tile = CAP

    def body(i, total):
        rows = pl.ds(pl.multiple_of(i * tile, tile), tile)
        act, slope = gelu_parts(dot_ab(c_ref[rows, :], wu) + bias_ref[0])
        act = act.astype(bf16)
        du = (slope * dot_ab(dm_ref[rows, :], wd)).astype(bf16)
        act_scr[rows, :] = act
        du_scr[rows, :] = du
        mlp_ref[rows, :] += dot_ab(act, wd, 1, 1)
        dc_ref[rows, :] += dot_ab(du, wu, 1, 1)
        return total + jnp.sum(du.astype(f32), 0, keepdims=True)

    total = lax.fori_loop(0, c_ref.shape[0] // tile, body, jnp.zeros((1, width), f32))
    gbias_ref[0] = jnp.broadcast_to(total, (8, width))
    act, du = act_scr[...], du_scr[...]
    size = D // blocks
    for which, grad in enumerate((dot_ab(ct_scr[...], du), dot_ab(dmt_scr[...], act))):
        if not split:
            keep_ref[which, 0, 0] = grad.astype(bf16)
            continue
        on_high = (me_ref[2] & 1) != 0
        for block in range(0, blocks, 2):
            low = grad[block * size : (block + 1) * size]
            high = grad[(block + 1) * size : (block + 2) * size]
            slot = block // 2
            keep_ref[which, slot, 0] = jnp.where(on_high, high, low).astype(bf16)
            send_ref[which, slot, 0] = jnp.where(on_high, low, high).astype(bf16)
    if not split:
        send_ref[...] = jnp.zeros_like(send_ref)


def mlp_all(me, c, dm, weights, bias, split):
    count = c.shape[0]
    blocks, mp, _, units = weights.shape
    size = D // blocks
    width = 768
    subs = units // width
    half = blocks // 2 if split else 1
    sent = size if split else 8
    rows_out = size if split else D
    all_rows = pl.BlockSpec((count, D), lambda j, s, me: (0, 0))

    def weight_spec(which):
        return pl.BlockSpec(
            (blocks, 1, size, width), lambda j, s, me, which=which: (0, me[1] ^ j, which, s)
        )

    return pl.pallas_call(
        partial(mlp_kernel, blocks=blocks, split=split),
        grid_spec=pltpu.PrefetchScalarGridSpec(
            num_scalar_prefetch=1,
            grid=(mp, subs),
            in_specs=[
                all_rows, all_rows, weight_spec(0), weight_spec(1),
                pl.BlockSpec((1, 1, width), lambda j, s, me: ((me[1] ^ j) * subs + s, 0, 0)),
            ],
            out_specs=[
                all_rows, all_rows,
                pl.BlockSpec((2, half, 1, rows_out, width), lambda j, s, me: (0, 0, j, 0, s)),
                pl.BlockSpec((2, half, 1, sent, width), lambda j, s, me: (0, 0, j, 0, s)),
                pl.BlockSpec((1, 8, width), lambda j, s, me: (me[1] ^ j, 0, s)),
            ],
            scratch_shapes=[pltpu.VMEM((D, count), bf16)] * 2
            + [pltpu.VMEM((count, width), bf16)] * 2,
        ),
        out_shape=[
            hbm((count, D), f32),
            hbm((count, D), f32),
            hbm((2, half, mp, rows_out, units), bf16),
            hbm((2, half, mp, sent, units), bf16),
            hbm((mp, 8, units), f32),
        ],
        compiler_params=params(62),
        cost_estimate=cost(
            12 * count * D * mp * units, 12 * count * D + 8 * mp * units * D, 2 * count * mp * units
        ),
        name="mlp_all",
    )(me, *pinned(c, dm, weights, weights, bias.reshape(mp * subs, 1, width)))


def turn_kernel(
    x_ref, dy_ref, att_ref, mlp_ref, dc_ref, ctx_ref, wo_ref, vec_ref,
    y_ref, part_ref, dctx_ref, gwo_ref, gvec_ref, datt_scr,
):
    step = pl.program_id(0)

    @pl.when(step == 0)
    def _():
        gvec_ref[...] = jnp.zeros_like(gvec_ref)
        gwo_ref[...] = jnp.zeros_like(gwo_ref)

    tile = 64
    router = vec_ref[4:5, :]

    def body(i, carry):
        rows = pl.ds(pl.multiple_of(i * tile, tile), tile)
        x = x_ref[rows, :].astype(f32)
        dy = dy_ref[rows, :].astype(f32)
        att = att_ref[rows, :]
        branch = att + mlp_ref[rows, :] + vec_ref[6:7, :]
        gate = jax.nn.sigmoid(jnp.sum(x * router, -1, keepdims=True) * ROUTER_SCALE)
        y_ref[rows, :] = (x + gate * branch).astype(bf16)
        dr = jnp.sum(dy * branch, -1, keepdims=True) * gate * (1.0 - gate) * ROUTER_SCALE
        e = gate * dy
        normalized, inverse = norm_parts(x + att)
        dc = dc_ref[rows, :]
        dh = norm_back(dc, normalized, inverse, vec_ref[2:3, :])
        datt = (e + dh).astype(bf16)
        datt_scr[rows, :] = datt
        part_ref[rows, :] = dy + dr * router + dh
        for place, term in enumerate(
            (dc * normalized, dc, dr * x, datt.astype(f32), e.astype(bf16).astype(f32))
        ):
            gvec_ref[place : place + 1, :] += jnp.sum(term, 0, keepdims=True)
        return carry

    lax.fori_loop(0, x_ref.shape[0] // tile, body, 0, unroll=True)
    datt = datt_scr[...]
    dctx_ref[...] = dot_ab(datt, wo_ref[...], 1, 1).astype(bf16)
    gwo_ref[...] += dot_ab(ctx_ref[...], datt, 0, 0)


def turn(x, dy, att, mlp, dc, ctx, w_o, vectors):
    count = x.shape[0]
    tile = 320
    wide = pl.BlockSpec((tile, D), lambda t: (t, 0))
    return pl.pallas_call(
        turn_kernel,
        grid=(count // tile,),
        in_specs=[
            wide, wide, wide, wide, wide, wide, pl.BlockSpec((D, D), lambda t: (0, 0)),
            pl.BlockSpec((7, D), lambda t: (0, 0)),
        ],
        out_specs=[
            wide, wide, wide, pl.BlockSpec((D, D), lambda t: (0, 0)),
            pl.BlockSpec((8, D), lambda t: (0, 0)),
        ],
        out_shape=[
            hbm((count, D), bf16),
            hbm((count, D), f32),
            hbm((count, D), bf16),
            hbm((D, D), f32),
            hbm((8, D), f32),
        ],
        scratch_shapes=[pltpu.VMEM((tile, D), bf16)],
        compiler_params=params(48),
        cost_estimate=cost(4 * count * D * D, 26 * count * D),
        name="turn",
    )(*pinned(x, dy, att, mlp, dc, ctx, w_o, vectors))


def entry_kernel(
    *refs, spans,
):
    count = len(spans)
    grads = refs[:count]
    w_refs, refs = refs[count : count + GROUPS], refs[count + GROUPS :]
    x_ref, part_ref, vec_ref, out_ref, gvec_ref, da_scr = refs

    @pl.when(pl.program_id(0) == 0)
    def _():
        gvec_ref[...] = jnp.zeros_like(gvec_ref)

    da = None
    for ref, (start, groups) in zip(grads, spans):
        for at in range(groups):
            term = dot_ab(ref[:, at * D : (at + 1) * D], w_refs[start + at][...], 1, 1)
            da = term if da is None else da + term
    da_scr[...] = da
    tile = 64

    def body(i, carry):
        rows = pl.ds(pl.multiple_of(i * tile, tile), tile)
        normalized, inverse = norm_parts(x_ref[rows, :].astype(f32))
        da = da_scr[rows, :]
        for place, term in enumerate((da * normalized, da)):
            gvec_ref[place : place + 1, :] += jnp.sum(term, 0, keepdims=True)
        grad = part_ref[rows, :] + norm_back(da, normalized, inverse, vec_ref[0:1, :])
        high = grad.astype(bf16)
        out_ref[rows, 0:D] = high
        out_ref[rows, D:] = (grad - high.astype(f32)).astype(bf16)
        return carry

    lax.fori_loop(0, x_ref.shape[0] // tile, body, 0, unroll=True)


def entry(grads, spans, w_all, x, part, vectors):
    count = x.shape[0]
    tile = 320
    wide = pl.BlockSpec((tile, D), lambda r: (r, 0))
    return pl.pallas_call(
        partial(entry_kernel, spans=spans),
        grid=(count // tile,),
        in_specs=[pl.BlockSpec((tile, g.shape[1]), lambda r: (r, 0)) for g in grads]
        + [pl.BlockSpec((D, D), lambda r, group=group: (0, group)) for group in range(GROUPS)]
        + [
            wide, wide, pl.BlockSpec((7, D), lambda r: (0, 0)),
        ],
        out_specs=[
            pl.BlockSpec((tile, 2 * D), lambda r: (r, 0)),
            pl.BlockSpec((8, D), lambda r: (0, 0)),
        ],
        out_shape=[
            hbm((count, 2 * D), bf16),
            hbm((8, D), f32),
        ],
        scratch_shapes=[pltpu.VMEM((tile, D), f32)],
        compiler_params=params(32),
        cost_estimate=cost(2 * count * D * 3 * D, 24 * count * D),
        name="entry",
    )(*pinned(*grads, *[w_all] * GROUPS, x, part, vectors))


def put_kernel(value_ref, rank_ref, base_ref, *refs, parts):
    out_ref, ext_scr = refs[-2:]
    ext_scr[:, 0 : parts * D] = value_ref[...]
    ext_scr[:, parts * D :] = jnp.ones((CAP, 128), bf16)
    placed = dot_ab(one_hot(rank_ref[0, 0:1, :]), ext_scr[...], 0, 0)
    kept = 1.0 - placed[:, parts * D : parts * D + 1]
    result = placed[:, 0:D]
    for part in range(1, parts):
        result = result + placed[:, part * D : (part + 1) * D]
    out_ref[0] = (result + kept * base_ref[0].astype(f32)).astype(out_ref.dtype)


def put_row(value, rank, base, row, dtype, before=None):
    parts = value.shape[1] // D
    full = pl.BlockSpec((1, SEQ, D), lambda r: (row, 0, 0))
    held = [] if before is None else [before]
    return pl.pallas_call(
        partial(put_kernel, parts=parts),
        grid=(1,),
        in_specs=[
            pl.BlockSpec((CAP, parts * D), lambda r: (row, 0)),
            pl.BlockSpec((1, 8, SEQ), lambda r: (row, 0, 0)),
            full,
        ]
        + [pl.BlockSpec(memory_space=pl.ANY)] * len(held),
        out_specs=full,
        out_shape=hbm(base.shape, dtype),
        input_output_aliases={3: 0} if held else {},
        scratch_shapes=[pltpu.VMEM((CAP, parts * D + 128), bf16)],
        compiler_params=params(48),
        cost_estimate=cost(2 * parts * CAP * SEQ * D, 5 * parts * CAP * D),
        name=f"put_row_{parts}",
    )(*pinned(value, rank, base), *held)


def lamb_moments(weight, gradient, first_mom, second_mom, decay):
    first_new = beta_one * first_mom + (1.0 - beta_one) * gradient
    second_new = beta_two * second_mom + (1.0 - beta_two) * gradient * gradient
    update = (
        first_new
        / (1.0 - beta_one**STEP)
        / (jnp.sqrt(second_new / (1.0 - beta_two**STEP)) + eps_adam)
        + decay * weight
    )
    return (first_new, second_new, update)


def square_sum(value):
    return jnp.sum(jnp.sum(value * value, 1, keepdims=True), 0, keepdims=True)


def added(mine_ref, got_refs, place):
    result = mine_ref[place]
    for ref in got_refs:
        result = result + ref[place].astype(f32)
    return result


def lanes_of(pairs):
    lane = lax.broadcasted_iota(jnp.int32, (8, 128), 1)
    result = jnp.zeros((8, 128), f32)
    for place, value in pairs:
        result = result + jnp.where(lane == place, value, 0.0)
    return result


def mlp_lamb_kernel(*refs, gots):
    weights, (mine_ref, *rest) = refs[:6], refs[6:]
    got_refs, outs = rest[:gots], rest[gots:]
    pairs = []
    for which in range(2):
        weight_ref, first_ref, second_ref = weights[3 * which : 3 * which + 3]
        grad = added(mine_ref, got_refs, which)
        weight = weight_ref[...]
        news = lamb_moments(weight, grad, first_ref[...], second_ref[...], decay_mat)
        for ref, value in zip(outs[3 * which : 3 * which + 3], news):
            ref[...] = value
        pairs += [(2 + which, square_sum(weight)), (6 + which, square_sum(news[2]))]
    outs[6][...] = lanes_of(pairs)


def mlp_lamb(moments, mine, gots):
    like = jax.ShapeDtypeStruct(moments[0].shape, f32)
    return pl.pallas_call(
        partial(mlp_lamb_kernel, gots=len(gots)),
        out_shape=[like] * 6 + [jax.ShapeDtypeStruct((8, 128), f32)],
        compiler_params=params(24),
        cost_estimate=cost(40 * mine.size, 40 * mine.size),
        name="mlp_lamb",
    )(*moments, mine, *gots)


def attn_lamb_kernel(*refs, gots):
    moments, (mine_ref, *rest) = refs[:6], refs[6:]
    got_refs, rest = rest[:gots], rest[gots:]
    one_ref, two_ref, bias_ref, sq_ref, *outs = rest
    sums = [jnp.zeros((1, 1), f32) for _ in range(4)]
    for part in range(4):
        tensor = part // 3
        weight_ref, first_ref, second_ref = moments[3 * tensor : 3 * tensor + 3]
        for group in range(GROUPS):
            left = (group * 4 + part) * GROUP
            grad = added(mine_ref, got_refs, (slice(None), slice(left, left + GROUP)))
            left = (part % 3) * D + group * GROUP
            cols = (slice(None), slice(left, left + GROUP))
            weight = weight_ref[cols]
            news = lamb_moments(weight, grad, first_ref[cols], second_ref[cols], decay_mat)
            for ref, value in zip(outs[3 * tensor : 3 * tensor + 3], news):
                ref[cols] = value
            sums[tensor] += square_sum(weight)
            sums[2 + tensor] += square_sum(news[2])
    load_ref = outs[6]
    load_ref[...] = jnp.zeros_like(load_ref)
    load_ref[0:2, :] = one_ref[0:2, :]
    load_ref[2:7, :] = two_ref[0:5, :]
    for i in range(FF // D):
        load_ref[7 + i : 8 + i, :] = bias_ref[i, 0:1, :]
    squares = sq_ref[...] + lanes_of(list(zip((0, 1, 4, 5), sums)))
    load_ref[LOAD_SQ : LOAD_SQ + 1, 0:128] = squares[0:1]


LOAD_SQ = 7 + FF // D
LOAD_ROWS = 16


def attn_lamb(moments, mine, gots, gvec_one, gvec_two, gbias, squares):
    qkv_like = jax.ShapeDtypeStruct(moments[0].shape, f32)
    proj_like = jax.ShapeDtypeStruct(moments[3].shape, f32)
    return pl.pallas_call(
        partial(attn_lamb_kernel, gots=len(gots)),
        out_shape=[qkv_like] * 3 + [proj_like] * 3
        + [jax.ShapeDtypeStruct((LOAD_ROWS, D), f32)],
        compiler_params=params(24),
        cost_estimate=cost(40 * mine.size, 40 * mine.size),
        name="attn_lamb",
    )(*moments, mine, *gots, gvec_one, gvec_two, gbias, squares)


def last_kernel(
    load_ref, qkv_ref, proj_ref, up_ref, down_ref, qkv_upd, proj_upd, up_upd, down_upd,
    bias_ref, bias_one, bias_two, vec_ref, vec_one, vec_two,
    norms_ref, qkv_new, proj_new, up_new, down_new,
    bias_new, bias_first, bias_second, vec_new, vec_first, vec_second, bias_scr,
):
    norms = jnp.sqrt(load_ref[LOAD_SQ : LOAD_SQ + 1, 0:128])
    norms_ref[0:1, :] = norms[:, 0:4]
    norms_ref[1:2, :] = norms[:, 4:8]
    for i, (weight, upd, new) in enumerate(
        (
            (qkv_ref, qkv_upd, qkv_new), (proj_ref, proj_upd, proj_new),
            (up_ref, up_upd, up_new), (down_ref, down_upd, down_new),
        )
    ):
        ratio = norms[:, i : i + 1] / norms[:, 4 + i : 5 + i]
        new[...] = weight[...] - rate_lamb * ratio * upd[...]
    for i in range(FF // 128):
        row, left = 7 + i // (D // 128), i % (D // 128) * 128
        bias_scr[i : i + 1, :] = load_ref[row : row + 1, left : left + 128]
    bias = bias_ref[...]
    first, second, upd = lamb_moments(bias, bias_scr[...], bias_one[...], bias_two[...], 0.0)
    bias_first[...] = first
    bias_second[...] = second
    bias_new[...] = bias - rate_lamb * (
        jnp.sqrt(square_sum(bias)) / jnp.sqrt(square_sum(upd))
    ) * upd
    vec = vec_ref[...]
    first, second, upd = lamb_moments(vec, load_ref[0:7, :], vec_one[...], vec_two[...], 0.0)
    vec_first[...] = first
    vec_second[...] = second
    ratio = jnp.sqrt(jnp.sum(vec * vec, -1, keepdims=True)) / jnp.sqrt(
        jnp.sum(upd * upd, -1, keepdims=True)
    )
    vec_new[...] = vec - rate_lamb * ratio * upd


def last(load, weights, upds, bias, vecs):
    def like(value):
        return jax.ShapeDtypeStruct(value.shape, f32)

    return pl.pallas_call(
        last_kernel,
        out_shape=[jax.ShapeDtypeStruct((2, 4), f32)] + [like(w) for w in weights]
        + [like(b) for b in bias] + [like(v) for v in vecs],
        scratch_shapes=[pltpu.VMEM((FF // 128, 128), f32)],
        compiler_params=params(24),
        cost_estimate=cost(1 << 20, 4 << 20),
        name="last",
    )(load, *weights, *upds, *bias, *vecs)


def swap(value, axis, size, bit):
    return lax.ppermute(value, axis, [(i, i ^ bit) for i in range(size)])


def on_device(
    tokens, image_ids, selected, cotangent,
    qkv_weight, qkv_first, qkv_second, proj_weight, proj_first, proj_second,
    up_weight, up_first, up_second, down_weight, down_first, down_second,
    up_bias, bias_first, bias_second, vectors, vector_first, vector_second,
    *, dp, mp,
):
    world = dp * mp
    rows = tokens.shape[0]
    dq_at, dc_at, mp_at = (lax.axis_index(name) for name in ("dq", "dc", "mp"))
    dp_at = dq_at * 2 + dc_at
    me = jnp.stack([dp_at * mp + mp_at, mp_at, dp_at]).astype(jnp.int32)
    everyone = ("dq", "dc", "mp")
    fast = (D // world) % 8 == 0 and dp >= 4 and (D // dp) % 16 == 0

    def swap_dp(value, bit):
        if bit == 1:
            return swap(value, "dc", 2, 1)
        return swap(value, "dq", dp // 2, bit // 2)

    def swap_mp(value, bit):
        return swap(value, "mp", mp, bit)

    bits = []
    bit = 2
    while bit < dp:
        bits.append(bit)
        bit *= 2
    ups, downs = tuple(bits), tuple(reversed(bits))

    def tie(*values):
        return lax.optimization_barrier(values)

    def total(terms):
        result = terms[0].astype(f32)
        for term in terms[1:]:
            result = result + term.astype(f32)
        return result

    def merge(held, came, high, axis):
        return jnp.where(high, jnp.stack([came, held], axis), jnp.stack([held, came], axis))

    size = D // world
    low_qkv = qkv_weight.astype(bf16).reshape(size, 3, GROUPS, GROUP).transpose(0, 2, 1, 3)
    low_qkv = low_qkv.reshape(size, 3 * D)
    proj_low = proj_weight.astype(bf16)
    mlp_low = jnp.concatenate([up_weight.astype(bf16), down_weight.astype(bf16).T], 0)
    picked = pick_rows(selected, image_ids, tokens, cotangent, vectors)
    mlp_mat = lax.all_gather(mlp_low, everyone, axis=0, tiled=True)
    mlp_mat = mlp_mat.reshape(dp, mp, 2 * (D // dp), FF // mp)

    def grown(value, bit, done):
        axis = sum(other > bit for other in done)
        done.append(bit)
        return merge(value, swap_dp(value, bit), (dp_at & bit) != 0, axis)

    low_all = jnp.concatenate([low_qkv, proj_low], 1)
    if fast:
        held = [low_all] + [swap_mp(low_all, k) for k in range(1, mp)]
        held, picked = tie(held, picked)
        held = jnp.stack(held).reshape((2,) * (mp.bit_length() - 1) + (size, 4 * D))
        for axis in range(mp.bit_length() - 1):
            flip = ((mp_at >> (mp.bit_length() - 2 - axis)) & 1) != 0
            held = jnp.where(flip, jnp.flip(held, axis), held)
        held = held.reshape(mp, size, 4 * D)
        halves = [held[:, :, half * 2 * D : (half + 1) * 2 * D] for half in range(2)]
        for half, order in enumerate((ups, downs)):
            done = []
            for bit in order + (1,):
                halves[half] = grown(halves[half], bit, done)
        halves = [value.reshape(D, 2 * D) for value in halves]
        w_all = jnp.concatenate([halves[0], halves[1][:, :D]], 1)
        w_o = halves[1][:, D:]
    else:
        w_all = lax.all_gather(low_all, everyone, axis=0, tiled=True)
        w_all, w_o = w_all[:, : 3 * D], w_all[:, 3 * D :]
        mlp_mat = mlp_mat.reshape(dp, mp, 2, D // dp, FF // mp).transpose(1, 2, 0, 3, 4)
        mlp_mat = mlp_mat.reshape(1, mp, 2 * D, FF // mp)

    def view(term, **more):
        array, names, fixed = term
        fixed = {**fixed, **more}
        start = [fixed.get(name, 0) for name in names] + [0, 0]
        extent = [1 if name in fixed else n for name, n in zip(names, array.shape)]
        kept = [n for name, n in zip(names, array.shape) if name not in fixed]
        out = lax.dynamic_slice(array, start, tuple(extent) + array.shape[-2:])
        return out.reshape(tuple(kept) + array.shape[-2:])

    def name_of(bit):
        return f"b{bit}"

    def opened(array, which=None):
        names = [name_of(bit) for bit in reversed(bits)] + ["mp"]
        fixed = {}
        shape = (2,) * len(bits) + (mp,) + array.shape[-2:]
        if which is not None:
            names, shape, fixed = ["which"] + names, (2,) + shape, {"which": which}
        return (array.reshape(shape), names, fixed)

    def step(chains):
        for chain in chains:
            terms, order = chain
            bit = order.pop(0)
            name, mine = name_of(bit), (dp_at // bit) & 1
            give = total([view(term, **{name: 1 - mine}) for term in terms]).astype(bf16)
            left = [n for n in terms[0][1] if n not in terms[0][2] and n != name]
            chain[0] = [(t[0], t[1], {**t[2], name: mine}) for t in terms]
            chain[0].append((swap_dp(give, bit), left, {}))

    def newest(chains):
        return [chain[0][-1][0] for chain in chains]

    def renew(chains, arrays):
        for chain, array in zip(chains, arrays):
            chain[0][-1] = (array,) + chain[0][-1][1:]

    x, dy, a, at, dm, rank, bounds = picked
    q, k, v, ctx, probs = attend_forward(a, w_all, bounds)
    att, c = middle(ctx, w_o, x, vectors)
    mlp, dc, mlp_keep, mlp_send, gbias = mlp_all(me, c, dm, mlp_mat, up_bias, fast)
    plan = (world, mp) if fast else None
    spans = ((0, GROUPS - 1), (GROUPS - 1, 1))
    back = partial(attend_backward, me, at, q, k, v, ctx, probs)
    if fast:
        mlp_came = swap_dp(mlp_send, 1)
    y, part, dctx, gwo, gvec_two = turn(x, dy, att, mlp, dc, ctx, w_o, vectors)
    if fast:
        mlp_came, dctx = tie(mlp_came, dctx)
        chains = [
            [[opened(mlp_keep, which), opened(mlp_came, which)], list(order)]
            for which, order in enumerate((ups, downs))
        ]
        step(chains)
        d_one, keep_one, send_one = back(dctx, gwo, plan, *spans[0])
        arrays, d_one, send_one, dctx = tie(newest(chains), d_one, send_one, dctx)
        renew(chains, arrays)
        while chains[0][1]:
            step(chains)
        came_one = swap_dp(send_one, 1)
        d_two, keep_two, send_two = back(dctx, gwo, plan, *spans[1])
        arrays, came_one, send_two, d_two, y = tie(newest(chains), came_one, send_two, d_two, y)
        renew(chains, arrays)
        mlp_sent = []
        for k_at in range(1, mp):
            give = jnp.stack([total([view(t, mp=k_at) for t in chain[0]]) for chain in chains])
            mlp_sent.append(swap_mp(give.astype(bf16), k_at))
        mlp_mine = jnp.stack([total([view(t, mp=0) for t in chain[0]]) for chain in chains])
        one = [[opened(keep_one), opened(came_one)], list(ups)]
        came_two = swap_dp(send_two, 1)
        step([one])
        two = [[opened(keep_two), opened(came_two)], list(downs)]
        grad, gvec_one = entry((d_one, d_two), spans, w_all, x, part, vectors)
        arrays, grad, gvec_one = tie(newest([one, two]), grad, gvec_one)
        renew([one, two], arrays)
        step([two])
        while one[1]:
            step([one])
        input_grad = put_row(grad, rank, cotangent, 0, f32)
        arrays, input_grad, y = tie(newest([one, two]), input_grad, y)
        renew([one, two], arrays)
        while two[1]:
            step([two])
        block_output = put_row(y, rank, tokens, 0, bf16)
        arrays, block_output, grad = tie(newest([one, two]), block_output, grad)
        renew([one, two], arrays)
        attn_sent = []
        for k_at in range(1, mp):
            give = [
                total([view(t, mp=mp_at ^ k_at) for t in chain[0]]).astype(bf16)
                for chain in (one, two)
            ]
            attn_sent.append(swap_mp(jnp.concatenate(give, 1), k_at))
        attn_mine = jnp.concatenate(
            [total([view(t, mp=mp_at) for t in chain[0]]) for chain in (one, two)], 1
        )
        for row in range(1, rows):
            input_grad = put_row(grad, rank, cotangent, row, f32, input_grad)
        mlp_sent, input_grad = tie(mlp_sent, input_grad)
    else:
        d_all, attn_keep, _ = back(dctx, gwo, plan, 0, GROUPS)
        grad, gvec_one = entry((d_all,), ((0, GROUPS),), w_all, x, part, vectors)
        input_grad = put_row(grad, rank, cotangent, 0, f32)
        block_output = put_row(y, rank, tokens, 0, bf16)
        for row in range(1, rows):
            input_grad = put_row(grad, rank, cotangent, row, f32, input_grad)
        shaped = mlp_keep[:, 0].reshape(2, mp, dp, D // dp, FF // mp)
        shaped = jnp.take(shaped, mp_at ^ jnp.arange(mp), axis=1)
        shaped = shaped.transpose(2, 1, 0, 3, 4).reshape(world, 2, D // dp, FF // mp)
        mlp_mine = lax.psum_scatter(shaped, everyone, scatter_dimension=0, tiled=True)[0]
        mlp_mine = mlp_mine.astype(f32)
        attn_mine = lax.psum_scatter(attn_keep[0], everyone, scatter_dimension=0, tiled=True)
        attn_mine = attn_mine.astype(f32)
        mlp_sent, attn_sent = [], []

    *mlp_news, squares = mlp_lamb(
        (up_weight, up_first, up_second, down_weight.T, down_first.T, down_second.T),
        mlp_mine, mlp_sent,
    )
    *attn_news, load = attn_lamb(
        (qkv_weight, qkv_first, qkv_second, proj_weight, proj_first, proj_second),
        attn_mine, attn_sent, gvec_one, gvec_two, gbias, squares,
    )
    load, y = tie(load, y)
    came = swap_dp(load, 1) if fast else lax.psum(load, everyone)
    for row in range(1, rows):
        block_output = put_row(y, rank, tokens, row, bf16, block_output)
    came, block_output = tie(came, block_output)
    if fast:
        load = load + came
        bit = 2
        while bit < dp:
            load = load + swap_dp(load, bit)
            bit *= 2
        bit = 1
        while bit < mp:
            load = load + swap_mp(load, bit)
            bit *= 2
    else:
        load = came
    square = (FF // 128, 128)
    (
        weight_norms, qkv_new, proj_new, up_new, down_new,
        bias_new, bias_first_new, bias_second_new, *vector_news,
    ) = last(
        load,
        (qkv_weight, proj_weight, up_weight, down_weight.T),
        (attn_news[2], attn_news[5], mlp_news[2], mlp_news[5]),
        [value.reshape(square) for value in (up_bias, bias_first, bias_second)],
        (vectors, vector_first, vector_second),
    )
    return (
        block_output, input_grad, weight_norms,
        qkv_new, attn_news[0], attn_news[1],
        proj_new, attn_news[3], attn_news[4],
        up_new, mlp_news[0], mlp_news[1],
        down_new.T, mlp_news[3].T, mlp_news[4].T,
        bias_new.reshape(FF), bias_first_new.reshape(FF), bias_second_new.reshape(FF),
        *vector_news,
    )


def solution(mesh):
    dp, mp = mesh.shape["dp"], mesh.shape["mp"]
    split = Mesh(mesh.devices.reshape(dp // 2, 2, mp), ("dq", "dc", "mp"))
    rows = ("dq", "dc", "mp")
    by_rows = (P(rows, None),) * 3
    shared = (P(),) * 3
    up_spec = (P(("dq", "dc"), "mp"),) * 3
    down_spec = (P("mp", ("dq", "dc")),) * 3
    in_specs = (
        (P(rows, None, None), P(rows, None), P(rows, None), P(rows, None, None))
        + by_rows + by_rows + up_spec + down_spec + shared + shared
    )
    out_specs = (
        (P(rows, None, None), P(rows, None, None), P())
        + by_rows + by_rows + up_spec + down_spec + shared + shared
    )
    return jax.shard_map(
        partial(on_device, dp=dp, mp=mp),
        mesh=split, in_specs=in_specs, out_specs=out_specs, check_vma=False,
    )
```

```python
from functools import partial
import math

import jax
import jax.numpy as jnp
from jax import lax
from jax.experimental import pallas as pl
from jax.experimental.pallas import tpu as pltpu
from jax.sharding import Mesh, PartitionSpec as P

D = 768
FF = 3072
HEADS = 12
HEAD_DIM = 64
CAP = 640
SEQ = 1280
STEP = 10

eps_norm = 1e-06
eps_adam = 1e-06
beta_one = 0.9
beta_two = 0.999
decay_mat = 0.01
rate_lamb = 0.3
masked_score = -1e30

f32 = jnp.float32
bf16 = jnp.bfloat16
GROUP = 256
GROUPS = D // GROUP
LOG2E = 1.0 / math.log(2.0)
SCORE_SCALE = 1.0 / math.sqrt(HEAD_DIM)
ROUTER_SCALE = 1.0 / math.sqrt(D)


def dot_ab(left, right, left_dim=1, right_dim=0):
    return lax.dot_general(
        left, right, (((left_dim,), (right_dim,)), ((), ())), preferred_element_type=f32
    )


def params(mib, **more):
    return pltpu.CompilerParams(vmem_limit_bytes=mib << 20, **more)


def hbm(shape, dtype):
    return pltpu.HBM(shape, dtype)


def pinned(*arrays):
    return [
        pltpu.with_memory_space_constraint(array, pltpu.HBM) if array.size >= 1 << 17 else array
        for array in arrays
    ]


def cost(flops, nbytes, trans=0):
    return pl.CostEstimate(flops=int(flops), bytes_accessed=int(nbytes), transcendentals=int(trans))


def norm_parts(values):
    center = jnp.mean(values, -1, keepdims=True)
    offset = values - center
    spread = jnp.mean(offset * offset, -1, keepdims=True)
    inverse = lax.rsqrt(spread + eps_norm)
    return offset * inverse, inverse


def norm_back(grad, normalized, inverse, gain):
    scaled = grad * gain
    return inverse * (
        scaled
        - jnp.mean(scaled, -1, keepdims=True)
        - normalized * jnp.mean(scaled * normalized, -1, keepdims=True)
    )


def ranks_of(sel, ids):
    kind = jnp.where(ids < 0, 2, ids)
    sub = lax.broadcasted_iota(jnp.int32, (8, SEQ), 0)
    lane = lax.broadcasted_iota(jnp.int32, (8, SEQ), 1)
    member = jnp.where(jnp.broadcast_to(kind, (8, SEQ)) == sub, jnp.broadcast_to(sel, (8, SEQ)), 0)
    total = member
    step = 1
    while step < SEQ:
        total = total + jnp.where(lane >= step, pltpu.roll(total, step, 1), 0)
        step *= 2
    count = jnp.max(total, axis=1, keepdims=True)
    first = count[0:1]
    second = first + count[1:2]
    base = jnp.where(sub == 0, 0, jnp.where(sub == 1, first, second))
    rank = jnp.sum(member * (total + base), axis=0, keepdims=True) - 1
    return rank, first, second


def one_hot(rank):
    place = lax.broadcasted_iota(jnp.int32, (CAP, rank.shape[1]), 0)
    return jnp.where(place == rank, 1.0, 0.0).astype(bf16)


def pick_kernel(
    sel_ref, ids_ref, tok_ref, cot_ref, vec_ref,
    x_ref, dy_ref, a_ref, at_ref, dm_ref, rank_ref, bounds_ref, x_scr, dy_scr,
):
    rank, first, second = ranks_of(sel_ref[0], ids_ref[0])
    rank_ref[0] = jnp.broadcast_to(rank, (8, SEQ))
    lane = lax.broadcasted_iota(jnp.int32, (8, 128), 1)
    bounds_ref[0] = jnp.where(lane == 0, first, second)
    hot = one_hot(rank)
    x_scr[...] = dot_ab(hot, tok_ref[0])
    dy_scr[...] = dot_ab(hot, cot_ref[0])
    tile = 128

    def body(i, carry):
        rows = pl.ds(pl.multiple_of(i * tile, tile), tile)
        x = x_scr[rows, :]
        dy = dy_scr[rows, :]
        normalized, _ = norm_parts(x)
        low = (normalized * vec_ref[0:1, :] + vec_ref[1:2, :]).astype(bf16)
        gate = jax.nn.sigmoid(jnp.sum(x * vec_ref[4:5, :], -1, keepdims=True) * ROUTER_SCALE)
        x_ref[rows, :] = x.astype(bf16)
        dy_ref[rows, :] = dy.astype(bf16)
        a_ref[rows, :] = low
        dm_ref[rows, :] = (gate * dy).astype(bf16)
        return carry

    lax.fori_loop(0, CAP // tile, body, 0, unroll=True)
    at_ref[...] = a_ref[...].T


def pick_rows(sel, ids, tokens, cotangent, vectors):
    rows = tokens.shape[0]
    count = rows * CAP
    wide = pl.BlockSpec((CAP, D), lambda r: (r, 0))
    line = pl.BlockSpec((1, 1, SEQ), lambda r: (r, 0, 0))
    full = pl.BlockSpec((1, SEQ, D), lambda r: (r, 0, 0))
    return pl.pallas_call(
        pick_kernel,
        grid=(rows,),
        in_specs=[line, line, full, full, pl.BlockSpec((7, D), lambda r: (0, 0))],
        out_specs=[
            wide, wide, wide, pl.BlockSpec((D, CAP), lambda r: (0, r)), wide,
            pl.BlockSpec((1, 8, SEQ), lambda r: (r, 0, 0)),
            pl.BlockSpec((1, 8, 128), lambda r: (r, 0, 0)),
        ],
        out_shape=[
            hbm((count, D), bf16),
            hbm((count, D), bf16),
            hbm((count, D), bf16),
            hbm((D, count), bf16),
            hbm((count, D), bf16),
            hbm((rows, 8, SEQ), jnp.int32),
            hbm((rows, 8, 128), jnp.int32),
        ],
        scratch_shapes=[pltpu.VMEM((CAP, D), f32), pltpu.VMEM((CAP, D), f32)],
        compiler_params=params(40),
        cost_estimate=cost(4 * count * SEQ * D, 4 * rows * SEQ * D * 2),
        name="pick_rows",
    )(*pinned(sel[:, None, :], ids[:, None, :], tokens, cotangent, vectors))


def fill_bias(bias_scr, bounds_ref):
    first = bounds_ref[0, 0:1, 0:1]
    second = bounds_ref[0, 0:1, 1:2]
    tile = 128
    key = lax.broadcasted_iota(jnp.int32, (tile, CAP), 1)
    key_kind = jnp.where(key >= first, 1, 0) + jnp.where(key >= second, 1, 0)
    for i in range(CAP // tile):
        row = lax.broadcasted_iota(jnp.int32, (tile, CAP), 0) + i * tile
        row_kind = jnp.where(row >= first, 1, 0) + jnp.where(row >= second, 1, 0)
        bias_scr[i * tile : (i + 1) * tile, :] = jnp.where(row_kind == key_kind, 0.0, masked_score)


def half_masks():
    lane = lax.broadcasted_iota(jnp.int32, (1, 128), 1)
    low = jnp.where(lane < HEAD_DIM, 1.0, 0.0)
    return low, 1.0 - low


def attend_kernel(
    a_ref, w_ref, bounds_ref,
    q_ref, k_ref, v_ref, ctx_ref, probs_ref, bias_scr,
):
    @pl.when(pl.program_id(1) == 0)
    def _():
        fill_bias(bias_scr, bounds_ref)

    a = a_ref[...]
    for part, ref in enumerate((q_ref, k_ref, v_ref)):
        ref[...] = dot_ab(a, w_ref[:, part * GROUP : (part + 1) * GROUP]).astype(bf16)
    masks = half_masks()
    lane = lax.broadcasted_iota(jnp.int32, (1, 128), 1)
    for pair in range(GROUP // 128):
        cols = slice(pair * 128, pair * 128 + 128)
        queries, key_rows, values = q_ref[:, cols], k_ref[:, cols], v_ref[:, cols]
        halves = []
        for half in range(2):
            scores = dot_ab(queries * masks[half].astype(bf16), key_rows, 1, 1)
            scores = scores * (SCORE_SCALE * LOG2E) + bias_scr[...]
            row_max = jnp.max(scores, -1, keepdims=True)
            probs = jnp.exp2(scores - row_max)
            row_total = jnp.sum(probs, -1, keepdims=True)
            probs = (probs * (1.0 / row_total)).astype(bf16)
            probs_ref[0, pair * 2 + half] = probs
            halves.append(dot_ab(probs, values))
        ctx_ref[:, cols] = jnp.where(lane < HEAD_DIM, halves[0], halves[1]).astype(bf16)


def attend_forward(a, w_all, bounds):
    count = a.shape[0]
    rows = count // CAP
    piece = pl.BlockSpec((CAP, GROUP), lambda r, g: (r, g))
    narrow = hbm((count, D), bf16)
    return pl.pallas_call(
        attend_kernel,
        grid=(rows, GROUPS),
        in_specs=[
            pl.BlockSpec((CAP, D), lambda r, g: (r, 0)),
            pl.BlockSpec((D, 3 * GROUP), lambda r, g: (0, g)),
            pl.BlockSpec((1, 8, 128), lambda r, g: (r, 0, 0)),
        ],
        out_specs=[
            piece, piece, piece, piece,
            pl.BlockSpec((1, GROUP // HEAD_DIM, CAP, CAP), lambda r, g: (r, g, 0, 0)),
        ],
        out_shape=[narrow, narrow, narrow, narrow, hbm((rows, HEADS, CAP, CAP), bf16)],
        scratch_shapes=[pltpu.VMEM((CAP, CAP), f32)],
        compiler_params=params(48),
        cost_estimate=cost(
            2 * count * D * 3 * D + rows * HEADS * 16 * CAP * CAP * HEAD_DIM, 12 * count * D,
            rows * HEADS * CAP * CAP,
        ),
        name="attend_forward",
    )(*pinned(a, w_all, bounds))


def attend_back_kernel(
    me_ref, at_ref, q_ref, k_ref, v_ref, ctx_ref, dctx_ref, probs_ref, gwo_ref,
    d_ref, keep_ref, send_ref, held_scr, acc_scr, *, plan,
):
    row = pl.program_id(1)
    masks = half_masks()
    lane = lax.broadcasted_iota(jnp.int32, (1, 128), 1)
    for pair in range(GROUP // 128):
        cols = slice(pair * 128, pair * 128 + 128)
        queries, key_rows, values = q_ref[:, cols], k_ref[:, cols], v_ref[:, cols]
        grads = dctx_ref[:, cols]
        product = ctx_ref[:, cols].astype(f32) * grads.astype(f32)
        queries_t, grads_t = queries.T, grads.T
        dq, dk_t, dv_t = [], [], []
        for half in range(2):
            mask_low = masks[half].astype(bf16)
            span = slice(half * HEAD_DIM, half * HEAD_DIM + HEAD_DIM)
            probs = probs_ref[0, pair * 2 + half]
            delta = jnp.sum(product * masks[half], -1, keepdims=True)
            probs_grad = dot_ab(grads * mask_low, values, 1, 1)
            score_grad = (probs.astype(f32) * (probs_grad - delta)).astype(bf16)
            dq.append(dot_ab(score_grad, key_rows))
            dk_t.append(dot_ab(queries_t[span], score_grad))
            dv_t.append(dot_ab(grads_t[span], probs))
        place = pair * 128
        d_ref[:, place : place + 128] = (jnp.where(lane < HEAD_DIM, dq[0], dq[1]) * SCORE_SCALE).astype(bf16)
        place += GROUP
        d_ref[:, place : place + 128] = (jnp.concatenate(dk_t, 0) * SCORE_SCALE).astype(bf16).T
        place += GROUP
        d_ref[:, place : place + 128] = jnp.concatenate(dv_t, 0).astype(bf16).T
    held_scr[pl.ds(pl.multiple_of(row * CAP, CAP), CAP), :] = d_ref[...]

    @pl.when(row == pl.num_programs(1) - 1)
    def _():
        acc_scr[:, : 3 * GROUP] = dot_ab(at_ref[...], held_scr[...])
        acc_scr[:, 3 * GROUP :] = gwo_ref[...]
        split_blocks(me_ref, acc_scr, keep_ref, send_ref, plan)


def split_blocks(me_ref, acc_scr, keep_ref, send_ref, plan):
    if plan is None:
        keep_ref[0] = acc_scr[...].astype(bf16)
        send_ref[0] = jnp.zeros_like(send_ref[0])
        return
    blocks, core_bit = plan
    size = D // blocks
    on_high = (me_ref[0] & core_bit) != 0
    for block in range(blocks):
        if block & core_bit:
            continue
        low = acc_scr[block * size : (block + 1) * size, :]
        other = block | core_bit
        high = acc_scr[other * size : (other + 1) * size, :]
        slot = (block // (2 * core_bit)) * core_bit + block % core_bit
        keep_ref[slot] = jnp.where(on_high, high, low).astype(bf16)
        send_ref[slot] = jnp.where(on_high, low, high).astype(bf16)


def attend_backward(me, at, q, k, v, ctx, probs, dctx, gwo, plan, start, groups):
    count = q.shape[0]
    rows = count // CAP
    piece = pl.BlockSpec((CAP, GROUP), lambda g, r, me: (r, g + start))
    if plan is None:
        half, size, sent = 1, D, 8
    else:
        half, size = plan[0] // 2, D // plan[0]
        sent = size
    width = 4 * GROUP
    return pl.pallas_call(
        partial(attend_back_kernel, plan=plan),
        grid_spec=pltpu.PrefetchScalarGridSpec(
            num_scalar_prefetch=1,
            grid=(groups, rows),
            in_specs=[
                pl.BlockSpec((D, count), lambda g, r, me: (0, 0)),
                piece, piece, piece, piece, piece,
                pl.BlockSpec(
                    (1, GROUP // HEAD_DIM, CAP, CAP), lambda g, r, me: (r, g + start, 0, 0)
                ),
                pl.BlockSpec((D, GROUP), lambda g, r, me: (0, g + start)),
            ],
            out_specs=[
                pl.BlockSpec((CAP, 3 * GROUP), lambda g, r, me: (r, g)),
                pl.BlockSpec((half, size, width), lambda g, r, me: (0, 0, g)),
                pl.BlockSpec((half, sent, width), lambda g, r, me: (0, 0, g)),
            ],
            scratch_shapes=[
                pltpu.VMEM((count, 3 * GROUP), bf16), pltpu.VMEM((D, width), f32),
            ],
        ),
        out_shape=[
            hbm((count, groups * 3 * GROUP), bf16),
            hbm((half, size, groups * width), bf16),
            hbm((half, sent, groups * width), bf16),
        ],
        compiler_params=params(40),
        cost_estimate=cost(
            groups * GROUP * (6 * count * D + 40 * count * CAP),
            groups * GROUP * 20 * count,
            groups * (GROUP // HEAD_DIM) * count * CAP,
        ),
        name="attend_backward",
    )(me, *pinned(at, q, k, v, ctx, dctx, probs, gwo))


def middle_kernel(ctx_ref, wo_ref, x_ref, vec_ref, att_ref, c_ref):
    att = dot_ab(ctx_ref[...], wo_ref[...]) + vec_ref[5:6, :]
    att_ref[...] = att
    normalized, _ = norm_parts(x_ref[...].astype(f32) + att)
    c_ref[...] = (normalized * vec_ref[2:3, :] + vec_ref[3:4, :]).astype(bf16)


def middle(ctx, w_o, x, vectors):
    count = ctx.shape[0]
    tile = 640
    wide = pl.BlockSpec((tile, D), lambda t: (t, 0))
    return pl.pallas_call(
        middle_kernel,
        grid=(count // tile,),
        in_specs=[
            wide, pl.BlockSpec((D, D), lambda t: (0, 0)), wide,
            pl.BlockSpec((7, D), lambda t: (0, 0)),
        ],
        out_specs=[wide, wide],
        out_shape=[
            hbm((count, D), f32),
            hbm((count, D), bf16),
        ],
        compiler_params=params(60),
        cost_estimate=cost(2 * count * D * D, 10 * count * D),
        name="middle",
    )(*pinned(ctx, w_o, x, vectors))


ERF_P = 0.3275911 / math.sqrt(2.0)
ERF_COEF = (0.254829592, -0.284496736, 1.421413741, -1.453152027, 1.061405429)


def gelu_parts(u):
    bell = jnp.exp2(u * u * (-0.5 * LOG2E))
    t = 1.0 / (1.0 + ERF_P * jnp.abs(u))
    poly = ERF_COEF[4]
    for coef in ERF_COEF[3::-1]:
        poly = poly * t + coef
    tail = (0.5 * poly * t) * bell
    phi = jnp.where(u >= 0, 1.0 - tail, tail)
    return u * phi, phi + u * (bell * (1.0 / math.sqrt(2.0 * math.pi)))


def mlp_kernel(
    me_ref, c_ref, dm_ref, wu_ref, wd_ref, bias_ref,
    mlp_ref, dc_ref, keep_ref, send_ref, gbias_ref, ct_scr, dmt_scr, act_scr, du_scr,
    *, blocks, split,
):
    first = (pl.program_id(0) == 0) & (pl.program_id(1) == 0)

    @pl.when(first)
    def _():
        ct_scr[...] = c_ref[...].T
        dmt_scr[...] = dm_ref[...].T
        mlp_ref[...] = jnp.zeros_like(mlp_ref)
        dc_ref[...] = jnp.zeros_like(dc_ref)

    width = wu_ref.shape[-1]
    wu = wu_ref[...].reshape(D, width)
    wd = wd_ref[...].reshape(D, width)
    tile = CAP

    def body(i, total):
        rows = pl.ds(pl.multiple_of(i * tile, tile), tile)
        act, slope = gelu_parts(dot_ab(c_ref[rows, :], wu) + bias_ref[0])
        act = act.astype(bf16)
        du = (slope * dot_ab(dm_ref[rows, :], wd)).astype(bf16)
        act_scr[rows, :] = act
        du_scr[rows, :] = du
        mlp_ref[rows, :] += dot_ab(act, wd, 1, 1)
        dc_ref[rows, :] += dot_ab(du, wu, 1, 1)
        return total + jnp.sum(du.astype(f32), 0, keepdims=True)

    total = lax.fori_loop(0, c_ref.shape[0] // tile, body, jnp.zeros((1, width), f32))
    gbias_ref[0] = jnp.broadcast_to(total, (8, width))
    act, du = act_scr[...], du_scr[...]
    size = D // blocks
    for which, grad in enumerate((dot_ab(ct_scr[...], du), dot_ab(dmt_scr[...], act))):
        if not split:
            keep_ref[which, 0, 0] = grad.astype(bf16)
            continue
        on_high = (me_ref[2] & 1) != 0
        for block in range(0, blocks, 2):
            low = grad[block * size : (block + 1) * size]
            high = grad[(block + 1) * size : (block + 2) * size]
            slot = block // 2
            keep_ref[which, slot, 0] = jnp.where(on_high, high, low).astype(bf16)
            send_ref[which, slot, 0] = jnp.where(on_high, low, high).astype(bf16)
    if not split:
        send_ref[...] = jnp.zeros_like(send_ref)


def mlp_all(me, c, dm, weights, bias, split):
    count = c.shape[0]
    blocks, mp, _, units = weights.shape
    size = D // blocks
    width = 768
    subs = units // width
    half = blocks // 2 if split else 1
    sent = size if split else 8
    rows_out = size if split else D
    all_rows = pl.BlockSpec((count, D), lambda j, s, me: (0, 0))

    def weight_spec(which):
        return pl.BlockSpec(
            (blocks, 1, size, width), lambda j, s, me, which=which: (0, me[1] ^ j, which, s)
        )

    return pl.pallas_call(
        partial(mlp_kernel, blocks=blocks, split=split),
        grid_spec=pltpu.PrefetchScalarGridSpec(
            num_scalar_prefetch=1,
            grid=(mp, subs),
            in_specs=[
                all_rows, all_rows, weight_spec(0), weight_spec(1),
                pl.BlockSpec((1, 1, width), lambda j, s, me: ((me[1] ^ j) * subs + s, 0, 0)),
            ],
            out_specs=[
                all_rows, all_rows,
                pl.BlockSpec((2, half, 1, rows_out, width), lambda j, s, me: (0, 0, j, 0, s)),
                pl.BlockSpec((2, half, 1, sent, width), lambda j, s, me: (0, 0, j, 0, s)),
                pl.BlockSpec((1, 8, width), lambda j, s, me: (me[1] ^ j, 0, s)),
            ],
            scratch_shapes=[pltpu.VMEM((D, count), bf16)] * 2
            + [pltpu.VMEM((count, width), bf16)] * 2,
        ),
        out_shape=[
            hbm((count, D), f32),
            hbm((count, D), f32),
            hbm((2, half, mp, rows_out, units), bf16),
            hbm((2, half, mp, sent, units), bf16),
            hbm((mp, 8, units), f32),
        ],
        compiler_params=params(62),
        cost_estimate=cost(
            12 * count * D * mp * units, 12 * count * D + 8 * mp * units * D, 2 * count * mp * units
        ),
        name="mlp_all",
    )(me, *pinned(c, dm, weights, weights, bias.reshape(mp * subs, 1, width)))


def turn_kernel(
    x_ref, dy_ref, att_ref, mlp_ref, dc_ref, ctx_ref, wo_ref, vec_ref,
    y_ref, part_ref, dctx_ref, gwo_ref, gvec_ref, datt_scr,
):
    step = pl.program_id(0)

    @pl.when(step == 0)
    def _():
        gvec_ref[...] = jnp.zeros_like(gvec_ref)
        gwo_ref[...] = jnp.zeros_like(gwo_ref)

    tile = 64
    router = vec_ref[4:5, :]

    def body(i, carry):
        rows = pl.ds(pl.multiple_of(i * tile, tile), tile)
        x = x_ref[rows, :].astype(f32)
        dy = dy_ref[rows, :].astype(f32)
        att = att_ref[rows, :]
        branch = att + mlp_ref[rows, :] + vec_ref[6:7, :]
        gate = jax.nn.sigmoid(jnp.sum(x * router, -1, keepdims=True) * ROUTER_SCALE)
        y_ref[rows, :] = (x + gate * branch).astype(bf16)
        dr = jnp.sum(dy * branch, -1, keepdims=True) * gate * (1.0 - gate) * ROUTER_SCALE
        e = gate * dy
        normalized, inverse = norm_parts(x + att)
        dc = dc_ref[rows, :]
        dh = norm_back(dc, normalized, inverse, vec_ref[2:3, :])
        datt = (e + dh).astype(bf16)
        datt_scr[rows, :] = datt
        part_ref[rows, :] = dy + dr * router + dh
        for place, term in enumerate(
            (dc * normalized, dc, dr * x, datt.astype(f32), e.astype(bf16).astype(f32))
        ):
            gvec_ref[place : place + 1, :] += jnp.sum(term, 0, keepdims=True)
        return carry

    lax.fori_loop(0, x_ref.shape[0] // tile, body, 0, unroll=True)
    datt = datt_scr[...]
    dctx_ref[...] = dot_ab(datt, wo_ref[...], 1, 1).astype(bf16)
    gwo_ref[...] += dot_ab(ctx_ref[...], datt, 0, 0)


def turn(x, dy, att, mlp, dc, ctx, w_o, vectors):
    count = x.shape[0]
    tile = 320
    wide = pl.BlockSpec((tile, D), lambda t: (t, 0))
    return pl.pallas_call(
        turn_kernel,
        grid=(count // tile,),
        in_specs=[
            wide, wide, wide, wide, wide, wide, pl.BlockSpec((D, D), lambda t: (0, 0)),
            pl.BlockSpec((7, D), lambda t: (0, 0)),
        ],
        out_specs=[
            wide, wide, wide, pl.BlockSpec((D, D), lambda t: (0, 0)),
            pl.BlockSpec((8, D), lambda t: (0, 0)),
        ],
        out_shape=[
            hbm((count, D), bf16),
            hbm((count, D), f32),
            hbm((count, D), bf16),
            hbm((D, D), f32),
            hbm((8, D), f32),
        ],
        scratch_shapes=[pltpu.VMEM((tile, D), bf16)],
        compiler_params=params(48),
        cost_estimate=cost(4 * count * D * D, 26 * count * D),
        name="turn",
    )(*pinned(x, dy, att, mlp, dc, ctx, w_o, vectors))


def entry_kernel(
    *refs, spans,
):
    count = len(spans)
    grads = refs[:count]
    w_refs, refs = refs[count : count + GROUPS], refs[count + GROUPS :]
    x_ref, part_ref, vec_ref, out_ref, gvec_ref, da_scr = refs

    @pl.when(pl.program_id(0) == 0)
    def _():
        gvec_ref[...] = jnp.zeros_like(gvec_ref)

    da = None
    for ref, (start, groups) in zip(grads, spans):
        for at in range(groups):
            term = dot_ab(ref[:, at * D : (at + 1) * D], w_refs[start + at][...], 1, 1)
            da = term if da is None else da + term
    da_scr[...] = da
    tile = 64

    def body(i, carry):
        rows = pl.ds(pl.multiple_of(i * tile, tile), tile)
        normalized, inverse = norm_parts(x_ref[rows, :].astype(f32))
        da = da_scr[rows, :]
        for place, term in enumerate((da * normalized, da)):
            gvec_ref[place : place + 1, :] += jnp.sum(term, 0, keepdims=True)
        grad = part_ref[rows, :] + norm_back(da, normalized, inverse, vec_ref[0:1, :])
        out_ref[rows, :] = grad.astype(bf16)
        return carry

    lax.fori_loop(0, x_ref.shape[0] // tile, body, 0, unroll=True)


def entry(grads, spans, w_all, x, part, vectors):
    count = x.shape[0]
    tile = 320
    wide = pl.BlockSpec((tile, D), lambda r: (r, 0))
    return pl.pallas_call(
        partial(entry_kernel, spans=spans),
        grid=(count // tile,),
        in_specs=[pl.BlockSpec((tile, g.shape[1]), lambda r: (r, 0)) for g in grads]
        + [pl.BlockSpec((D, D), lambda r, group=group: (0, group)) for group in range(GROUPS)]
        + [
            wide, wide, pl.BlockSpec((7, D), lambda r: (0, 0)),
        ],
        out_specs=[
            wide,
            pl.BlockSpec((8, D), lambda r: (0, 0)),
        ],
        out_shape=[
            hbm((count, D), bf16),
            hbm((8, D), f32),
        ],
        scratch_shapes=[pltpu.VMEM((tile, D), f32)],
        compiler_params=params(32),
        cost_estimate=cost(2 * count * D * 3 * D, 24 * count * D),
        name="entry",
    )(*pinned(*grads, *[w_all] * GROUPS, x, part, vectors))


def put_kernel(value_ref, rank_ref, base_ref, *refs):
    out_ref, ext_scr = refs[-2:]
    ext_scr[:, 0:D] = value_ref[...]
    ext_scr[:, D:] = jnp.ones((CAP, 128), bf16)
    placed = dot_ab(one_hot(rank_ref[0, 0:1, :]), ext_scr[...], 0, 0)
    kept = 1.0 - placed[:, D : D + 1]
    out_ref[0] = (placed[:, 0:D] + kept * base_ref[0].astype(f32)).astype(out_ref.dtype)


def put_row(value, rank, base, row, dtype, before=None):
    full = pl.BlockSpec((1, SEQ, D), lambda r: (row, 0, 0))
    held = [] if before is None else [before]
    return pl.pallas_call(
        put_kernel,
        grid=(1,),
        in_specs=[
            pl.BlockSpec((CAP, D), lambda r: (row, 0)),
            pl.BlockSpec((1, 8, SEQ), lambda r: (row, 0, 0)),
            full,
        ]
        + [pl.BlockSpec(memory_space=pl.ANY)] * len(held),
        out_specs=full,
        out_shape=hbm(base.shape, dtype),
        input_output_aliases={3: 0} if held else {},
        scratch_shapes=[pltpu.VMEM((CAP, D + 128), bf16)],
        compiler_params=params(48),
        cost_estimate=cost(2 * CAP * SEQ * D, 5 * CAP * D),
        name="put_row",
    )(*pinned(value, rank, base), *held)


def lamb_moments(weight, gradient, first_mom, second_mom, decay):
    first_new = beta_one * first_mom + (1.0 - beta_one) * gradient
    second_new = beta_two * second_mom + (1.0 - beta_two) * gradient * gradient
    update = (
        first_new
        / (1.0 - beta_one**STEP)
        / (jnp.sqrt(second_new / (1.0 - beta_two**STEP)) + eps_adam)
        + decay * weight
    )
    return (first_new, second_new, update)


def square_sum(value):
    return jnp.sum(jnp.sum(value * value, 1, keepdims=True), 0, keepdims=True)


def added(mine_ref, got_refs, place):
    result = mine_ref[place]
    for ref in got_refs:
        result = result + ref[place].astype(f32)
    return result


def lanes_of(pairs):
    lane = lax.broadcasted_iota(jnp.int32, (8, 128), 1)
    result = jnp.zeros((8, 128), f32)
    for place, value in pairs:
        result = result + jnp.where(lane == place, value, 0.0)
    return result


def mlp_lamb_kernel(*refs, gots):
    weights, (mine_ref, *rest) = refs[:6], refs[6:]
    got_refs, outs = rest[:gots], rest[gots:]
    pairs = []
    for which in range(2):
        weight_ref, first_ref, second_ref = weights[3 * which : 3 * which + 3]
        grad = added(mine_ref, got_refs, which)
        weight = weight_ref[...]
        news = lamb_moments(weight, grad, first_ref[...], second_ref[...], decay_mat)
        for ref, value in zip(outs[3 * which : 3 * which + 3], news):
            ref[...] = value
        pairs += [(2 + which, square_sum(weight)), (6 + which, square_sum(news[2]))]
    outs[6][...] = lanes_of(pairs)


def mlp_lamb(moments, mine, gots):
    like = jax.ShapeDtypeStruct(moments[0].shape, f32)
    return pl.pallas_call(
        partial(mlp_lamb_kernel, gots=len(gots)),
        out_shape=[like] * 6 + [jax.ShapeDtypeStruct((8, 128), f32)],
        compiler_params=params(24),
        cost_estimate=cost(40 * mine.size, 40 * mine.size),
        name="mlp_lamb",
    )(*moments, mine, *gots)


def attn_lamb_kernel(*refs, gots):
    moments, (mine_ref, *rest) = refs[:6], refs[6:]
    got_refs, rest = rest[:gots], rest[gots:]
    one_ref, two_ref, bias_ref, sq_ref, *outs = rest
    sums = [jnp.zeros((1, 1), f32) for _ in range(4)]
    for part in range(4):
        tensor = part // 3
        weight_ref, first_ref, second_ref = moments[3 * tensor : 3 * tensor + 3]
        for group in range(GROUPS):
            left = (group * 4 + part) * GROUP
            grad = added(mine_ref, got_refs, (slice(None), slice(left, left + GROUP)))
            left = (part % 3) * D + group * GROUP
            cols = (slice(None), slice(left, left + GROUP))
            weight = weight_ref[cols]
            news = lamb_moments(weight, grad, first_ref[cols], second_ref[cols], decay_mat)
            for ref, value in zip(outs[3 * tensor : 3 * tensor + 3], news):
                ref[cols] = value
            sums[tensor] += square_sum(weight)
            sums[2 + tensor] += square_sum(news[2])
    load_ref = outs[6]
    load_ref[...] = jnp.zeros_like(load_ref)
    load_ref[0:2, :] = one_ref[0:2, :]
    load_ref[2:7, :] = two_ref[0:5, :]
    for i in range(FF // D):
        load_ref[7 + i : 8 + i, :] = bias_ref[i, 0:1, :]
    squares = sq_ref[...] + lanes_of(list(zip((0, 1, 4, 5), sums)))
    load_ref[LOAD_SQ : LOAD_SQ + 1, 0:128] = squares[0:1]


LOAD_SQ = 7 + FF // D
LOAD_ROWS = 16


def attn_lamb(moments, mine, gots, gvec_one, gvec_two, gbias, squares):
    qkv_like = jax.ShapeDtypeStruct(moments[0].shape, f32)
    proj_like = jax.ShapeDtypeStruct(moments[3].shape, f32)
    return pl.pallas_call(
        partial(attn_lamb_kernel, gots=len(gots)),
        out_shape=[qkv_like] * 3 + [proj_like] * 3
        + [jax.ShapeDtypeStruct((LOAD_ROWS, D), f32)],
        compiler_params=params(24),
        cost_estimate=cost(40 * mine.size, 40 * mine.size),
        name="attn_lamb",
    )(*moments, mine, *gots, gvec_one, gvec_two, gbias, squares)


def last_kernel(
    load_ref, qkv_ref, proj_ref, up_ref, down_ref, qkv_upd, proj_upd, up_upd, down_upd,
    bias_ref, bias_one, bias_two, vec_ref, vec_one, vec_two,
    norms_ref, qkv_new, proj_new, up_new, down_new,
    bias_new, bias_first, bias_second, vec_new, vec_first, vec_second, bias_scr,
):
    norms = jnp.sqrt(load_ref[LOAD_SQ : LOAD_SQ + 1, 0:128])
    norms_ref[0:1, :] = norms[:, 0:4]
    norms_ref[1:2, :] = norms[:, 4:8]
    for i, (weight, upd, new) in enumerate(
        (
            (qkv_ref, qkv_upd, qkv_new), (proj_ref, proj_upd, proj_new),
            (up_ref, up_upd, up_new), (down_ref, down_upd, down_new),
        )
    ):
        ratio = norms[:, i : i + 1] / norms[:, 4 + i : 5 + i]
        new[...] = weight[...] - rate_lamb * ratio * upd[...]
    for i in range(FF // 128):
        row, left = 7 + i // (D // 128), i % (D // 128) * 128
        bias_scr[i : i + 1, :] = load_ref[row : row + 1, left : left + 128]
    bias = bias_ref[...]
    first, second, upd = lamb_moments(bias, bias_scr[...], bias_one[...], bias_two[...], 0.0)
    bias_first[...] = first
    bias_second[...] = second
    bias_new[...] = bias - rate_lamb * (
        jnp.sqrt(square_sum(bias)) / jnp.sqrt(square_sum(upd))
    ) * upd
    vec = vec_ref[...]
    first, second, upd = lamb_moments(vec, load_ref[0:7, :], vec_one[...], vec_two[...], 0.0)
    vec_first[...] = first
    vec_second[...] = second
    ratio = jnp.sqrt(jnp.sum(vec * vec, -1, keepdims=True)) / jnp.sqrt(
        jnp.sum(upd * upd, -1, keepdims=True)
    )
    vec_new[...] = vec - rate_lamb * ratio * upd


def last(load, weights, upds, bias, vecs):
    def like(value):
        return jax.ShapeDtypeStruct(value.shape, f32)

    return pl.pallas_call(
        last_kernel,
        out_shape=[jax.ShapeDtypeStruct((2, 4), f32)] + [like(w) for w in weights]
        + [like(b) for b in bias] + [like(v) for v in vecs],
        scratch_shapes=[pltpu.VMEM((FF // 128, 128), f32)],
        compiler_params=params(24),
        cost_estimate=cost(1 << 20, 4 << 20),
        name="last",
    )(load, *weights, *upds, *bias, *vecs)


def swap(value, axis, size, bit):
    return lax.ppermute(value, axis, [(i, i ^ bit) for i in range(size)])


def on_device(
    tokens, image_ids, selected, cotangent,
    qkv_weight, qkv_first, qkv_second, proj_weight, proj_first, proj_second,
    up_weight, up_first, up_second, down_weight, down_first, down_second,
    up_bias, bias_first, bias_second, vectors, vector_first, vector_second,
    *, dp, mp,
):
    world = dp * mp
    rows = tokens.shape[0]
    dq_at, dc_at, mp_at = (lax.axis_index(name) for name in ("dq", "dc", "mp"))
    dp_at = dq_at * 2 + dc_at
    me = jnp.stack([dp_at * mp + mp_at, mp_at, dp_at]).astype(jnp.int32)
    everyone = ("dq", "dc", "mp")
    fast = (D // world) % 8 == 0 and dp >= 4 and (D // dp) % 16 == 0

    def swap_dp(value, bit):
        if bit == 1:
            return swap(value, "dc", 2, 1)
        return swap(value, "dq", dp // 2, bit // 2)

    def swap_mp(value, bit):
        return swap(value, "mp", mp, bit)

    bits = []
    bit = 2
    while bit < dp:
        bits.append(bit)
        bit *= 2
    ups, downs = tuple(bits), tuple(reversed(bits))

    def tie(*values):
        return lax.optimization_barrier(values)

    def total(terms):
        result = terms[0].astype(f32)
        for term in terms[1:]:
            result = result + term.astype(f32)
        return result

    def merge(held, came, high, axis):
        return jnp.where(high, jnp.stack([came, held], axis), jnp.stack([held, came], axis))

    size = D // world
    low_qkv = qkv_weight.astype(bf16).reshape(size, 3, GROUPS, GROUP).transpose(0, 2, 1, 3)
    low_qkv = low_qkv.reshape(size, 3 * D)
    proj_low = proj_weight.astype(bf16)
    mlp_low = jnp.concatenate([up_weight.astype(bf16), down_weight.astype(bf16).T], 0)
    picked = pick_rows(selected, image_ids, tokens, cotangent, vectors)
    mlp_mat = lax.all_gather(mlp_low, everyone, axis=0, tiled=True)
    mlp_mat = mlp_mat.reshape(dp, mp, 2 * (D // dp), FF // mp)

    def grown(value, bit, done):
        axis = sum(other > bit for other in done)
        done.append(bit)
        return merge(value, swap_dp(value, bit), (dp_at & bit) != 0, axis)

    low_all = jnp.concatenate([low_qkv, proj_low], 1)
    if fast:
        held = [low_all] + [swap_mp(low_all, k) for k in range(1, mp)]
        held, picked = tie(held, picked)
        held = jnp.stack(held).reshape((2,) * (mp.bit_length() - 1) + (size, 4 * D))
        for axis in range(mp.bit_length() - 1):
            flip = ((mp_at >> (mp.bit_length() - 2 - axis)) & 1) != 0
            held = jnp.where(flip, jnp.flip(held, axis), held)
        held = held.reshape(mp, size, 4 * D)
        halves = [held[:, :, half * 2 * D : (half + 1) * 2 * D] for half in range(2)]
        for half, order in enumerate((ups, downs)):
            done = []
            for bit in order + (1,):
                halves[half] = grown(halves[half], bit, done)
        halves = [value.reshape(D, 2 * D) for value in halves]
        w_all = jnp.concatenate([halves[0], halves[1][:, :D]], 1)
        w_o = halves[1][:, D:]
    else:
        w_all = lax.all_gather(low_all, everyone, axis=0, tiled=True)
        w_all, w_o = w_all[:, : 3 * D], w_all[:, 3 * D :]
        mlp_mat = mlp_mat.reshape(dp, mp, 2, D // dp, FF // mp).transpose(1, 2, 0, 3, 4)
        mlp_mat = mlp_mat.reshape(1, mp, 2 * D, FF // mp)

    def view(term, **more):
        array, names, fixed = term
        fixed = {**fixed, **more}
        start = [fixed.get(name, 0) for name in names] + [0, 0]
        extent = [1 if name in fixed else n for name, n in zip(names, array.shape)]
        kept = [n for name, n in zip(names, array.shape) if name not in fixed]
        out = lax.dynamic_slice(array, start, tuple(extent) + array.shape[-2:])
        return out.reshape(tuple(kept) + array.shape[-2:])

    def name_of(bit):
        return f"b{bit}"

    def opened(array, which=None):
        names = [name_of(bit) for bit in reversed(bits)] + ["mp"]
        fixed = {}
        shape = (2,) * len(bits) + (mp,) + array.shape[-2:]
        if which is not None:
            names, shape, fixed = ["which"] + names, (2,) + shape, {"which": which}
        return (array.reshape(shape), names, fixed)

    def step(chains):
        for chain in chains:
            terms, order = chain
            bit = order.pop(0)
            name, mine = name_of(bit), (dp_at // bit) & 1
            give = total([view(term, **{name: 1 - mine}) for term in terms]).astype(bf16)
            left = [n for n in terms[0][1] if n not in terms[0][2] and n != name]
            chain[0] = [(t[0], t[1], {**t[2], name: mine}) for t in terms]
            chain[0].append((swap_dp(give, bit), left, {}))

    def newest(chains):
        return [chain[0][-1][0] for chain in chains]

    def renew(chains, arrays):
        for chain, array in zip(chains, arrays):
            chain[0][-1] = (array,) + chain[0][-1][1:]

    x, dy, a, at, dm, rank, bounds = picked
    q, k, v, ctx, probs = attend_forward(a, w_all, bounds)
    att, c = middle(ctx, w_o, x, vectors)
    mlp, dc, mlp_keep, mlp_send, gbias = mlp_all(me, c, dm, mlp_mat, up_bias, fast)
    plan = (world, mp) if fast else None
    spans = ((0, GROUPS - 1), (GROUPS - 1, 1))
    back = partial(attend_backward, me, at, q, k, v, ctx, probs)
    if fast:
        mlp_came = swap_dp(mlp_send, 1)
    y, part, dctx, gwo, gvec_two = turn(x, dy, att, mlp, dc, ctx, w_o, vectors)
    if fast:
        mlp_came, dctx = tie(mlp_came, dctx)
        chains = [
            [[opened(mlp_keep, which), opened(mlp_came, which)], list(order)]
            for which, order in enumerate((ups, downs))
        ]
        step(chains)
        d_one, keep_one, send_one = back(dctx, gwo, plan, *spans[0])
        arrays, d_one, send_one, dctx = tie(newest(chains), d_one, send_one, dctx)
        renew(chains, arrays)
        while chains[0][1]:
            step(chains)
        came_one = swap_dp(send_one, 1)
        d_two, keep_two, send_two = back(dctx, gwo, plan, *spans[1])
        arrays, came_one, send_two, d_two, y = tie(newest(chains), came_one, send_two, d_two, y)
        renew(chains, arrays)
        mlp_sent = []
        for k_at in range(1, mp):
            give = jnp.stack([total([view(t, mp=k_at) for t in chain[0]]) for chain in chains])
            mlp_sent.append(swap_mp(give.astype(bf16), k_at))
        mlp_mine = jnp.stack([total([view(t, mp=0) for t in chain[0]]) for chain in chains])
        one = [[opened(keep_one), opened(came_one)], list(ups)]
        came_two = swap_dp(send_two, 1)
        step([one])
        two = [[opened(keep_two), opened(came_two)], list(downs)]
        grad, gvec_one = entry((d_one, d_two), spans, w_all, x, part, vectors)
        arrays, grad, gvec_one = tie(newest([one, two]), grad, gvec_one)
        renew([one, two], arrays)
        step([two])
        while one[1]:
            step([one])
        input_grad = put_row(grad, rank, cotangent, 0, f32)
        arrays, input_grad, y = tie(newest([one, two]), input_grad, y)
        renew([one, two], arrays)
        while two[1]:
            step([two])
        block_output = put_row(y, rank, tokens, 0, bf16)
        arrays, block_output, grad = tie(newest([one, two]), block_output, grad)
        renew([one, two], arrays)
        attn_sent = []
        for k_at in range(1, mp):
            give = [
                total([view(t, mp=mp_at ^ k_at) for t in chain[0]]).astype(bf16)
                for chain in (one, two)
            ]
            attn_sent.append(swap_mp(jnp.concatenate(give, 1), k_at))
        attn_mine = jnp.concatenate(
            [total([view(t, mp=mp_at) for t in chain[0]]) for chain in (one, two)], 1
        )
        for row in range(1, rows):
            input_grad = put_row(grad, rank, cotangent, row, f32, input_grad)
        mlp_sent, input_grad = tie(mlp_sent, input_grad)
    else:
        d_all, attn_keep, _ = back(dctx, gwo, plan, 0, GROUPS)
        grad, gvec_one = entry((d_all,), ((0, GROUPS),), w_all, x, part, vectors)
        input_grad = put_row(grad, rank, cotangent, 0, f32)
        block_output = put_row(y, rank, tokens, 0, bf16)
        for row in range(1, rows):
            input_grad = put_row(grad, rank, cotangent, row, f32, input_grad)
        shaped = mlp_keep[:, 0].reshape(2, mp, dp, D // dp, FF // mp)
        shaped = jnp.take(shaped, mp_at ^ jnp.arange(mp), axis=1)
        shaped = shaped.transpose(2, 1, 0, 3, 4).reshape(world, 2, D // dp, FF // mp)
        mlp_mine = lax.psum_scatter(shaped, everyone, scatter_dimension=0, tiled=True)[0]
        mlp_mine = mlp_mine.astype(f32)
        attn_mine = lax.psum_scatter(attn_keep[0], everyone, scatter_dimension=0, tiled=True)
        attn_mine = attn_mine.astype(f32)
        mlp_sent, attn_sent = [], []

    *mlp_news, squares = mlp_lamb(
        (up_weight, up_first, up_second, down_weight.T, down_first.T, down_second.T),
        mlp_mine, mlp_sent,
    )
    *attn_news, load = attn_lamb(
        (qkv_weight, qkv_first, qkv_second, proj_weight, proj_first, proj_second),
        attn_mine, attn_sent, gvec_one, gvec_two, gbias, squares,
    )
    load, y = tie(load, y)
    came = swap_dp(load, 1) if fast else lax.psum(load, everyone)
    for row in range(1, rows):
        block_output = put_row(y, rank, tokens, row, bf16, block_output)
    came, block_output = tie(came, block_output)
    if fast:
        load = load + came
        bit = 2
        while bit < dp:
            load = load + swap_dp(load, bit)
            bit *= 2
        bit = 1
        while bit < mp:
            load = load + swap_mp(load, bit)
            bit *= 2
    else:
        load = came
    square = (FF // 128, 128)
    (
        weight_norms, qkv_new, proj_new, up_new, down_new,
        bias_new, bias_first_new, bias_second_new, *vector_news,
    ) = last(
        load,
        (qkv_weight, proj_weight, up_weight, down_weight.T),
        (attn_news[2], attn_news[5], mlp_news[2], mlp_news[5]),
        [value.reshape(square) for value in (up_bias, bias_first, bias_second)],
        (vectors, vector_first, vector_second),
    )
    return (
        block_output, input_grad, weight_norms,
        qkv_new, attn_news[0], attn_news[1],
        proj_new, attn_news[3], attn_news[4],
        up_new, mlp_news[0], mlp_news[1],
        down_new.T, mlp_news[3].T, mlp_news[4].T,
        bias_new.reshape(FF), bias_first_new.reshape(FF), bias_second_new.reshape(FF),
        *vector_news,
    )


def solution(mesh):
    dp, mp = mesh.shape["dp"], mesh.shape["mp"]
    split = Mesh(mesh.devices.reshape(dp // 2, 2, mp), ("dq", "dc", "mp"))
    rows = ("dq", "dc", "mp")
    by_rows = (P(rows, None),) * 3
    shared = (P(),) * 3
    up_spec = (P(("dq", "dc"), "mp"),) * 3
    down_spec = (P("mp", ("dq", "dc")),) * 3
    in_specs = (
        (P(rows, None, None), P(rows, None), P(rows, None), P(rows, None, None))
        + by_rows + by_rows + up_spec + down_spec + shared + shared
    )
    out_specs = (
        (P(rows, None, None), P(rows, None, None), P())
        + by_rows + by_rows + up_spec + down_spec + shared + shared
    )
    return jax.shard_map(
        partial(on_device, dp=dp, mp=mp),
        mesh=split, in_specs=in_specs, out_specs=out_specs, check_vma=False,
    )
```

```python
from functools import partial
import math

import jax
import jax.numpy as jnp
from jax import lax
from jax.experimental import pallas as pl
from jax.experimental.pallas import tpu as pltpu
from jax.sharding import Mesh, PartitionSpec as P

D = 768
FF = 3072
HEADS = 12
HEAD_DIM = 64
CAP = 640
SEQ = 1280
STEP = 10

eps_norm = 1e-06
eps_adam = 1e-06
beta_one = 0.9
beta_two = 0.999
decay_mat = 0.01
rate_lamb = 0.3
masked_score = -1e30

f32 = jnp.float32
bf16 = jnp.bfloat16
GROUP = 256
GROUPS = D // GROUP
LOG2E = 1.0 / math.log(2.0)
SCORE_SCALE = 1.0 / math.sqrt(HEAD_DIM)
ROUTER_SCALE = 1.0 / math.sqrt(D)


def dot_ab(left, right, left_dim=1, right_dim=0):
    return lax.dot_general(
        left, right, (((left_dim,), (right_dim,)), ((), ())), preferred_element_type=f32
    )


def params(mib, **more):
    return pltpu.CompilerParams(vmem_limit_bytes=mib << 20, **more)


def hbm(shape, dtype):
    return pltpu.HBM(shape, dtype)


def pinned(*arrays):
    return [
        pltpu.with_memory_space_constraint(array, pltpu.HBM) if array.size >= 1 << 17 else array
        for array in arrays
    ]


def cost(flops, nbytes, trans=0):
    return pl.CostEstimate(flops=int(flops), bytes_accessed=int(nbytes), transcendentals=int(trans))


def norm_parts(values):
    center = jnp.mean(values, -1, keepdims=True)
    offset = values - center
    spread = jnp.mean(offset * offset, -1, keepdims=True)
    inverse = lax.rsqrt(spread + eps_norm)
    return offset * inverse, inverse


def norm_back(grad, normalized, inverse, gain):
    scaled = grad * gain
    return inverse * (
        scaled
        - jnp.mean(scaled, -1, keepdims=True)
        - normalized * jnp.mean(scaled * normalized, -1, keepdims=True)
    )


def ranks_of(sel, ids):
    kind = jnp.where(ids < 0, 2, ids)
    sub = lax.broadcasted_iota(jnp.int32, (8, SEQ), 0)
    lane = lax.broadcasted_iota(jnp.int32, (8, SEQ), 1)
    member = jnp.where(jnp.broadcast_to(kind, (8, SEQ)) == sub, jnp.broadcast_to(sel, (8, SEQ)), 0)
    total = member
    step = 1
    while step < SEQ:
        total = total + jnp.where(lane >= step, pltpu.roll(total, step, 1), 0)
        step *= 2
    count = jnp.max(total, axis=1, keepdims=True)
    first = count[0:1]
    second = first + count[1:2]
    base = jnp.where(sub == 0, 0, jnp.where(sub == 1, first, second))
    rank = jnp.sum(member * (total + base), axis=0, keepdims=True) - 1
    return rank, first, second


def one_hot(rank):
    place = lax.broadcasted_iota(jnp.int32, (CAP, rank.shape[1]), 0)
    return jnp.where(place == rank, 1.0, 0.0).astype(bf16)


def pick_kernel(
    sel_ref, ids_ref, tok_ref, cot_ref, vec_ref,
    x_ref, dy_ref, a_ref, at_ref, dm_ref, rank_ref, bounds_ref, x_scr, dy_scr,
):
    rank, first, second = ranks_of(sel_ref[0], ids_ref[0])
    rank_ref[0] = jnp.broadcast_to(rank, (8, SEQ))
    lane = lax.broadcasted_iota(jnp.int32, (8, 128), 1)
    bounds_ref[0] = jnp.where(lane == 0, first, second)
    hot = one_hot(rank)
    x_scr[...] = dot_ab(hot, tok_ref[0])
    dy_scr[...] = dot_ab(hot, cot_ref[0])
    tile = 128

    def body(i, carry):
        rows = pl.ds(pl.multiple_of(i * tile, tile), tile)
        x = x_scr[rows, :]
        dy = dy_scr[rows, :]
        normalized, _ = norm_parts(x)
        low = (normalized * vec_ref[0:1, :] + vec_ref[1:2, :]).astype(bf16)
        gate = jax.nn.sigmoid(jnp.sum(x * vec_ref[4:5, :], -1, keepdims=True) * ROUTER_SCALE)
        x_ref[rows, :] = x.astype(bf16)
        dy_ref[rows, :] = dy.astype(bf16)
        a_ref[rows, :] = low
        dm_ref[rows, :] = (gate * dy).astype(bf16)
        return carry

    lax.fori_loop(0, CAP // tile, body, 0, unroll=True)
    at_ref[...] = a_ref[...].T


def pick_rows(sel, ids, tokens, cotangent, vectors):
    rows = tokens.shape[0]
    count = rows * CAP
    wide = pl.BlockSpec((CAP, D), lambda r: (r, 0))
    line = pl.BlockSpec((1, 1, SEQ), lambda r: (r, 0, 0))
    full = pl.BlockSpec((1, SEQ, D), lambda r: (r, 0, 0))
    return pl.pallas_call(
        pick_kernel,
        grid=(rows,),
        in_specs=[line, line, full, full, pl.BlockSpec((7, D), lambda r: (0, 0))],
        out_specs=[
            wide, wide, wide, pl.BlockSpec((D, CAP), lambda r: (0, r)), wide,
            pl.BlockSpec((1, 8, SEQ), lambda r: (r, 0, 0)),
            pl.BlockSpec((1, 8, 128), lambda r: (r, 0, 0)),
        ],
        out_shape=[
            hbm((count, D), bf16),
            hbm((count, D), bf16),
            hbm((count, D), bf16),
            hbm((D, count), bf16),
            hbm((count, D), bf16),
            hbm((rows, 8, SEQ), jnp.int32),
            hbm((rows, 8, 128), jnp.int32),
        ],
        scratch_shapes=[pltpu.VMEM((CAP, D), f32), pltpu.VMEM((CAP, D), f32)],
        compiler_params=params(40),
        cost_estimate=cost(4 * count * SEQ * D, 4 * rows * SEQ * D * 2),
        name="pick_rows",
    )(*pinned(sel[:, None, :], ids[:, None, :], tokens, cotangent, vectors))


def fill_bias(bias_scr, bounds_ref):
    first = bounds_ref[0, 0:1, 0:1]
    second = bounds_ref[0, 0:1, 1:2]
    tile = 128
    key = lax.broadcasted_iota(jnp.int32, (tile, CAP), 1)
    key_kind = jnp.where(key >= first, 1, 0) + jnp.where(key >= second, 1, 0)
    for i in range(CAP // tile):
        row = lax.broadcasted_iota(jnp.int32, (tile, CAP), 0) + i * tile
        row_kind = jnp.where(row >= first, 1, 0) + jnp.where(row >= second, 1, 0)
        bias_scr[i * tile : (i + 1) * tile, :] = jnp.where(row_kind == key_kind, 0.0, masked_score)


def half_masks():
    lane = lax.broadcasted_iota(jnp.int32, (1, 128), 1)
    low = jnp.where(lane < HEAD_DIM, 1.0, 0.0)
    return low, 1.0 - low


def attend_kernel(
    a_ref, w_ref, bounds_ref,
    q_ref, k_ref, v_ref, ctx_ref, probs_ref, bias_scr,
):
    @pl.when(pl.program_id(1) == 0)
    def _():
        fill_bias(bias_scr, bounds_ref)

    a = a_ref[...]
    for part, ref in enumerate((q_ref, k_ref, v_ref)):
        ref[...] = dot_ab(a, w_ref[:, part * GROUP : (part + 1) * GROUP]).astype(bf16)
    masks = half_masks()
    lane = lax.broadcasted_iota(jnp.int32, (1, 128), 1)
    for pair in range(GROUP // 128):
        cols = slice(pair * 128, pair * 128 + 128)
        queries, key_rows, values = q_ref[:, cols], k_ref[:, cols], v_ref[:, cols]
        halves = []
        for half in range(2):
            scores = dot_ab(queries * masks[half].astype(bf16), key_rows, 1, 1)
            scores = scores * (SCORE_SCALE * LOG2E) + bias_scr[...]
            row_max = jnp.max(scores, -1, keepdims=True)
            probs = jnp.exp2(scores - row_max)
            row_total = jnp.sum(probs, -1, keepdims=True)
            probs = (probs * (1.0 / row_total)).astype(bf16)
            probs_ref[0, pair * 2 + half] = probs
            halves.append(dot_ab(probs, values))
        ctx_ref[:, cols] = jnp.where(lane < HEAD_DIM, halves[0], halves[1]).astype(bf16)


def attend_forward(a, w_all, bounds):
    count = a.shape[0]
    rows = count // CAP
    piece = pl.BlockSpec((CAP, GROUP), lambda r, g: (r, g))
    narrow = hbm((count, D), bf16)
    return pl.pallas_call(
        attend_kernel,
        grid=(rows, GROUPS),
        in_specs=[
            pl.BlockSpec((CAP, D), lambda r, g: (r, 0)),
            pl.BlockSpec((D, 3 * GROUP), lambda r, g: (0, g)),
            pl.BlockSpec((1, 8, 128), lambda r, g: (r, 0, 0)),
        ],
        out_specs=[
            piece, piece, piece, piece,
            pl.BlockSpec((1, GROUP // HEAD_DIM, CAP, CAP), lambda r, g: (r, g, 0, 0)),
        ],
        out_shape=[narrow, narrow, narrow, narrow, hbm((rows, HEADS, CAP, CAP), bf16)],
        scratch_shapes=[pltpu.VMEM((CAP, CAP), f32)],
        compiler_params=params(48),
        cost_estimate=cost(
            2 * count * D * 3 * D + rows * HEADS * 16 * CAP * CAP * HEAD_DIM, 12 * count * D,
            rows * HEADS * CAP * CAP,
        ),
        name="attend_forward",
    )(*pinned(a, w_all, bounds))


def attend_back_kernel(
    me_ref, at_ref, q_ref, k_ref, v_ref, ctx_ref, dctx_ref, probs_ref, gwo_ref,
    d_ref, keep_ref, send_ref, held_scr, acc_scr, *, plan,
):
    row = pl.program_id(1)
    masks = half_masks()
    lane = lax.broadcasted_iota(jnp.int32, (1, 128), 1)
    for pair in range(GROUP // 128):
        cols = slice(pair * 128, pair * 128 + 128)
        queries, key_rows, values = q_ref[:, cols], k_ref[:, cols], v_ref[:, cols]
        grads = dctx_ref[:, cols]
        product = ctx_ref[:, cols].astype(f32) * grads.astype(f32)
        queries_t, grads_t = queries.T, grads.T
        dq, dk_t, dv_t = [], [], []
        for half in range(2):
            mask_low = masks[half].astype(bf16)
            span = slice(half * HEAD_DIM, half * HEAD_DIM + HEAD_DIM)
            probs = probs_ref[0, pair * 2 + half]
            delta = jnp.sum(product * masks[half], -1, keepdims=True)
            probs_grad = dot_ab(grads * mask_low, values, 1, 1)
            score_grad = (probs.astype(f32) * (probs_grad - delta)).astype(bf16)
            dq.append(dot_ab(score_grad, key_rows))
            dk_t.append(dot_ab(queries_t[span], score_grad))
            dv_t.append(dot_ab(grads_t[span], probs))
        place = pair * 128
        d_ref[:, place : place + 128] = (jnp.where(lane < HEAD_DIM, dq[0], dq[1]) * SCORE_SCALE).astype(bf16)
        place += GROUP
        d_ref[:, place : place + 128] = (jnp.concatenate(dk_t, 0) * SCORE_SCALE).astype(bf16).T
        place += GROUP
        d_ref[:, place : place + 128] = jnp.concatenate(dv_t, 0).astype(bf16).T
    held_scr[pl.ds(pl.multiple_of(row * CAP, CAP), CAP), :] = d_ref[...]

    @pl.when(row == pl.num_programs(1) - 1)
    def _():
        acc_scr[:, : 3 * GROUP] = dot_ab(at_ref[...], held_scr[...])
        acc_scr[:, 3 * GROUP :] = gwo_ref[...]
        split_blocks(me_ref, acc_scr, keep_ref, send_ref, plan)


def split_blocks(me_ref, acc_scr, keep_ref, send_ref, plan):
    if plan is None:
        keep_ref[0] = acc_scr[...].astype(bf16)
        send_ref[0] = jnp.zeros_like(send_ref[0])
        return
    blocks, core_bit = plan
    size = D // blocks
    on_high = (me_ref[0] & core_bit) != 0
    for block in range(blocks):
        if block & core_bit:
            continue
        low = acc_scr[block * size : (block + 1) * size, :]
        other = block | core_bit
        high = acc_scr[other * size : (other + 1) * size, :]
        slot = (block // (2 * core_bit)) * core_bit + block % core_bit
        keep_ref[slot] = jnp.where(on_high, high, low).astype(bf16)
        send_ref[slot] = jnp.where(on_high, low, high).astype(bf16)


def attend_backward(me, at, q, k, v, ctx, probs, dctx, gwo, plan, start, groups):
    count = q.shape[0]
    rows = count // CAP
    piece = pl.BlockSpec((CAP, GROUP), lambda g, r, me: (r, g + start))
    if plan is None:
        half, size, sent = 1, D, 8
    else:
        half, size = plan[0] // 2, D // plan[0]
        sent = size
    width = 4 * GROUP
    return pl.pallas_call(
        partial(attend_back_kernel, plan=plan),
        grid_spec=pltpu.PrefetchScalarGridSpec(
            num_scalar_prefetch=1,
            grid=(groups, rows),
            in_specs=[
                pl.BlockSpec((D, count), lambda g, r, me: (0, 0)),
                piece, piece, piece, piece, piece,
                pl.BlockSpec(
                    (1, GROUP // HEAD_DIM, CAP, CAP), lambda g, r, me: (r, g + start, 0, 0)
                ),
                pl.BlockSpec((D, GROUP), lambda g, r, me: (0, g + start)),
            ],
            out_specs=[
                pl.BlockSpec((CAP, 3 * GROUP), lambda g, r, me: (r, g)),
                pl.BlockSpec((half, size, width), lambda g, r, me: (0, 0, g)),
                pl.BlockSpec((half, sent, width), lambda g, r, me: (0, 0, g)),
            ],
            scratch_shapes=[
                pltpu.VMEM((count, 3 * GROUP), bf16), pltpu.VMEM((D, width), f32),
            ],
        ),
        out_shape=[
            hbm((count, groups * 3 * GROUP), bf16),
            hbm((half, size, groups * width), bf16),
            hbm((half, sent, groups * width), bf16),
        ],
        compiler_params=params(40),
        cost_estimate=cost(
            groups * GROUP * (6 * count * D + 40 * count * CAP),
            groups * GROUP * 20 * count,
            groups * (GROUP // HEAD_DIM) * count * CAP,
        ),
        name="attend_backward",
    )(me, *pinned(at, q, k, v, ctx, dctx, probs, gwo))


def middle_kernel(ctx_ref, wo_ref, x_ref, vec_ref, att_ref, c_ref):
    att = dot_ab(ctx_ref[...], wo_ref[...]) + vec_ref[5:6, :]
    att_ref[...] = att
    normalized, _ = norm_parts(x_ref[...].astype(f32) + att)
    c_ref[...] = (normalized * vec_ref[2:3, :] + vec_ref[3:4, :]).astype(bf16)


def middle(ctx, w_o, x, vectors):
    count = ctx.shape[0]
    tile = 640
    wide = pl.BlockSpec((tile, D), lambda t: (t, 0))
    return pl.pallas_call(
        middle_kernel,
        grid=(count // tile,),
        in_specs=[
            wide, pl.BlockSpec((D, D), lambda t: (0, 0)), wide,
            pl.BlockSpec((7, D), lambda t: (0, 0)),
        ],
        out_specs=[wide, wide],
        out_shape=[
            hbm((count, D), f32),
            hbm((count, D), bf16),
        ],
        compiler_params=params(60),
        cost_estimate=cost(2 * count * D * D, 10 * count * D),
        name="middle",
    )(*pinned(ctx, w_o, x, vectors))


ERF_P = 0.3275911 / math.sqrt(2.0)
ERF_COEF = (0.254829592, -0.284496736, 1.421413741, -1.453152027, 1.061405429)


def gelu_parts(u):
    bell = jnp.exp2(u * u * (-0.5 * LOG2E))
    t = 1.0 / (1.0 + ERF_P * jnp.abs(u))
    poly = ERF_COEF[4]
    for coef in ERF_COEF[3::-1]:
        poly = poly * t + coef
    tail = (0.5 * poly * t) * bell
    phi = jnp.where(u >= 0, 1.0 - tail, tail)
    return u * phi, phi + u * (bell * (1.0 / math.sqrt(2.0 * math.pi)))


def mlp_kernel(
    me_ref, c_ref, dm_ref, wu_ref, wd_ref, bias_ref,
    mlp_ref, dc_ref, keep_ref, send_ref, gbias_ref, ct_scr, dmt_scr, act_scr, du_scr,
    *, blocks, split,
):
    first = (pl.program_id(0) == 0) & (pl.program_id(1) == 0)

    @pl.when(first)
    def _():
        ct_scr[...] = c_ref[...].T
        dmt_scr[...] = dm_ref[...].T
        mlp_ref[...] = jnp.zeros_like(mlp_ref)
        dc_ref[...] = jnp.zeros_like(dc_ref)

    width = wu_ref.shape[-1]
    wu = wu_ref[...].reshape(D, width)
    wd = wd_ref[...].reshape(D, width)
    tile = CAP

    def body(i, total):
        rows = pl.ds(pl.multiple_of(i * tile, tile), tile)
        act, slope = gelu_parts(dot_ab(c_ref[rows, :], wu) + bias_ref[0])
        act = act.astype(bf16)
        du = (slope * dot_ab(dm_ref[rows, :], wd)).astype(bf16)
        act_scr[rows, :] = act
        du_scr[rows, :] = du
        mlp_ref[rows, :] += dot_ab(act, wd, 1, 1)
        dc_ref[rows, :] += dot_ab(du, wu, 1, 1)
        return total + jnp.sum(du.astype(f32), 0, keepdims=True)

    total = lax.fori_loop(0, c_ref.shape[0] // tile, body, jnp.zeros((1, width), f32))
    gbias_ref[0] = jnp.broadcast_to(total, (8, width))
    act, du = act_scr[...], du_scr[...]
    size = D // blocks
    for which, grad in enumerate((dot_ab(ct_scr[...], du), dot_ab(dmt_scr[...], act))):
        if not split:
            keep_ref[which, 0, 0] = grad.astype(bf16)
            continue
        on_high = (me_ref[2] & 1) != 0
        for block in range(0, blocks, 2):
            low = grad[block * size : (block + 1) * size]
            high = grad[(block + 1) * size : (block + 2) * size]
            slot = block // 2
            keep_ref[which, slot, 0] = jnp.where(on_high, high, low).astype(bf16)
            send_ref[which, slot, 0] = jnp.where(on_high, low, high).astype(bf16)
    if not split:
        send_ref[...] = jnp.zeros_like(send_ref)


def mlp_all(me, c, dm, weights, bias, split):
    count = c.shape[0]
    blocks, mp, _, units = weights.shape
    size = D // blocks
    width = 768
    subs = units // width
    half = blocks // 2 if split else 1
    sent = size if split else 8
    rows_out = size if split else D
    all_rows = pl.BlockSpec((count, D), lambda j, s, me: (0, 0))

    def weight_spec(which):
        return pl.BlockSpec(
            (blocks, 1, size, width), lambda j, s, me, which=which: (0, me[1] ^ j, which, s)
        )

    return pl.pallas_call(
        partial(mlp_kernel, blocks=blocks, split=split),
        grid_spec=pltpu.PrefetchScalarGridSpec(
            num_scalar_prefetch=1,
            grid=(mp, subs),
            in_specs=[
                all_rows, all_rows, weight_spec(0), weight_spec(1),
                pl.BlockSpec((1, 1, width), lambda j, s, me: ((me[1] ^ j) * subs + s, 0, 0)),
            ],
            out_specs=[
                all_rows, all_rows,
                pl.BlockSpec((2, half, 1, rows_out, width), lambda j, s, me: (0, 0, j, 0, s)),
                pl.BlockSpec((2, half, 1, sent, width), lambda j, s, me: (0, 0, j, 0, s)),
                pl.BlockSpec((1, 8, width), lambda j, s, me: (me[1] ^ j, 0, s)),
            ],
            scratch_shapes=[pltpu.VMEM((D, count), bf16)] * 2
            + [pltpu.VMEM((count, width), bf16)] * 2,
        ),
        out_shape=[
            hbm((count, D), f32),
            hbm((count, D), f32),
            hbm((2, half, mp, rows_out, units), bf16),
            hbm((2, half, mp, sent, units), bf16),
            hbm((mp, 8, units), f32),
        ],
        compiler_params=params(62),
        cost_estimate=cost(
            12 * count * D * mp * units, 12 * count * D + 8 * mp * units * D, 2 * count * mp * units
        ),
        name="mlp_all",
    )(me, *pinned(c, dm, weights, weights, bias.reshape(mp * subs, 1, width)))


def turn_kernel(
    x_ref, dy_ref, att_ref, mlp_ref, dc_ref, ctx_ref, wo_ref, vec_ref,
    y_ref, part_ref, dctx_ref, gwo_ref, gvec_ref, datt_scr,
):
    step = pl.program_id(0)

    @pl.when(step == 0)
    def _():
        gvec_ref[...] = jnp.zeros_like(gvec_ref)
        gwo_ref[...] = jnp.zeros_like(gwo_ref)

    tile = 64
    router = vec_ref[4:5, :]

    def body(i, carry):
        rows = pl.ds(pl.multiple_of(i * tile, tile), tile)
        x = x_ref[rows, :].astype(f32)
        dy = dy_ref[rows, :].astype(f32)
        att = att_ref[rows, :]
        branch = att + mlp_ref[rows, :] + vec_ref[6:7, :]
        gate = jax.nn.sigmoid(jnp.sum(x * router, -1, keepdims=True) * ROUTER_SCALE)
        y_ref[rows, :] = (x + gate * branch).astype(bf16)
        dr = jnp.sum(dy * branch, -1, keepdims=True) * gate * (1.0 - gate) * ROUTER_SCALE
        e = gate * dy
        normalized, inverse = norm_parts(x + att)
        dc = dc_ref[rows, :]
        dh = norm_back(dc, normalized, inverse, vec_ref[2:3, :])
        datt = (e + dh).astype(bf16)
        datt_scr[rows, :] = datt
        part_ref[rows, :] = dy + dr * router + dh
        for place, term in enumerate(
            (dc * normalized, dc, dr * x, datt.astype(f32), e.astype(bf16).astype(f32))
        ):
            gvec_ref[place : place + 1, :] += jnp.sum(term, 0, keepdims=True)
        return carry

    lax.fori_loop(0, x_ref.shape[0] // tile, body, 0, unroll=True)
    datt = datt_scr[...]
    dctx_ref[...] = dot_ab(datt, wo_ref[...], 1, 1).astype(bf16)
    gwo_ref[...] += dot_ab(ctx_ref[...], datt, 0, 0)


def turn(x, dy, att, mlp, dc, ctx, w_o, vectors):
    count = x.shape[0]
    tile = 320
    wide = pl.BlockSpec((tile, D), lambda t: (t, 0))
    return pl.pallas_call(
        turn_kernel,
        grid=(count // tile,),
        in_specs=[
            wide, wide, wide, wide, wide, wide, pl.BlockSpec((D, D), lambda t: (0, 0)),
            pl.BlockSpec((7, D), lambda t: (0, 0)),
        ],
        out_specs=[
            wide, wide, wide, pl.BlockSpec((D, D), lambda t: (0, 0)),
            pl.BlockSpec((8, D), lambda t: (0, 0)),
        ],
        out_shape=[
            hbm((count, D), bf16),
            hbm((count, D), f32),
            hbm((count, D), bf16),
            hbm((D, D), f32),
            hbm((8, D), f32),
        ],
        scratch_shapes=[pltpu.VMEM((tile, D), bf16)],
        compiler_params=params(48),
        cost_estimate=cost(4 * count * D * D, 26 * count * D),
        name="turn",
    )(*pinned(x, dy, att, mlp, dc, ctx, w_o, vectors))


def entry_kernel(
    *refs, spans,
):
    count = len(spans)
    grads = refs[:count]
    w_refs, refs = refs[count : count + GROUPS], refs[count + GROUPS :]
    x_ref, part_ref, vec_ref, out_ref, gvec_ref, da_scr = refs

    @pl.when(pl.program_id(0) == 0)
    def _():
        gvec_ref[...] = jnp.zeros_like(gvec_ref)

    da = None
    for ref, (start, groups) in zip(grads, spans):
        for at in range(groups):
            term = dot_ab(ref[:, at * D : (at + 1) * D], w_refs[start + at][...], 1, 1)
            da = term if da is None else da + term
    da_scr[...] = da
    tile = 64

    def body(i, carry):
        rows = pl.ds(pl.multiple_of(i * tile, tile), tile)
        normalized, inverse = norm_parts(x_ref[rows, :].astype(f32))
        da = da_scr[rows, :]
        for place, term in enumerate((da * normalized, da)):
            gvec_ref[place : place + 1, :] += jnp.sum(term, 0, keepdims=True)
        grad = part_ref[rows, :] + norm_back(da, normalized, inverse, vec_ref[0:1, :])
        out_ref[rows, :] = grad.astype(bf16)
        return carry

    lax.fori_loop(0, x_ref.shape[0] // tile, body, 0, unroll=True)


def entry(grads, spans, w_all, x, part, vectors):
    count = x.shape[0]
    tile = 320
    wide = pl.BlockSpec((tile, D), lambda r: (r, 0))
    return pl.pallas_call(
        partial(entry_kernel, spans=spans),
        grid=(count // tile,),
        in_specs=[pl.BlockSpec((tile, g.shape[1]), lambda r: (r, 0)) for g in grads]
        + [pl.BlockSpec((D, D), lambda r, group=group: (0, group)) for group in range(GROUPS)]
        + [
            wide, wide, pl.BlockSpec((7, D), lambda r: (0, 0)),
        ],
        out_specs=[
            wide,
            pl.BlockSpec((8, D), lambda r: (0, 0)),
        ],
        out_shape=[
            hbm((count, D), bf16),
            hbm((8, D), f32),
        ],
        scratch_shapes=[pltpu.VMEM((tile, D), f32)],
        compiler_params=params(32),
        cost_estimate=cost(2 * count * D * 3 * D, 24 * count * D),
        name="entry",
    )(*pinned(*grads, *[w_all] * GROUPS, x, part, vectors))


def put_kernel(value_ref, rank_ref, base_ref, *refs):
    out_ref, ext_scr = refs[-2:]
    ext_scr[:, 0:D] = value_ref[...]
    ext_scr[:, D:] = jnp.ones((CAP, 128), bf16)
    placed = dot_ab(one_hot(rank_ref[0, 0:1, :]), ext_scr[...], 0, 0)
    kept = 1.0 - placed[:, D : D + 1]
    out_ref[0] = (placed[:, 0:D] + kept * base_ref[0].astype(f32)).astype(out_ref.dtype)


def put_row(value, rank, base, row, dtype, before=None):
    full = pl.BlockSpec((1, SEQ, D), lambda r: (row, 0, 0))
    held = [] if before is None else [before]
    weight = jnp.dtype(dtype).itemsize // 2
    return pl.pallas_call(
        put_kernel,
        grid=(1,),
        in_specs=[
            pl.BlockSpec((CAP, D), lambda r: (row, 0)),
            pl.BlockSpec((1, 8, SEQ), lambda r: (row, 0, 0)),
            full,
        ]
        + [pl.BlockSpec(memory_space=pl.ANY)] * len(held),
        out_specs=full,
        out_shape=hbm(base.shape, dtype),
        input_output_aliases={3: 0} if held else {},
        scratch_shapes=[pltpu.VMEM((CAP, D + 128), bf16)],
        compiler_params=params(48),
        cost_estimate=cost(2 * weight * CAP * SEQ * D, 5 * weight * CAP * D),
        name="put_row",
    )(*pinned(value, rank, base), *held)


def lamb_moments(weight, gradient, first_mom, second_mom, decay):
    first_new = beta_one * first_mom + (1.0 - beta_one) * gradient
    second_new = beta_two * second_mom + (1.0 - beta_two) * gradient * gradient
    update = (
        first_new
        / (1.0 - beta_one**STEP)
        / (jnp.sqrt(second_new / (1.0 - beta_two**STEP)) + eps_adam)
        + decay * weight
    )
    return (first_new, second_new, update)


def square_sum(value):
    return jnp.sum(jnp.sum(value * value, 1, keepdims=True), 0, keepdims=True)


def added(mine_ref, got_refs, place):
    result = mine_ref[place]
    for ref in got_refs:
        result = result + ref[place].astype(f32)
    return result


def lanes_of(pairs):
    lane = lax.broadcasted_iota(jnp.int32, (8, 128), 1)
    result = jnp.zeros((8, 128), f32)
    for place, value in pairs:
        result = result + jnp.where(lane == place, value, 0.0)
    return result


def mlp_lamb_kernel(*refs, gots):
    weights, (mine_ref, *rest) = refs[:6], refs[6:]
    got_refs, outs = rest[:gots], rest[gots:]
    pairs = []
    for which in range(2):
        weight_ref, first_ref, second_ref = weights[3 * which : 3 * which + 3]
        grad = added(mine_ref, got_refs, which)
        weight = weight_ref[...]
        news = lamb_moments(weight, grad, first_ref[...], second_ref[...], decay_mat)
        for ref, value in zip(outs[3 * which : 3 * which + 3], news):
            ref[...] = value
        pairs += [(2 + which, square_sum(weight)), (6 + which, square_sum(news[2]))]
    outs[6][...] = lanes_of(pairs)


def mlp_lamb(moments, mine, gots):
    like = jax.ShapeDtypeStruct(moments[0].shape, f32)
    return pl.pallas_call(
        partial(mlp_lamb_kernel, gots=len(gots)),
        out_shape=[like] * 6 + [jax.ShapeDtypeStruct((8, 128), f32)],
        compiler_params=params(24),
        cost_estimate=cost(40 * mine.size, 40 * mine.size),
        name="mlp_lamb",
    )(*moments, mine, *gots)


def attn_lamb_kernel(*refs, gots):
    moments, (mine_ref, *rest) = refs[:6], refs[6:]
    got_refs, rest = rest[:gots], rest[gots:]
    one_ref, two_ref, bias_ref, sq_ref, *outs = rest
    sums = [jnp.zeros((1, 1), f32) for _ in range(4)]
    for part in range(4):
        tensor = part // 3
        weight_ref, first_ref, second_ref = moments[3 * tensor : 3 * tensor + 3]
        for group in range(GROUPS):
            left = (group * 4 + part) * GROUP
            grad = added(mine_ref, got_refs, (slice(None), slice(left, left + GROUP)))
            left = (part % 3) * D + group * GROUP
            cols = (slice(None), slice(left, left + GROUP))
            weight = weight_ref[cols]
            news = lamb_moments(weight, grad, first_ref[cols], second_ref[cols], decay_mat)
            for ref, value in zip(outs[3 * tensor : 3 * tensor + 3], news):
                ref[cols] = value
            sums[tensor] += square_sum(weight)
            sums[2 + tensor] += square_sum(news[2])
    load_ref = outs[6]
    load_ref[...] = jnp.zeros_like(load_ref)
    load_ref[0:2, :] = one_ref[0:2, :]
    load_ref[2:7, :] = two_ref[0:5, :]
    for i in range(FF // D):
        load_ref[7 + i : 8 + i, :] = bias_ref[i, 0:1, :]
    squares = sq_ref[...] + lanes_of(list(zip((0, 1, 4, 5), sums)))
    load_ref[LOAD_SQ : LOAD_SQ + 1, 0:128] = squares[0:1]


LOAD_SQ = 7 + FF // D
LOAD_ROWS = 16


def attn_lamb(moments, mine, gots, gvec_one, gvec_two, gbias, squares):
    qkv_like = jax.ShapeDtypeStruct(moments[0].shape, f32)
    proj_like = jax.ShapeDtypeStruct(moments[3].shape, f32)
    return pl.pallas_call(
        partial(attn_lamb_kernel, gots=len(gots)),
        out_shape=[qkv_like] * 3 + [proj_like] * 3
        + [jax.ShapeDtypeStruct((LOAD_ROWS, D), f32)],
        compiler_params=params(24),
        cost_estimate=cost(40 * mine.size, 40 * mine.size),
        name="attn_lamb",
    )(*moments, mine, *gots, gvec_one, gvec_two, gbias, squares)


def last_kernel(
    load_ref, qkv_ref, proj_ref, up_ref, down_ref, qkv_upd, proj_upd, up_upd, down_upd,
    bias_ref, bias_one, bias_two, vec_ref, vec_one, vec_two,
    norms_ref, qkv_new, proj_new, up_new, down_new,
    bias_new, bias_first, bias_second, vec_new, vec_first, vec_second, bias_scr,
):
    norms = jnp.sqrt(load_ref[LOAD_SQ : LOAD_SQ + 1, 0:128])
    norms_ref[0:1, :] = norms[:, 0:4]
    norms_ref[1:2, :] = norms[:, 4:8]
    for i, (weight, upd, new) in enumerate(
        (
            (qkv_ref, qkv_upd, qkv_new), (proj_ref, proj_upd, proj_new),
            (up_ref, up_upd, up_new), (down_ref, down_upd, down_new),
        )
    ):
        ratio = norms[:, i : i + 1] / norms[:, 4 + i : 5 + i]
        new[...] = weight[...] - rate_lamb * ratio * upd[...]
    for i in range(FF // 128):
        row, left = 7 + i // (D // 128), i % (D // 128) * 128
        bias_scr[i : i + 1, :] = load_ref[row : row + 1, left : left + 128]
    bias = bias_ref[...]
    first, second, upd = lamb_moments(bias, bias_scr[...], bias_one[...], bias_two[...], 0.0)
    bias_first[...] = first
    bias_second[...] = second
    bias_new[...] = bias - rate_lamb * (
        jnp.sqrt(square_sum(bias)) / jnp.sqrt(square_sum(upd))
    ) * upd
    vec = vec_ref[...]
    first, second, upd = lamb_moments(vec, load_ref[0:7, :], vec_one[...], vec_two[...], 0.0)
    vec_first[...] = first
    vec_second[...] = second
    ratio = jnp.sqrt(jnp.sum(vec * vec, -1, keepdims=True)) / jnp.sqrt(
        jnp.sum(upd * upd, -1, keepdims=True)
    )
    vec_new[...] = vec - rate_lamb * ratio * upd


def last(load, weights, upds, bias, vecs):
    def like(value):
        return jax.ShapeDtypeStruct(value.shape, f32)

    return pl.pallas_call(
        last_kernel,
        out_shape=[jax.ShapeDtypeStruct((2, 4), f32)] + [like(w) for w in weights]
        + [like(b) for b in bias] + [like(v) for v in vecs],
        scratch_shapes=[pltpu.VMEM((FF // 128, 128), f32)],
        compiler_params=params(24),
        cost_estimate=cost(1 << 20, 4 << 20),
        name="last",
    )(load, *weights, *upds, *bias, *vecs)


def swap(value, axis, size, bit):
    return lax.ppermute(value, axis, [(i, i ^ bit) for i in range(size)])


def on_device(
    tokens, image_ids, selected, cotangent,
    qkv_weight, qkv_first, qkv_second, proj_weight, proj_first, proj_second,
    up_weight, up_first, up_second, down_weight, down_first, down_second,
    up_bias, bias_first, bias_second, vectors, vector_first, vector_second,
    *, dp, mp,
):
    world = dp * mp
    rows = tokens.shape[0]
    dq_at, dc_at, mp_at = (lax.axis_index(name) for name in ("dq", "dc", "mp"))
    dp_at = dq_at * 2 + dc_at
    me = jnp.stack([dp_at * mp + mp_at, mp_at, dp_at]).astype(jnp.int32)
    everyone = ("dq", "dc", "mp")
    fast = (D // world) % 8 == 0 and dp >= 4 and (D // dp) % 16 == 0

    def swap_dp(value, bit):
        if bit == 1:
            return swap(value, "dc", 2, 1)
        return swap(value, "dq", dp // 2, bit // 2)

    def swap_mp(value, bit):
        return swap(value, "mp", mp, bit)

    bits = []
    bit = 2
    while bit < dp:
        bits.append(bit)
        bit *= 2
    ups, downs = tuple(bits), tuple(reversed(bits))

    def tie(*values):
        return lax.optimization_barrier(values)

    def total(terms):
        result = terms[0].astype(f32)
        for term in terms[1:]:
            result = result + term.astype(f32)
        return result

    def merge(held, came, high, axis):
        return jnp.where(high, jnp.stack([came, held], axis), jnp.stack([held, came], axis))

    size = D // world
    low_qkv = qkv_weight.astype(bf16).reshape(size, 3, GROUPS, GROUP).transpose(0, 2, 1, 3)
    low_qkv = low_qkv.reshape(size, 3 * D)
    proj_low = proj_weight.astype(bf16)
    mlp_low = jnp.concatenate([up_weight.astype(bf16), down_weight.astype(bf16).T], 0)
    picked = pick_rows(selected, image_ids, tokens, cotangent, vectors)
    mlp_mat = lax.all_gather(mlp_low, everyone, axis=0, tiled=True)
    mlp_mat = mlp_mat.reshape(dp, mp, 2 * (D // dp), FF // mp)

    def grown(value, bit, done):
        axis = sum(other > bit for other in done)
        done.append(bit)
        return merge(value, swap_dp(value, bit), (dp_at & bit) != 0, axis)

    low_all = jnp.concatenate([low_qkv, proj_low], 1)
    if fast:
        held = [low_all] + [swap_mp(low_all, k) for k in range(1, mp)]
        held, picked = tie(held, picked)
        held = jnp.stack(held).reshape((2,) * (mp.bit_length() - 1) + (size, 4 * D))
        for axis in range(mp.bit_length() - 1):
            flip = ((mp_at >> (mp.bit_length() - 2 - axis)) & 1) != 0
            held = jnp.where(flip, jnp.flip(held, axis), held)
        held = held.reshape(mp, size, 4 * D)
        halves = [held[:, :, half * 2 * D : (half + 1) * 2 * D] for half in range(2)]
        for half, order in enumerate((ups, downs)):
            done = []
            for bit in order + (1,):
                halves[half] = grown(halves[half], bit, done)
        halves = [value.reshape(D, 2 * D) for value in halves]
        w_all = jnp.concatenate([halves[0], halves[1][:, :D]], 1)
        w_o = halves[1][:, D:]
    else:
        w_all = lax.all_gather(low_all, everyone, axis=0, tiled=True)
        w_all, w_o = w_all[:, : 3 * D], w_all[:, 3 * D :]
        mlp_mat = mlp_mat.reshape(dp, mp, 2, D // dp, FF // mp).transpose(1, 2, 0, 3, 4)
        mlp_mat = mlp_mat.reshape(1, mp, 2 * D, FF // mp)

    def view(term, **more):
        array, names, fixed = term
        fixed = {**fixed, **more}
        start = [fixed.get(name, 0) for name in names] + [0, 0]
        extent = [1 if name in fixed else n for name, n in zip(names, array.shape)]
        kept = [n for name, n in zip(names, array.shape) if name not in fixed]
        out = lax.dynamic_slice(array, start, tuple(extent) + array.shape[-2:])
        return out.reshape(tuple(kept) + array.shape[-2:])

    def name_of(bit):
        return f"b{bit}"

    def opened(array, which=None):
        names = [name_of(bit) for bit in reversed(bits)] + ["mp"]
        fixed = {}
        shape = (2,) * len(bits) + (mp,) + array.shape[-2:]
        if which is not None:
            names, shape, fixed = ["which"] + names, (2,) + shape, {"which": which}
        return (array.reshape(shape), names, fixed)

    def step(chains):
        for chain in chains:
            terms, order = chain
            bit = order.pop(0)
            name, mine = name_of(bit), (dp_at // bit) & 1
            give = total([view(term, **{name: 1 - mine}) for term in terms]).astype(bf16)
            left = [n for n in terms[0][1] if n not in terms[0][2] and n != name]
            chain[0] = [(t[0], t[1], {**t[2], name: mine}) for t in terms]
            chain[0].append((swap_dp(give, bit), left, {}))

    def newest(chains):
        return [chain[0][-1][0] for chain in chains]

    def renew(chains, arrays):
        for chain, array in zip(chains, arrays):
            chain[0][-1] = (array,) + chain[0][-1][1:]

    x, dy, a, at, dm, rank, bounds = picked
    q, k, v, ctx, probs = attend_forward(a, w_all, bounds)
    att, c = middle(ctx, w_o, x, vectors)
    mlp, dc, mlp_keep, mlp_send, gbias = mlp_all(me, c, dm, mlp_mat, up_bias, fast)
    plan = (world, mp) if fast else None
    spans = ((0, GROUPS - 1), (GROUPS - 1, 1))
    back = partial(attend_backward, me, at, q, k, v, ctx, probs)
    if fast:
        mlp_came = swap_dp(mlp_send, 1)
    y, part, dctx, gwo, gvec_two = turn(x, dy, att, mlp, dc, ctx, w_o, vectors)
    if fast:
        mlp_came, dctx = tie(mlp_came, dctx)
        chains = [
            [[opened(mlp_keep, which), opened(mlp_came, which)], list(order)]
            for which, order in enumerate((ups, downs))
        ]
        step(chains)
        d_one, keep_one, send_one = back(dctx, gwo, plan, *spans[0])
        arrays, d_one, send_one, dctx = tie(newest(chains), d_one, send_one, dctx)
        renew(chains, arrays)
        while chains[0][1]:
            step(chains)
        came_one = swap_dp(send_one, 1)
        d_two, keep_two, send_two = back(dctx, gwo, plan, *spans[1])
        arrays, came_one, send_two, d_two, y = tie(newest(chains), came_one, send_two, d_two, y)
        renew(chains, arrays)
        mlp_sent = []
        for k_at in range(1, mp):
            give = jnp.stack([total([view(t, mp=k_at) for t in chain[0]]) for chain in chains])
            mlp_sent.append(swap_mp(give.astype(bf16), k_at))
        mlp_mine = jnp.stack([total([view(t, mp=0) for t in chain[0]]) for chain in chains])
        one = [[opened(keep_one), opened(came_one)], list(ups)]
        came_two = swap_dp(send_two, 1)
        step([one])
        two = [[opened(keep_two), opened(came_two)], list(downs)]
        grad, gvec_one = entry((d_one, d_two), spans, w_all, x, part, vectors)
        arrays, grad, gvec_one = tie(newest([one, two]), grad, gvec_one)
        renew([one, two], arrays)
        step([two])
        while one[1]:
            step([one])
        input_grad = put_row(grad, rank, cotangent, 0, f32)
        arrays, input_grad, y = tie(newest([one, two]), input_grad, y)
        renew([one, two], arrays)
        while two[1]:
            step([two])
        block_output = put_row(y, rank, tokens, 0, bf16)
        arrays, block_output, grad = tie(newest([one, two]), block_output, grad)
        renew([one, two], arrays)
        attn_sent = []
        for k_at in range(1, mp):
            give = [
                total([view(t, mp=mp_at ^ k_at) for t in chain[0]]).astype(bf16)
                for chain in (one, two)
            ]
            attn_sent.append(swap_mp(jnp.concatenate(give, 1), k_at))
        attn_mine = jnp.concatenate(
            [total([view(t, mp=mp_at) for t in chain[0]]) for chain in (one, two)], 1
        )
        for row in range(1, rows):
            input_grad = put_row(grad, rank, cotangent, row, f32, input_grad)
        mlp_sent, input_grad = tie(mlp_sent, input_grad)
    else:
        d_all, attn_keep, _ = back(dctx, gwo, plan, 0, GROUPS)
        grad, gvec_one = entry((d_all,), ((0, GROUPS),), w_all, x, part, vectors)
        input_grad = put_row(grad, rank, cotangent, 0, f32)
        block_output = put_row(y, rank, tokens, 0, bf16)
        for row in range(1, rows):
            input_grad = put_row(grad, rank, cotangent, row, f32, input_grad)
        shaped = mlp_keep[:, 0].reshape(2, mp, dp, D // dp, FF // mp)
        shaped = jnp.take(shaped, mp_at ^ jnp.arange(mp), axis=1)
        shaped = shaped.transpose(2, 1, 0, 3, 4).reshape(world, 2, D // dp, FF // mp)
        mlp_mine = lax.psum_scatter(shaped, everyone, scatter_dimension=0, tiled=True)[0]
        mlp_mine = mlp_mine.astype(f32)
        attn_mine = lax.psum_scatter(attn_keep[0], everyone, scatter_dimension=0, tiled=True)
        attn_mine = attn_mine.astype(f32)
        mlp_sent, attn_sent = [], []

    *mlp_news, squares = mlp_lamb(
        (up_weight, up_first, up_second, down_weight.T, down_first.T, down_second.T),
        mlp_mine, mlp_sent,
    )
    *attn_news, load = attn_lamb(
        (qkv_weight, qkv_first, qkv_second, proj_weight, proj_first, proj_second),
        attn_mine, attn_sent, gvec_one, gvec_two, gbias, squares,
    )
    load, y = tie(load, y)
    came = swap_dp(load, 1) if fast else lax.psum(load, everyone)
    for row in range(1, rows):
        block_output = put_row(y, rank, tokens, row, bf16, block_output)
    came, block_output = tie(came, block_output)
    if fast:
        load = load + came
        bit = 2
        while bit < dp:
            load = load + swap_dp(load, bit)
            bit *= 2
        bit = 1
        while bit < mp:
            load = load + swap_mp(load, bit)
            bit *= 2
    else:
        load = came
    square = (FF // 128, 128)
    (
        weight_norms, qkv_new, proj_new, up_new, down_new,
        bias_new, bias_first_new, bias_second_new, *vector_news,
    ) = last(
        load,
        (qkv_weight, proj_weight, up_weight, down_weight.T),
        (attn_news[2], attn_news[5], mlp_news[2], mlp_news[5]),
        [value.reshape(square) for value in (up_bias, bias_first, bias_second)],
        (vectors, vector_first, vector_second),
    )
    return (
        block_output, input_grad, weight_norms,
        qkv_new, attn_news[0], attn_news[1],
        proj_new, attn_news[3], attn_news[4],
        up_new, mlp_news[0], mlp_news[1],
        down_new.T, mlp_news[3].T, mlp_news[4].T,
        bias_new.reshape(FF), bias_first_new.reshape(FF), bias_second_new.reshape(FF),
        *vector_news,
    )


def solution(mesh):
    dp, mp = mesh.shape["dp"], mesh.shape["mp"]
    split = Mesh(mesh.devices.reshape(dp // 2, 2, mp), ("dq", "dc", "mp"))
    rows = ("dq", "dc", "mp")
    by_rows = (P(rows, None),) * 3
    shared = (P(),) * 3
    up_spec = (P(("dq", "dc"), "mp"),) * 3
    down_spec = (P("mp", ("dq", "dc")),) * 3
    in_specs = (
        (P(rows, None, None), P(rows, None), P(rows, None), P(rows, None, None))
        + by_rows + by_rows + up_spec + down_spec + shared + shared
    )
    out_specs = (
        (P(rows, None, None), P(rows, None, None), P())
        + by_rows + by_rows + up_spec + down_spec + shared + shared
    )
    return jax.shard_map(
        partial(on_device, dp=dp, mp=mp),
        mesh=split, in_specs=in_specs, out_specs=out_specs, check_vma=False,
    )
```
